32 devices in a mesh: dp: 4 (over y, x), replica: 8 (over z, core).
Axes of the slice: x: 2, y: 2, z: 4, core: 2. Of those that a mesh axis runs over, the one named last changes fastest.
Arguments:
- events: bfloat16 [8192, 512], P(('dp', 'replica')), may hold values from -6 to 6
- cotangent: bfloat16 [8192, 512], P(('dp', 'replica')), may hold values from -6 to 6
- weight_in: bfloat16 [512, 2048], replicated, may hold values from -0.25 to 0.25
- weight_out: bfloat16 [512, 512], replicated, may hold values from -0.25 to 0.25
- plan_dest: int32 [8192], P(('dp', 'replica')), may hold values from 0 to 3, as said below
- plan_pos: int32 [8192], P(('dp', 'replica')), may hold values from 0 to 255, as said below
- seq_lengths: int32 [32, 8], P(('dp', 'replica')), may hold values from 1 to 128, 256 in all within a row
Outputs:
- grad_events: bfloat16 [8192, 512], P(('dp', 'replica'))
- grad_weight_in: float32 [512, 2048], P(None, 'dp')
- grad_weight_out: float32 [512, 512], P('dp')
The draws below stay inside these ranges and needn't reach their ends.
Inputs may be any that keep to these rules, and one draw needn't show every extreme that they name: `plan_dest`: rows stay within their replica's group. From one loader to one compute device go at most 96 rows, and exactly 96 for some pairs of every group; every compute device receives 256 rows. `plan_pos`: the rows that one compute device receives take each position 0 to 255 once. `seq_lengths`: each row sums to 256.
All inputs are finite; a program needn't handle non-finite values.
Results may differ from the reference program's by a relative error of at most 0.014.
Values may be sent and summed in bfloat16 or wider, within the bound.
A program may use at most 64 MiB of HBM per device.

```python
import math
import jax
import jax.numpy as jnp
import numpy as np
from jax import lax

D = 512
HEADS = 8
ROWS = 256
NSEQ = 8
MAXLEN = 128
LOADERS = 4
REPLICAS = 8
COMPUTE = 32
TOKENS = 8192


def plan_tables(key):

    def one_group(group_key):
        key_shift, key_rank, key_place = jax.random.split(group_key, 3)
        shift = jax.random.randint(key_shift, (), 0, LOADERS)
        half = ROWS // (2 * LOADERS)
        steps = jnp.arange(LOADERS)
        share = ROWS // LOADERS + half * (1 - 2 * (steps % 2))
        source = jnp.arange(LOADERS)[:, None]
        target = steps[None, :]
        counts = share[(target - source + shift) % LOADERS]
        ends = jnp.cumsum(counts, axis=1)
        starts = ends - counts
        ranks = jax.vmap(lambda subkey: jax.random.permutation(subkey, ROWS))(jax.random.split(key_rank, LOADERS))
        dest = jnp.sum((ranks[:, :, None] >= ends[:, None, :]).astype(jnp.int32), axis=2)
        slot = ranks - jnp.take_along_axis(starts, dest, axis=1)
        before = jnp.cumsum(counts, axis=0) - counts
        index = jnp.take_along_axis(before, dest, axis=1) + slot
        places = jax.vmap(lambda subkey: jax.random.permutation(subkey, ROWS))(jax.random.split(key_place, LOADERS))
        position = places[dest, index]
        return (dest.astype(jnp.int32), position.astype(jnp.int32))
    dest, position = jax.vmap(one_group)(jax.random.split(jax.random.fold_in(key, 7), REPLICAS))
    dest = jnp.swapaxes(dest, 0, 1).reshape(TOKENS)
    position = jnp.swapaxes(position, 0, 1).reshape(TOKENS)
    return (dest, position)


def draw_plan_dest(key, part):
    return plan_tables(key)[0]


def draw_plan_pos(key, part):
    return plan_tables(key)[1]


def levels(own_key, shape, cuts, low, high):
    def one(axis_at, shards_of):
        steps = jax.random.uniform(jax.random.fold_in(jax.random.fold_in(own_key, 6), axis_at), (shards_of,), jnp.float32, low / len(cuts), high / len(cuts))
        return jnp.repeat(jnp.exp(steps), shape[axis_at] // shards_of).reshape((-1,) + (1,) * (len(shape) - axis_at - 1))

    gain = one(*cuts[0])
    for cut in cuts[1:]:
        gain = gain * one(*cut)
    return gain


def split_up(number_of, total, most, skew):
    portions = [(1 << 20) // math.isqrt(grade ** skew) + 1 for grade in range(2, number_of + 1)]
    surplus, holding = total - most - (number_of - 1), [1] * (number_of - 1)
    while surplus > 0:
        candidates = [i for i in range(number_of - 1) if holding[i] < most]
        mass, budget = sum([portions[i] for i in candidates]), surplus
        for i in candidates:
            more = min(most - holding[i], max(1, budget * portions[i] // mass), surplus)
            holding[i] = holding[i] + more
            surplus = surplus - more
    return np.array([most] + holding)


def ragged_sizes(own_key, number_of, total, bound, lean):
    if number_of == 2:
        one = jax.random.randint(own_key, (), max(1, total - bound), min(bound, total - 1) + 1)
        return jnp.stack([one, total - one])
    sizes = jnp.asarray(split_up(number_of, total, bound, lean), jnp.int32)
    twos = (number_of - 1) // 2
    source_of, taker = sizes[1:1 + 2 * twos:2], sizes[2:2 + 2 * twos:2]
    slack = jnp.minimum(source_of - 1, bound - taker)
    moved = jax.random.randint(jax.random.fold_in(own_key, 1), (twos,), 0, 1 << 20) % (slack + 1)
    sizes = sizes.at[1:1 + 2 * twos:2].set(source_of - moved).at[2:2 + 2 * twos:2].set(taker + moved)
    return sizes[jax.random.permutation(jax.random.fold_in(own_key, 2), number_of)]


def centred(stream_key, extent, spread, limit, pieces=(), dtype=jnp.bfloat16):
    factor_of = levels(stream_key, extent, pieces, -0.22, 0.18) if pieces else 1.0
    values = jax.random.normal(stream_key, extent, jnp.float32) * spread * factor_of
    return jnp.minimum(jnp.maximum(values, -limit), limit).astype(dtype)


def setup_inputs(seed: int = 0) -> dict:
    streams_of = jax.random.split(jax.random.key(seed), 8)
    events = centred(streams_of[0], (TOKENS, D), 1.0, 6.0, ((0, 32),))
    cotangent = centred(streams_of[1], (TOKENS, D), 1.0, 6.0, ((0, 32),))
    weight_in = centred(streams_of[2], (D, 4 * D), D ** -0.5, 0.25)
    weight_out = centred(streams_of[3], (D, D), D ** -0.5, 0.25)
    plan_dest = draw_plan_dest(jax.random.fold_in(streams_of[7], 71), 0)
    plan_pos = draw_plan_pos(jax.random.fold_in(streams_of[7], 71), 0)
    seq_lengths = jax.vmap(lambda own: ragged_sizes(own, NSEQ, ROWS, MAXLEN, 2))(jax.random.split(streams_of[6], COMPUTE)).reshape((COMPUTE, NSEQ)).astype(jnp.int32)
    return {"events": events, "cotangent": cotangent, "weight_in": weight_in, "weight_out": weight_out, "plan_dest": plan_dest, "plan_pos": plan_pos, "seq_lengths": seq_lengths}


eps_norm = 1e-05

def rounded(values):
    return lax.optimization_barrier(values.astype(jnp.bfloat16))

def multiply(form, left, right):
    return jnp.einsum(form, left.astype(jnp.float32), right.astype(jnp.float32))

def normalize(values):
    center = values - lax.optimization_barrier(jnp.mean(values, axis=-1, keepdims=True))
    inverse = lax.rsqrt(lax.optimization_barrier(jnp.mean(center * center, axis=-1, keepdims=True)) + eps_norm)
    return (center * inverse, inverse)

def norm_back(grad, normed, inverse):
    return inverse * (grad - lax.optimization_barrier(jnp.mean(grad, axis=-1, keepdims=True)) - normed * lax.optimization_barrier(jnp.mean(grad * normed, axis=-1, keepdims=True)))

def layer_grads(token_rows, grad_rows, weight_in, weight_out, seg_ids):
    row_count, model_width = token_rows.shape
    head_size = model_width // HEADS
    scale = 1.0 / head_size ** 0.5
    normed, inverse = normalize(token_rows.astype(jnp.float32))
    normed_in = rounded(normed)
    proj = jnp.dot(normed_in, weight_in, preferred_element_type=jnp.float32)
    sigma = jax.nn.sigmoid(proj)
    act = rounded(proj * sigma)
    gate_u = act[:, :model_width].astype(jnp.float32)
    value_h = act[:, model_width:2 * model_width].reshape(row_count, HEADS, head_size)
    query_h = act[:, 2 * model_width:3 * model_width].reshape(row_count, HEADS, head_size)
    key_h = act[:, 3 * model_width:].reshape(row_count, HEADS, head_size)
    places = jnp.arange(row_count)
    mask = (seg_ids[:, None] == seg_ids[None, :]) & (places[None, :] <= places[:, None])
    scores = multiply('ihd,jhd->hij', query_h, key_h) * scale
    score_sig = jax.nn.sigmoid(scores)
    attn = rounded(jnp.where(mask[None], scores * score_sig / MAXLEN, 0.0))
    heads_out = multiply('hij,jhd->ihd', attn, value_h).reshape(row_count, model_width)
    onorm, oinv = normalize(heads_out)
    gated = rounded(gate_u * onorm)
    grad_z = jnp.dot(grad_rows, weight_out.T, preferred_element_type=jnp.float32)
    grad_u = grad_z * onorm
    grad_out = rounded(norm_back(grad_z * gate_u, onorm, oinv)).reshape(row_count, HEADS, head_size)
    grad_attn = multiply('ihd,jhd->hij', grad_out, value_h)
    grad_v = multiply('hij,ihd->jhd', attn, grad_out).reshape(row_count, model_width)
    slope = score_sig * (1.0 + scores * (1.0 - score_sig))
    grad_scores = rounded(jnp.where(mask[None], grad_attn * slope * (scale / MAXLEN), 0.0))
    grad_q = multiply('hij,jhd->ihd', grad_scores, key_h).reshape(row_count, model_width)
    grad_k = multiply('hij,ihd->jhd', grad_scores, query_h).reshape(row_count, model_width)
    grad_act = jnp.concatenate([grad_u, grad_v, grad_q, grad_k], axis=1)
    grad_proj = rounded(grad_act * sigma * (1.0 + proj * (1.0 - sigma)))
    grad_xn = jnp.dot(grad_proj, weight_in.T, preferred_element_type=jnp.float32)
    grad_tokens = (grad_rows.astype(jnp.float32) + norm_back(grad_xn, normed, inverse)).astype(jnp.bfloat16)
    part_in = multiply('rd,rf->df', normed_in, grad_proj)
    part_out = multiply('re,rd->ed', gated, grad_rows)
    return (grad_tokens, part_in, part_out)

def segment_ids(lengths):
    bounds = jnp.cumsum(lengths)
    places = jnp.arange(ROWS)
    return lax.optimization_barrier(jnp.sum((places[:, None] >= bounds[None, :]).astype(jnp.int32), axis=1))

def reference(events, cotangent, weight_in, weight_out, plan_dest, plan_pos, seq_lengths):

    def regroup(values):
        shaped = values.reshape((LOADERS, REPLICAS) + values.shape[1:])
        return jnp.swapaxes(shaped, 0, 1)
    group_events = regroup(events.reshape(COMPUTE, ROWS, D))
    group_cot = regroup(cotangent.reshape(COMPUTE, ROWS, D))
    group_dest = regroup(plan_dest.reshape(COMPUTE, ROWS))
    group_pos = regroup(plan_pos.reshape(COMPUTE, ROWS))
    group_len = regroup(seq_lengths)

    def one_group(totals, inputs):
        loaded, loaded_cot, dest, place, lengths = inputs
        target = (dest * ROWS + place).reshape(-1).astype(jnp.int32)
        placed = jnp.zeros((LOADERS * ROWS, D), jnp.bfloat16).at[target].set(loaded.reshape(-1, D))
        placed_cot = jnp.zeros((LOADERS * ROWS, D), jnp.bfloat16).at[target].set(loaded_cot.reshape(-1, D))

        def one_device(items):
            token_rows, grad_rows, device_len = items
            return layer_grads(token_rows, grad_rows, weight_in, weight_out, segment_ids(device_len))
        grads, part_in, part_out = lax.map(one_device, (placed.reshape(LOADERS, ROWS, D), placed_cot.reshape(LOADERS, ROWS, D), lengths))
        returned = grads.reshape(-1, D)[target].reshape(LOADERS, ROWS, D)
        return ((totals[0] + lax.optimization_barrier(jnp.sum(part_in, axis=0)), totals[1] + lax.optimization_barrier(jnp.sum(part_out, axis=0))), returned)
    start = (jnp.zeros((D, 4 * D), jnp.float32), jnp.zeros((D, D), jnp.float32))
    totals, returned = lax.scan(one_group, start, (group_events, group_cot, group_dest, group_pos, group_len))
    grad_events = jnp.swapaxes(returned, 0, 1).reshape(TOKENS, D)
    factor = 1.0 / TOKENS ** 0.5
    return (grad_events, totals[0] * factor, totals[1] * factor)
```

```python
import functools

import jax
import jax.numpy as jnp
from jax import lax
from jax.experimental import pallas as pl
from jax.experimental.pallas import tpu as pltpu
from jax.sharding import PartitionSpec as P

HEADS = 8
MAXLEN = 128
COLORS = 1
EPS = 1e-05
LANES = 128
MESH = pl.DeviceIdType.MESH
F32 = jnp.float32
BF16 = jnp.bfloat16


def contract(left, right, dims):
    return lax.dot_general(left, right, ((dims[:1], dims[1:]), ((), ())), preferred_element_type=F32)


def nn(left, right):
    return contract(left, right, (1, 0))


def nt(left, right):
    return contract(left, right, (1, 1))


def tn(left, right):
    return contract(left, right, (0, 0))


def normalize(values):
    center = values - jnp.mean(values, axis=-1, keepdims=True)
    inverse = lax.rsqrt(jnp.mean(center * center, axis=-1, keepdims=True) + EPS)
    return center * inverse, inverse


def norm_back(grad, normed, inverse):
    return inverse * (
        grad
        - jnp.mean(grad, axis=-1, keepdims=True)
        - normed * jnp.mean(grad * normed, axis=-1, keepdims=True)
    )


def prep_kernel(slot_count, dest_ref, pos_ref, ev_ref, ct_ref, send_ref, pick_ref):
    rows, width = ev_ref.shape
    group = send_ref.shape[0]
    dest = dest_ref[...]
    hot = lax.broadcasted_iota(jnp.int32, (8, rows), 0) == dest
    upper = lax.broadcasted_iota(jnp.int32, (rows, rows), 0) < lax.broadcasted_iota(
        jnp.int32, (rows, rows), 1
    )
    earlier = nn(
        jnp.where(hot, 1.0, 0.0).astype(BF16), jnp.where(upper, 1.0, 0.0).astype(BF16)
    )
    slot = jnp.sum(jnp.where(hot, earlier, 0.0), axis=0, keepdims=True).astype(jnp.int32)
    flat = dest * slot_count + slot
    total = group * slot_count
    chosen = lax.broadcasted_iota(jnp.int32, (total, rows), 0) == flat
    pick = jnp.where(chosen, 1.0, 0.0).astype(BF16)
    pick_ref[...] = pick
    place = jnp.sum(
        jnp.where(chosen, pos_ref[...].astype(F32) + 1.0, 0.0), axis=1, keepdims=True
    )
    shape = (group, slot_count)
    send_ref[:, :, :width] = nn(pick, ev_ref[...]).astype(BF16).reshape(shape + (width,))
    send_ref[:, :, width : 2 * width] = nn(pick, ct_ref[...]).astype(BF16).reshape(shape + (width,))
    send_ref[:, :, 2 * width :] = (
        jnp.broadcast_to(place, (total, LANES)).astype(BF16).reshape(shape + (LANES,))
    )


def swap_kernel(send_ref, recv_ref, send_sem, recv_sem, own_sem):
    group = lax.axis_size("dp")
    me = lax.axis_index("dp")
    barrier = pltpu.get_barrier_semaphore()
    for step in range(1, group):
        pl.semaphore_signal(
            barrier, inc=1, device_id={"dp": lax.rem(me + step, group)}, device_id_type=MESH
        )
    own = pltpu.make_async_copy(send_ref.at[me], recv_ref.at[me], own_sem)
    own.start()
    pl.semaphore_wait(barrier, group - 1)
    copies = []
    for step in range(1, group):
        peer = lax.rem(me + step, group)
        copy = pltpu.make_async_remote_copy(
            src_ref=send_ref.at[peer],
            dst_ref=recv_ref.at[me],
            send_sem=send_sem.at[step],
            recv_sem=recv_sem.at[step],
            device_id={"dp": peer},
            device_id_type=MESH,
        )
        copy.start()
        copies.append(copy)
    own.wait()
    for copy in copies:
        copy.wait()


def layer_kernel(
    len_ref,
    recv_ref,
    win_ref,
    wout_ref,
    out_ref,
    *rest,
):
    xn_out, gproj, gated_out, g_out, act, slope_p, attn, slope_s = rest
    group, slots, packed = recv_ref.shape
    width = wout_ref.shape[0]
    rows = act.shape[0]
    head = width // HEADS
    scale = 1.0 / head**0.5
    total = group * slots
    got = recv_ref[...].reshape(total, packed)
    place = got[:, 2 * width : 2 * width + 1].astype(F32) - 1.0
    spots = lax.broadcasted_iota(jnp.int32, (total, rows), 1).astype(F32)
    pick = jnp.where(place == spots, 1.0, 0.0).astype(BF16)
    tokens = tn(pick, got[:, :width])
    grad = tn(pick, got[:, width : 2 * width])
    grad16 = grad.astype(BF16)
    normed, inverse = normalize(tokens)
    xn = normed.astype(BF16)
    for block in range(4):
        cols = slice(block * width, (block + 1) * width)
        proj = nn(xn, win_ref[:, cols])
        sig = jax.nn.sigmoid(proj)
        act[:, cols] = (proj * sig).astype(BF16)
        slope_p[:, cols] = sig * (1.0 + proj * (1.0 - sig))
    row_at = lax.broadcasted_iota(jnp.int32, (rows, 1), 0)
    col_at = lax.broadcasted_iota(jnp.int32, (1, rows), 1)
    bound = jnp.int32(0)
    row_seg = jnp.zeros((rows, 1), jnp.int32)
    col_seg = jnp.zeros((1, rows), jnp.int32)
    for seq in range(len_ref.shape[1]):
        bound = bound + len_ref[0, seq]
        row_seg = row_seg + jnp.where(row_at >= bound, 1, 0)
        col_seg = col_seg + jnp.where(col_at >= bound, 1, 0)
    mask = (row_seg == col_seg) & (col_at <= row_at)
    pair = 2 * head
    low = lax.broadcasted_iota(jnp.int32, (rows, pair), 1) < head

    def half(values, which):
        return jnp.where(low if which == 0 else ~low, values, jnp.zeros_like(values))

    def cut(block, duo):
        start = block * width + duo * pair
        return act[:, start : start + pair]

    outs = []
    for duo in range(HEADS // 2):
        value, query, key = cut(1, duo), cut(2, duo), cut(3, duo)
        parts = []
        for which in range(2):
            at = 2 * duo + which
            scores = nt(half(query, which), key) * scale
            sig = jax.nn.sigmoid(scores)
            weight = jnp.where(mask, scores * sig * (1.0 / MAXLEN), 0.0).astype(BF16)
            attn[at] = weight
            slope_s[at] = jnp.where(
                mask, sig * (1.0 + scores * (1.0 - sig)) * (scale / MAXLEN), 0.0
            )
            parts.append(nn(weight, value))
        outs.append(jnp.where(low, parts[0], parts[1]))
    onorm, oinv = normalize(jnp.concatenate(outs, axis=1))
    gate = act[:, :width].astype(F32)
    gated = (gate * onorm).astype(BF16)
    grad_z = nt(grad16, wout_ref[...])
    gproj[:, :width] = (grad_z * onorm * slope_p[:, :width]).astype(BF16)
    grad_out = norm_back(grad_z * gate, onorm, oinv).astype(BF16)
    for duo in range(HEADS // 2):
        value, query, key = cut(1, duo), cut(2, duo), cut(3, duo)
        gout = grad_out[:, duo * pair : (duo + 1) * pair]
        parts = ([], [], [])
        for which in range(2):
            at = 2 * duo + which
            gscore = (nt(half(gout, which), value) * slope_s[at]).astype(BF16)
            parts[0].append(tn(attn[at], gout))
            parts[1].append(nn(gscore, key))
            parts[2].append(tn(gscore, query))
        for block in range(3):
            start = (block + 1) * width + duo * pair
            cols = slice(start, start + pair)
            both = jnp.where(low, parts[block][0], parts[block][1])
            gproj[:, cols] = (both * slope_p[:, cols]).astype(BF16)
    grad_xn = nt(gproj[...], win_ref[...])
    grad_tokens = (grad + norm_back(grad_xn, normed, inverse)).astype(BF16)
    out_ref[...] = nn(pick, grad_tokens).astype(BF16).reshape(group, slots, width)
    xn_out[...] = xn
    gated_out[...] = gated
    g_out[...] = grad16


def whole_kernel(
    slots,
    factor,
    len_ref,
    dest_ref,
    pos_ref,
    ev_ref,
    ct_ref,
    win_any,
    wout_any,
    grad_ref,
    in_ref,
    sum_ref,
    final_ref,
    win_ref,
    wout_ref,
    pick_ref,
    back_ref,
    ev_send,
    ct_send,
    at_send,
    ev_got,
    ct_got,
    at_got,
    act,
    slope_p,
    gproj,
    attn,
    slope_s,
    xn_ref,
    out_ref,
    b_ref,
    give_ref,
    keep_ref,
    core_got,
    one_send,
    one_got,
    two_keep,
    two_send,
    two_got,
    dp_sum,
    z_got,
    own_sems,
    win_sem,
    wout_sem,
    row_send,
    row_recv,
    core_send,
    core_recv,
    one_ssem,
    one_rsem,
    two_ssem,
    two_rsem,
    z_send,
    z_recv,
    all_send,
    all_recv,
    fwd_send,
    fwd_recv,
):
    rows, width = ev_ref.shape
    group = ev_send.shape[0]
    chain = keep_ref.shape[0]
    total = group * slots
    head = width // HEADS
    scale = 1.0 / head**0.5
    me = lax.axis_index("dp")
    rep = lax.axis_index("replica")
    core = lax.rem(rep, 2)
    other = 1 - core
    spot = rep // 2
    partner = {"replica": spot * 2 + other}
    low_bit, high_bit = lax.rem(me, 2), me // 2
    near = high_bit * 2 + 1 - low_bit
    far = (1 - high_bit) * 2 + low_bit
    first = other * near + core * far
    second = core * near + other * far
    third = 3 - me

    def dp_peer(step):
        return lax.rem(me + step, group)

    def z_peer(step):
        return lax.rem(spot + step, chain)

    def z_id(step):
        return {"replica": z_peer(step) * 2 + core}

    win_copy = pltpu.make_async_copy(win_any, win_ref, win_sem)
    wout_copy = pltpu.make_async_copy(wout_any, wout_ref, wout_sem)
    barrier = pltpu.get_barrier_semaphore()
    for step in range(1, group):
        pl.semaphore_signal(barrier, inc=1, device_id={"dp": dp_peer(step)}, device_id_type=MESH)
    pl.semaphore_signal(barrier, inc=1, device_id=partner, device_id_type=MESH)
    for step in range(1, chain):
        pl.semaphore_signal(barrier, inc=1, device_id=z_id(step), device_id_type=MESH)

    def send(src, dst, sems, at, device):
        copy = pltpu.make_async_remote_copy(
            src_ref=src,
            dst_ref=dst,
            send_sem=sems[0].at[at],
            recv_sem=sems[1].at[at],
            device_id=device,
            device_id_type=MESH,
        )
        copy.start()
        return copy

    dest = dest_ref[...]
    hot = lax.broadcasted_iota(jnp.int32, (8, rows), 0) == dest
    upper = lax.broadcasted_iota(jnp.int32, (rows, rows), 0) < lax.broadcasted_iota(
        jnp.int32, (rows, rows), 1
    )
    earlier = nn(
        jnp.where(hot, 1.0, 0.0).astype(BF16), jnp.where(upper, 1.0, 0.0).astype(BF16)
    )
    slot = jnp.sum(jnp.where(hot, earlier, 0.0), axis=0, keepdims=True).astype(jnp.int32)
    slot_iota = lax.broadcasted_iota(jnp.int32, (total, rows), 0)
    pick = jnp.where(slot_iota == dest * slots + slot, 1.0, 0.0).astype(BF16)
    pick_ref[...] = pick
    packed = (group, slots, width)
    ev_send[...] = nn(pick, ev_ref[...]).astype(BF16).reshape(packed)
    win_copy.start()
    wout_copy.start()
    pl.semaphore_wait(barrier, group + chain - 1)
    row_copies = ([], [], [])
    own_copies = []

    def rows_out(kind, src, dst):
        for step in range(1, group):
            peer = dp_peer(step)
            row_copies[kind].append(
                send(
                    src.at[peer],
                    dst.at[me],
                    (row_send, row_recv),
                    kind * group + step,
                    {"dp": peer},
                )
            )
        own = pltpu.make_async_copy(src.at[me], dst.at[me], own_sems.at[kind])
        own.start()
        own_copies.append(own)

    rows_out(0, ev_send, ev_got)
    spots = jnp.broadcast_to(pos_ref[...] + 1, (8, rows)).astype(F32).astype(BF16)
    landing = slot_iota == me * slots + slot
    for dp in range(group):
        there = jnp.where(landing & (dest == dp), 1.0, 0.0).astype(BF16)
        at_send[dp] = nt(spots, there)
    rows_out(1, at_send, at_got)
    ct_send[...] = nn(pick, ct_ref[...]).astype(BF16).reshape(packed)
    rows_out(2, ct_send, ct_got)

    for kind in range(2):
        own_copies[kind].wait()
        for copy in row_copies[kind]:
            copy.wait_recv()
    place = at_got[0]
    for dp in range(1, group):
        place = place + at_got[dp]
    row_iota = lax.broadcasted_iota(jnp.int32, (rows, total), 0).astype(F32) + 1.0
    fetch = jnp.where(row_iota == place[:1], 1.0, 0.0).astype(BF16)
    tokens = nn(fetch, ev_got[...].reshape(total, width))
    normed, inverse = normalize(tokens)
    xn = normed.astype(BF16)
    xn_ref[...] = xn
    win_copy.wait()
    wout_copy.wait()
    for block in range(4):
        cols = slice(block * width, (block + 1) * width)
        proj = nn(xn, win_ref[:, cols])
        sig = jax.nn.sigmoid(proj)
        act[:, cols] = (proj * sig).astype(BF16)
        slope_p[:, cols] = sig * (1.0 + proj * (1.0 - sig))
    row_at = lax.broadcasted_iota(jnp.int32, (rows, 1), 0)
    col_at = lax.broadcasted_iota(jnp.int32, (1, rows), 1)
    bound = jnp.int32(0)
    row_seg = jnp.zeros((rows, 1), jnp.int32)
    col_seg = jnp.zeros((1, rows), jnp.int32)
    for seq in range(len_ref.shape[1]):
        bound = bound + len_ref[0, seq]
        row_seg = row_seg + jnp.where(row_at >= bound, 1, 0)
        col_seg = col_seg + jnp.where(col_at >= bound, 1, 0)
    mask = (row_seg == col_seg) & (col_at <= row_at)
    pair = 2 * head
    low = lax.broadcasted_iota(jnp.int32, (rows, pair), 1) < head

    def half(values, which):
        return jnp.where(low if which == 0 else ~low, values, jnp.zeros_like(values))

    def cut(block, duo):
        start = block * width + duo * pair
        return act[:, start : start + pair]

    outs = []
    for duo in range(HEADS // 2):
        value, query, key = cut(1, duo), cut(2, duo), cut(3, duo)
        parts = []
        for which in range(2):
            at = 2 * duo + which
            scores = nt(half(query, which), key) * scale
            sig = jax.nn.sigmoid(scores)
            weight = jnp.where(mask, scores * sig * (1.0 / MAXLEN), 0.0).astype(BF16)
            attn[at] = weight
            slope_s[at] = jnp.where(
                mask, sig * (1.0 + scores * (1.0 - sig)) * (scale / MAXLEN), 0.0
            )
            parts.append(nn(weight, value))
        outs.append(jnp.where(low, parts[0], parts[1]))
    onorm, oinv = normalize(jnp.concatenate(outs, axis=1))
    gate = act[:, :width].astype(F32)
    gated = (gate * onorm).astype(BF16)

    own_copies[2].wait()
    for copy in row_copies[2]:
        copy.wait_recv()
    grad = nn(fetch, ct_got[...].reshape(total, width))
    grad16 = grad.astype(BF16)
    grad_z = nt(grad16, wout_ref[...])
    gproj[:, :width] = (grad_z * onorm * slope_p[:, :width]).astype(BF16)
    share_in = width // (2 * chain)
    share_out = width // (group * 2 * chain)
    whole_out = tn(gated, grad16).astype(BF16).reshape(group, 2, chain, share_out, width)
    for dp in range(group):
        b_ref[:, :, dp] = whole_out[dp]
    grad_out = norm_back(grad_z * gate, onorm, oinv).astype(BF16)
    for duo in range(HEADS // 2):
        value, query, key = cut(1, duo), cut(2, duo), cut(3, duo)
        gout = grad_out[:, duo * pair : (duo + 1) * pair]
        parts = ([], [], [])
        for which in range(2):
            at = 2 * duo + which
            gscore = (nt(half(gout, which), value) * slope_s[at]).astype(BF16)
            parts[0].append(tn(attn[at], gout))
            parts[1].append(nn(gscore, key))
            parts[2].append(tn(gscore, query))
        for block in range(3):
            start = (block + 1) * width + duo * pair
            cols = slice(start, start + pair)
            both = jnp.where(low, parts[block][0], parts[block][1])
            gproj[:, cols] = (both * slope_p[:, cols]).astype(BF16)

    wave = width // COLORS

    def lanes(color):
        return slice(color * wave, (color + 1) * wave)

    def partials(which, into, color):
        across = width // 2
        columns = pl.ds(pl.multiple_of(which * across, across), across)
        left = xn_ref[:, columns]
        for dp in range(group):
            start = dp * width + color * wave
            shard = tn(left, gproj[:, start : start + wave]).astype(BF16)
            into[:, dp, :share_in, lanes(color)] = shard.reshape(chain, share_in, wave)
        into[:, :, share_in:, lanes(color)] = b_ref[which, :, :, :, lanes(color)]

    core_copies, one_copies, two_copies, z_copies = [], [], [], []
    for color in range(COLORS):
        partials(other, give_ref, color)
        for hop in range(1, chain + 1):
            step = color * chain + hop - 1
            core_copies.append(
                send(
                    give_ref.at[z_peer(hop), :, :, lanes(color)],
                    core_got.at[step],
                    (core_send, core_recv),
                    step,
                    partner,
                )
            )

    def stage_one(step):
        at = z_peer(step % chain + 1)
        cols = lanes(step // chain)
        core_copies[step].wait_recv()

        def both(dp):
            return keep_ref[at, dp, :, cols].astype(F32) + core_got[step, dp].astype(F32)

        one_send[step, 0] = both(first).astype(BF16)
        one_send[step, 1] = both(third).astype(BF16)
        one_copies.append(
            send(one_send.at[step], one_got.at[step], (one_ssem, one_rsem), step, {"dp": first})
        )
        two_keep[step, 0] = both(me)
        two_keep[step, 1] = both(second)

    def stage_two(step):
        one_copies[step].wait_recv()
        two_send[step] = (two_keep[step, 1] + one_got[step, 1].astype(F32)).astype(BF16)
        two_copies.append(
            send(two_send.at[step], two_got.at[step], (two_ssem, two_rsem), step, {"dp": second})
        )

    def stage_three(step):
        two_copies[step].wait_recv()
        dp_sum[step] = (
            two_keep[step, 0] + one_got[step, 0].astype(F32) + two_got[step].astype(F32)
        ).astype(BF16)
        hop = step % chain + 1
        if hop < chain:
            z_copies.append(
                send(dp_sum.at[step], z_got.at[step], (z_send, z_recv), step, z_id(hop))
            )

    all_copies, fwd_copies = [], []

    def stage_four(color):
        summed = dp_sum[color * chain + chain - 1].astype(F32)
        for hop in range(1, chain):
            z_copies[color * (chain - 1) + hop - 1].wait_recv()
            summed = summed + z_got[color * chain + hop - 1].astype(F32)
        final_ref[core, spot, :, lanes(color)] = summed.astype(BF16)
        mine = final_ref.at[core, spot, :, lanes(color)]
        for hop in range(1, chain):
            all_copies.append(
                send(mine, mine, (all_send, all_recv), color * chain + hop, z_id(hop))
            )
        fwd_copies.append(send(mine, mine, (fwd_send, fwd_recv), color * chain, partner))

    def stage_five(color):
        for hop in range(1, chain):
            all_copies[color * (chain - 1) + hop - 1].wait_recv()
            came = lax.rem(spot - hop + chain, chain)
            there = final_ref.at[core, came, :, lanes(color)]
            fwd_copies.append(send(there, there, (fwd_send, fwd_recv), color * chain + hop, partner))

    for color in range(COLORS):
        partials(core, keep_ref, color)
        for hop in range(chain):
            stage_one(color * chain + hop)

    grad_xn = nt(gproj[...], win_ref[...])
    grad_tokens = (grad + norm_back(grad_xn, normed, inverse)).astype(BF16)
    out_ref[...] = tn(fetch, grad_tokens).astype(BF16).reshape(packed)
    for step in range(COLORS * chain):
        stage_two(step)
        if step > 0:
            stage_three(step - 1)
        if step > chain and step % chain == 1:
            stage_four(step // chain - 1)
    ret_copies = [
        send(
            out_ref.at[dp_peer(step)],
            back_ref.at[me],
            (row_send, row_recv),
            3 * group + step,
            {"dp": dp_peer(step)},
        )
        for step in range(1, group)
    ]
    own = pltpu.make_async_copy(out_ref.at[me], back_ref.at[me], own_sems.at[3])
    own.start()
    stage_three(COLORS * chain - 1)
    stage_four(COLORS - 1)
    for color in range(COLORS - 1):
        stage_five(color)
    own.wait()
    for copy in ret_copies:
        copy.wait_recv()
    grad_ref[...] = tn(pick_ref[...], back_ref[...].reshape(total, width)).astype(BF16)
    stage_five(COLORS - 1)
    for copy in fwd_copies:
        copy.wait_recv()
    share = width // (2 * chain)
    in_ref[...] = (final_ref[:, :, :share, :].astype(F32) * factor).reshape(in_ref.shape)
    sum_ref[...] = (final_ref[:, :, share:, :].astype(F32) * factor).reshape(sum_ref.shape)
    for copies in row_copies + (
        core_copies,
        one_copies,
        two_copies,
        z_copies,
        all_copies,
        fwd_copies,
        ret_copies,
    ):
        for copy in copies:
            copy.wait_send()


def finish_kernel(*refs):
    count = len(refs) // 2
    sources, outs, sems = refs[:count], refs[count : 2 * count], refs[2 * count]
    copies = [
        pltpu.make_async_copy(sources[at], outs[at], sems.at[at]) for at in range(count)
    ]
    for copy in copies:
        copy.start()
    for copy in copies:
        copy.wait()


def gather_kernel(pick_ref, back_ref, ev_ref):
    group, slots, width = back_ref.shape
    ev_ref[...] = tn(pick_ref[...], back_ref[...].reshape(group * slots, width)).astype(BF16)


VMEM = pl.BlockSpec(memory_space=pltpu.VMEM)
SMEM = pl.BlockSpec(memory_space=pltpu.SMEM)


def shape_of(shape, dtype=BF16):
    return jax.ShapeDtypeStruct(shape, dtype)


def swap(send, ident):
    group = send.shape[0]
    return pl.pallas_call(
        swap_kernel,
        out_shape=shape_of(send.shape),
        in_specs=[VMEM],
        out_specs=VMEM,
        scratch_shapes=[
            pltpu.SemaphoreType.DMA((group,)),
            pltpu.SemaphoreType.DMA((group,)),
            pltpu.SemaphoreType.DMA,
        ],
        compiler_params=pltpu.CompilerParams(collective_id=ident, has_side_effects=True),
        name="swap",
    )(send)


def body(events, cotangent, weight_in, weight_out, plan_dest, plan_pos, seq_lengths):
    group = lax.axis_size("dp")
    replicas = lax.axis_size("replica")
    rows, width = events.shape
    inner = weight_in.shape[1]
    slots = 3 * rows // (2 * group)
    total = group * slots
    chain = replicas // 2
    stacked = group == 4 and inner == group * width and width % (group * replicas * 16) == 0
    factor = 1.0 / (rows * group * replicas) ** 0.5
    outgoing_shape = shape_of((group, slots, width))
    wide = [
        pltpu.VMEM((rows, inner), BF16),
        pltpu.VMEM((rows, inner), F32),
    ]
    square = [
        pltpu.VMEM((HEADS, rows, rows), BF16),
        pltpu.VMEM((HEADS, rows, rows), F32),
    ]
    dest, place = plan_dest.reshape(1, rows), plan_pos.reshape(1, rows)
    if stacked:
        share_out = width // (group * replicas)
        depth = width // replicas + share_out
        piece = (depth, width)
        packed = pltpu.VMEM((group, slots, width), BF16)
        spots = pltpu.VMEM((group, 8, total), F32)
        halves = pltpu.VMEM((chain, group) + piece, BF16)
        count = COLORS * chain
        wave = (depth, width // COLORS)
        dma = pltpu.SemaphoreType.DMA
        results = pl.pallas_call(
            functools.partial(whole_kernel, slots, factor),
            out_shape=(
                pltpu.VMEM((rows, width), BF16),
                pltpu.VMEM((width, width), F32),
                pltpu.VMEM((width // group, width), F32),
            ),
            in_specs=[SMEM] + [VMEM] * 4 + [pl.BlockSpec(memory_space=pl.ANY)] * 2,
            out_specs=(VMEM,) * 3,
            scratch_shapes=[
                pltpu.VMEM((2, chain) + piece, BF16),
                pltpu.VMEM(weight_in.shape, BF16),
                pltpu.VMEM(weight_out.shape, BF16),
                pltpu.VMEM((total, rows), BF16),
                packed,
            ]
            + [packed, packed, spots] * 2
            + wide
            + [pltpu.VMEM((rows, inner), BF16)]
            + square
            + [
                pltpu.VMEM((rows, width), BF16),
                packed,
                pltpu.VMEM((2, chain, group, share_out, width), BF16),
                halves,
                halves,
                pltpu.VMEM((count, group) + wave, BF16),
                pltpu.VMEM((count, 2) + wave, BF16),
                pltpu.VMEM((count, 2) + wave, BF16),
                pltpu.VMEM((count, 2) + wave, F32),
                pltpu.VMEM((count,) + wave, BF16),
                pltpu.VMEM((count,) + wave, BF16),
                pltpu.VMEM((count,) + wave, BF16),
                pltpu.VMEM((count,) + wave, BF16),
                dma((4,)),
                dma,
                dma,
                dma((4 * group,)),
                dma((4 * group,)),
            ]
            + [dma((count,))] * 12,
            compiler_params=pltpu.CompilerParams(collective_id=0, has_side_effects=True),
            name="whole",
        )(seq_lengths, dest, place, events, cotangent, weight_in, weight_out)
        return pl.pallas_call(
            finish_kernel,
            out_shape=tuple(shape_of(value.shape, value.dtype) for value in results),
            in_specs=[VMEM] * 3,
            out_specs=(pl.BlockSpec(memory_space=pltpu.HBM),) * 3,
            scratch_shapes=[pltpu.SemaphoreType.DMA((3,))],
            name="finish",
        )(*[pltpu.with_memory_space_constraint(value, pltpu.VMEM) for value in results])
    send, pick = pl.pallas_call(
        functools.partial(prep_kernel, slots),
        out_shape=(shape_of((group, slots, 2 * width + LANES)), shape_of((total, rows))),
        in_specs=[VMEM] * 4,
        out_specs=(VMEM, VMEM),
        name="prep",
    )(dest, place, events, cotangent)
    recv = swap(send, 0)
    outgoing, normed_in, grad_proj, gated, grad_rows = pl.pallas_call(
        layer_kernel,
        out_shape=(
            outgoing_shape,
            shape_of((rows, width)),
            shape_of((rows, inner)),
            shape_of((rows, width)),
            shape_of((rows, width)),
        ),
        in_specs=[SMEM] + [VMEM] * 3,
        out_specs=(VMEM,) * 5,
        scratch_shapes=wide + square,
        name="layer",
    )(seq_lengths, recv, weight_in, weight_out)
    back = swap(outgoing, 1)
    grad_events = pl.pallas_call(
        gather_kernel,
        out_shape=shape_of((rows, width)),
        in_specs=[VMEM] * 2,
        out_specs=VMEM,
        name="finish",
    )(pick, back)
    rows_all = lax.all_gather(normed_in, "dp", axis=0, tiled=True)
    cot_all = lax.all_gather(grad_rows, "dp", axis=0, tiled=True)
    proj_cols = lax.all_to_all(grad_proj, "dp", split_axis=1, concat_axis=0, tiled=True)
    gated_cols = lax.all_to_all(gated, "dp", split_axis=1, concat_axis=0, tiled=True)
    shard_in = jnp.einsum("rd,rf->df", rows_all, proj_cols, preferred_element_type=F32)
    shard_out = jnp.einsum("re,rd->ed", gated_cols, cot_all, preferred_element_type=F32)
    total_in, total_out = lax.psum((shard_in, shard_out), "replica")
    return grad_events, total_in * factor, total_out * factor


def solution(mesh):
    return jax.shard_map(
        body,
        mesh=mesh,
        in_specs=(
            P(("dp", "replica"), None),
            P(("dp", "replica"), None),
            P(),
            P(),
            P(("dp", "replica")),
            P(("dp", "replica")),
            P(("dp", "replica"), None),
        ),
        out_specs=(P(("dp", "replica"), None), P(None, "dp"), P("dp", None)),
        check_vma=False,
    )
```

```python
import functools

import jax
import jax.numpy as jnp
from jax import lax
from jax.experimental import pallas as pl
from jax.experimental.pallas import tpu as pltpu
from jax.sharding import PartitionSpec as P

HEADS = 8
MAXLEN = 128
EPS = 1e-05
RELAYED = 3
LANES = 128
MESH = pl.DeviceIdType.MESH
F32 = jnp.float32
BF16 = jnp.bfloat16


def contract(left, right, dims):
    return lax.dot_general(left, right, ((dims[:1], dims[1:]), ((), ())), preferred_element_type=F32)


def nn(left, right):
    return contract(left, right, (1, 0))


def nt(left, right):
    return contract(left, right, (1, 1))


def tn(left, right):
    return contract(left, right, (0, 0))


def normalize(values):
    center = values - jnp.mean(values, axis=-1, keepdims=True)
    inverse = lax.rsqrt(jnp.mean(center * center, axis=-1, keepdims=True) + EPS)
    return center * inverse, inverse


def norm_back(grad, normed, inverse):
    return inverse * (
        grad
        - jnp.mean(grad, axis=-1, keepdims=True)
        - normed * jnp.mean(grad * normed, axis=-1, keepdims=True)
    )


def prep_kernel(slot_count, dest_ref, pos_ref, ev_ref, ct_ref, send_ref, pick_ref):
    rows, width = ev_ref.shape
    group = send_ref.shape[0]
    dest = dest_ref[...]
    hot = lax.broadcasted_iota(jnp.int32, (8, rows), 0) == dest
    upper = lax.broadcasted_iota(jnp.int32, (rows, rows), 0) < lax.broadcasted_iota(
        jnp.int32, (rows, rows), 1
    )
    earlier = nn(
        jnp.where(hot, 1.0, 0.0).astype(BF16), jnp.where(upper, 1.0, 0.0).astype(BF16)
    )
    slot = jnp.sum(jnp.where(hot, earlier, 0.0), axis=0, keepdims=True).astype(jnp.int32)
    flat = dest * slot_count + slot
    total = group * slot_count
    chosen = lax.broadcasted_iota(jnp.int32, (total, rows), 0) == flat
    pick = jnp.where(chosen, 1.0, 0.0).astype(BF16)
    pick_ref[...] = pick
    place = jnp.sum(
        jnp.where(chosen, pos_ref[...].astype(F32) + 1.0, 0.0), axis=1, keepdims=True
    )
    shape = (group, slot_count)
    send_ref[:, :, :width] = nn(pick, ev_ref[...]).astype(BF16).reshape(shape + (width,))
    send_ref[:, :, width : 2 * width] = nn(pick, ct_ref[...]).astype(BF16).reshape(shape + (width,))
    send_ref[:, :, 2 * width :] = (
        jnp.broadcast_to(place, (total, LANES)).astype(BF16).reshape(shape + (LANES,))
    )


def swap_kernel(send_ref, recv_ref, send_sem, recv_sem, own_sem):
    group = lax.axis_size("dp")
    me = lax.axis_index("dp")
    barrier = pltpu.get_barrier_semaphore()
    for step in range(1, group):
        pl.semaphore_signal(
            barrier, inc=1, device_id={"dp": lax.rem(me + step, group)}, device_id_type=MESH
        )
    own = pltpu.make_async_copy(send_ref.at[me], recv_ref.at[me], own_sem)
    own.start()
    pl.semaphore_wait(barrier, group - 1)
    copies = []
    for step in range(1, group):
        peer = lax.rem(me + step, group)
        copy = pltpu.make_async_remote_copy(
            src_ref=send_ref.at[peer],
            dst_ref=recv_ref.at[me],
            send_sem=send_sem.at[step],
            recv_sem=recv_sem.at[step],
            device_id={"dp": peer},
            device_id_type=MESH,
        )
        copy.start()
        copies.append(copy)
    own.wait()
    for copy in copies:
        copy.wait()


def layer_kernel(
    len_ref,
    recv_ref,
    win_ref,
    wout_ref,
    out_ref,
    *rest,
):
    xn_out, gproj, gated_out, g_out, act, slope_p, attn, slope_s = rest
    group, slots, packed = recv_ref.shape
    width = wout_ref.shape[0]
    rows = act.shape[0]
    head = width // HEADS
    scale = 1.0 / head**0.5
    total = group * slots
    got = recv_ref[...].reshape(total, packed)
    place = got[:, 2 * width : 2 * width + 1].astype(F32) - 1.0
    spots = lax.broadcasted_iota(jnp.int32, (total, rows), 1).astype(F32)
    pick = jnp.where(place == spots, 1.0, 0.0).astype(BF16)
    tokens = tn(pick, got[:, :width])
    grad = tn(pick, got[:, width : 2 * width])
    grad16 = grad.astype(BF16)
    normed, inverse = normalize(tokens)
    xn = normed.astype(BF16)
    for block in range(4):
        cols = slice(block * width, (block + 1) * width)
        proj = nn(xn, win_ref[:, cols])
        sig = jax.nn.sigmoid(proj)
        act[:, cols] = (proj * sig).astype(BF16)
        slope_p[:, cols] = sig * (1.0 + proj * (1.0 - sig))
    row_at = lax.broadcasted_iota(jnp.int32, (rows, 1), 0)
    col_at = lax.broadcasted_iota(jnp.int32, (1, rows), 1)
    bound = jnp.int32(0)
    row_seg = jnp.zeros((rows, 1), jnp.int32)
    col_seg = jnp.zeros((1, rows), jnp.int32)
    for seq in range(len_ref.shape[1]):
        bound = bound + len_ref[0, seq]
        row_seg = row_seg + jnp.where(row_at >= bound, 1, 0)
        col_seg = col_seg + jnp.where(col_at >= bound, 1, 0)
    mask = (row_seg == col_seg) & (col_at <= row_at)
    pair = 2 * head
    low = lax.broadcasted_iota(jnp.int32, (rows, pair), 1) < head

    def half(values, which):
        return jnp.where(low if which == 0 else ~low, values, jnp.zeros_like(values))

    def cut(block, duo):
        start = block * width + duo * pair
        return act[:, start : start + pair]

    outs = []
    for duo in range(HEADS // 2):
        value, query, key = cut(1, duo), cut(2, duo), cut(3, duo)
        parts = []
        for which in range(2):
            at = 2 * duo + which
            scores = nt(half(query, which), key) * scale
            sig = jax.nn.sigmoid(scores)
            weight = jnp.where(mask, scores * sig * (1.0 / MAXLEN), 0.0).astype(BF16)
            attn[at] = weight
            slope_s[at] = jnp.where(
                mask, sig * (1.0 + scores * (1.0 - sig)) * (scale / MAXLEN), 0.0
            )
            parts.append(nn(weight, value))
        outs.append(jnp.where(low, parts[0], parts[1]))
    onorm, oinv = normalize(jnp.concatenate(outs, axis=1))
    gate = act[:, :width].astype(F32)
    gated = (gate * onorm).astype(BF16)
    grad_z = nt(grad16, wout_ref[...])
    gproj[:, :width] = (grad_z * onorm * slope_p[:, :width]).astype(BF16)
    grad_out = norm_back(grad_z * gate, onorm, oinv).astype(BF16)
    for duo in range(HEADS // 2):
        value, query, key = cut(1, duo), cut(2, duo), cut(3, duo)
        gout = grad_out[:, duo * pair : (duo + 1) * pair]
        parts = ([], [], [])
        for which in range(2):
            at = 2 * duo + which
            gscore = (nt(half(gout, which), value) * slope_s[at]).astype(BF16)
            parts[0].append(tn(attn[at], gout))
            parts[1].append(nn(gscore, key))
            parts[2].append(tn(gscore, query))
        for block in range(3):
            start = (block + 1) * width + duo * pair
            cols = slice(start, start + pair)
            both = jnp.where(low, parts[block][0], parts[block][1])
            gproj[:, cols] = (both * slope_p[:, cols]).astype(BF16)
    grad_xn = nt(gproj[...], win_ref[...])
    grad_tokens = (grad + norm_back(grad_xn, normed, inverse)).astype(BF16)
    out_ref[...] = nn(pick, grad_tokens).astype(BF16).reshape(group, slots, width)
    xn_out[...] = xn
    gated_out[...] = gated
    g_out[...] = grad16


def whole_kernel(
    slots,
    factor,
    len_any,
    dest_any,
    pos_any,
    ev_any,
    ct_any,
    win_any,
    wout_any,
    grad_ref,
    in_ref,
    sum_ref,
    final_ref,
    len_ref,
    dest_ref,
    pos_ref,
    ev_ref,
    ct_ref,
    win_ref,
    wout_ref,
    pick_ref,
    back_ref,
    ev_send,
    ct_send,
    at_send,
    ev_got,
    ct_got,
    at_got,
    act,
    slope_p,
    gproj,
    attn,
    slope_s,
    xn_ref,
    out_ref,
    part_ref,
    core_got,
    one_send,
    one_got,
    two_keep,
    two_send,
    two_got,
    up_send,
    rs_got,
    load_sems,
    row_ssem,
    row_rsem,
    core_ssem,
    core_rsem,
    one_ssem,
    one_rsem,
    two_ssem,
    two_rsem,
    up_ssem,
    up_rsem,
    mid_rsem,
    mate_ssem,
    rim_ssem,
    ag_rsem,
    fwd_ssem,
    fwd_rsem,
):
    rows, width = ev_ref.shape
    group = ev_send.shape[0]
    colors, depth, span = rs_got.shape[0], rs_got.shape[3], rs_got.shape[4]
    total = group * slots
    head = width // HEADS
    scale = 1.0 / head**0.5
    me = lax.axis_index("dp")
    rep = lax.axis_index("replica")
    core = lax.rem(rep, 2)
    other = 1 - core
    spot = rep // 2
    partner = {"replica": spot * 2 + other}
    low_bit, high_bit = lax.rem(me, 2), me // 2
    near = high_bit * 2 + 1 - low_bit
    far = (1 - high_bit) * 2 + low_bit
    third = 3 - me

    def dp_peer(step):
        return lax.rem(me + step, group)

    side = spot // 2
    away = 1 - side
    inner = (spot == 1) | (spot == 2)
    outer = ~inner
    hub = {"replica": (1 + side) * 2 + core}
    mate = {"replica": (3 - spot) * 2 + core}
    rim = {"replica": 3 * side * 2 + core}
    far_hub = {"replica": (2 - side) * 2 + core}
    far_rim = {"replica": 3 * away * 2 + core}

    loads = [
        pltpu.make_async_copy(source, target, load_sems.at[at])
        for at, (source, target) in enumerate(
            (
                (ev_any, ev_ref),
                (ct_any, ct_ref),
                (win_any, win_ref),
                (wout_any, wout_ref),
                (dest_any, dest_ref),
                (pos_any, pos_ref),
                (len_any, len_ref),
            )
        )
    ]
    for at in (4, 0, 5, 1, 6):
        loads[at].start()
    barrier = pltpu.get_barrier_semaphore()
    for step in range(1, group):
        pl.semaphore_signal(barrier, inc=1, device_id={"dp": dp_peer(step)}, device_id_type=MESH)
    pl.semaphore_signal(barrier, inc=1, device_id=partner, device_id_type=MESH)

    @pl.when(outer)
    def _():
        for device in (hub, far_hub):
            pl.semaphore_signal(barrier, inc=1, device_id=device, device_id_type=MESH)

    @pl.when(inner)
    def _():
        for device in (mate, rim, far_rim):
            pl.semaphore_signal(barrier, inc=1, device_id=device, device_id_type=MESH)

    def describe(src, dst, ssem, rsem, device):
        return pltpu.make_async_remote_copy(
            src_ref=src,
            dst_ref=dst,
            send_sem=ssem,
            recv_sem=rsem,
            device_id=device,
            device_id_type=MESH,
        )

    def send(src, dst, ssem, rsem, device):
        describe(src, dst, ssem, rsem, device).start()

    def sent(like, ssem):
        describe(like, like, ssem, ssem, partner).wait_send()

    def came(like, rsem):
        describe(like, like, rsem, rsem, partner).wait_recv()

    loads[4].wait()
    dest = dest_ref[...]
    hot = lax.broadcasted_iota(jnp.int32, (8, rows), 0) == dest
    upper = lax.broadcasted_iota(jnp.int32, (rows, rows), 0) < lax.broadcasted_iota(
        jnp.int32, (rows, rows), 1
    )
    earlier = nn(
        jnp.where(hot, 1.0, 0.0).astype(BF16), jnp.where(upper, 1.0, 0.0).astype(BF16)
    )
    slot = jnp.sum(jnp.where(hot, earlier, 0.0), axis=0, keepdims=True).astype(jnp.int32)
    slot_iota = lax.broadcasted_iota(jnp.int32, (total, rows), 0)
    pick = jnp.where(slot_iota == dest * slots + slot, 1.0, 0.0).astype(BF16)
    pick_ref[...] = pick
    packed = (group, slots, width)
    loads[0].wait()
    ev_send[...] = nn(pick, ev_ref[...]).astype(BF16).reshape(packed)
    pl.semaphore_wait(barrier, group + 2 + jnp.where(inner, 1, 0))

    def rows_out(kind, src, dst):
        for step in (3, 1, 2):
            peer = step ^ me
            send(src.at[peer], dst.at[me], row_ssem.at[kind], row_rsem.at[kind], {"dp": peer})
        dst[me] = src[me]

    def others(buffer):
        return buffer.at[pl.ds(0, group - 1)]

    rows_out(1, ev_send, ev_got)
    loads[2].start()
    loads[3].start()
    loads[5].wait()
    spots = jnp.broadcast_to(pos_ref[...] + 1, (8, rows)).astype(F32).astype(BF16)
    lane_iota = lax.broadcasted_iota(jnp.int32, (LANES, rows), 0)
    for dp in range(group):
        there = jnp.where((lane_iota == slot) & (dest == dp), 1.0, 0.0).astype(BF16)
        at_send[dp] = nt(spots, there)
    rows_out(0, at_send, at_got)
    loads[1].wait()
    ct_send[...] = nn(pick, ct_ref[...]).astype(BF16).reshape(packed)
    sent(others(ev_send), row_ssem.at[1])
    rows_out(2, ct_send, ct_got)

    came(others(at_got), row_rsem.at[0])
    came(others(ev_got), row_rsem.at[1])
    place = jnp.zeros((8, total), F32)
    blank = jnp.zeros((8, total - LANES), F32)
    for dp in range(group):
        there = jnp.concatenate([at_got[dp], blank], axis=1)
        place = place + pltpu.roll(there, dp * slots, 1)
    row_iota = lax.broadcasted_iota(jnp.int32, (rows, total), 0).astype(F32) + 1.0
    fetch = jnp.where(row_iota == place[:1], 1.0, 0.0).astype(BF16)
    tokens = nn(fetch, ev_got[...].reshape(total, width))
    normed, inverse = normalize(tokens)
    xn = normed.astype(BF16)
    xn_ref[...] = xn
    loads[2].wait()
    loads[3].wait()
    for block in range(4):
        cols = slice(block * width, (block + 1) * width)
        proj = nn(xn, win_ref[:, cols])
        sig = jax.nn.sigmoid(proj)
        act[:, cols] = (proj * sig).astype(BF16)
        slope_p[:, cols] = sig * (1.0 + proj * (1.0 - sig))
    row_at = lax.broadcasted_iota(jnp.int32, (rows, 1), 0)
    col_at = lax.broadcasted_iota(jnp.int32, (1, rows), 1)
    loads[6].wait()
    bound = jnp.int32(0)
    row_seg = jnp.zeros((rows, 1), jnp.int32)
    col_seg = jnp.zeros((1, rows), jnp.int32)
    for seq in range(len_ref.shape[1]):
        bound = bound + len_ref[0, seq]
        row_seg = row_seg + jnp.where(row_at >= bound, 1, 0)
        col_seg = col_seg + jnp.where(col_at >= bound, 1, 0)
    mask = (row_seg == col_seg) & (col_at <= row_at)
    pair = 2 * head
    low = lax.broadcasted_iota(jnp.int32, (rows, pair), 1) < head

    def half(values, which):
        return jnp.where(low if which == 0 else ~low, values, jnp.zeros_like(values))

    def cut(block, duo):
        start = block * width + duo * pair
        return act[:, start : start + pair]

    outs = []
    for duo in range(HEADS // 2):
        value, query, key = cut(1, duo), cut(2, duo), cut(3, duo)
        parts = []
        for which in range(2):
            at = 2 * duo + which
            scores = nt(half(query, which), key) * scale
            sig = jax.nn.sigmoid(scores)
            weight = jnp.where(mask, scores * sig * (1.0 / MAXLEN), 0.0).astype(BF16)
            attn[at] = weight
            slope_s[at] = jnp.where(
                mask, sig * (1.0 + scores * (1.0 - sig)) * (scale / MAXLEN), 0.0
            )
            parts.append(nn(weight, value))
        outs.append(jnp.where(low, parts[0], parts[1]))
    onorm, oinv = normalize(jnp.concatenate(outs, axis=1))
    gate = act[:, :width].astype(F32)
    gated = (gate * onorm).astype(BF16)

    came(others(ct_got), row_rsem.at[2])
    grad = nn(fetch, ct_got[...].reshape(total, width))
    grad16 = grad.astype(BF16)

    def store_part(color, whole, row_of, column_of):
        for edge in range(2):
            for piece in range(4):
                for dp in range(group):
                    row, column = row_of(edge, piece, dp), column_of(edge, piece, dp)
                    part_ref[color, edge, piece % 2, piece // 2, dp] = whole[
                        row : row + depth, column : column + span
                    ]
        send(
            part_ref.at[color, other],
            core_got.at[color],
            core_ssem.at[0],
            core_rsem.at[color],
            partner,
        )

    store_part(
        0,
        tn(gated, grad16).astype(BF16),
        lambda edge, piece, dp: (2 * dp + edge) * depth,
        lambda edge, piece, dp: piece * span,
    )
    grad_z = nt(grad16, wout_ref[...])
    gproj[:, :width] = (grad_z * onorm * slope_p[:, :width]).astype(BF16)
    grad_out = norm_back(grad_z * gate, onorm, oinv).astype(BF16)

    def back_duo(duo):
        value, query, key = cut(1, duo), cut(2, duo), cut(3, duo)
        gout = grad_out[:, duo * pair : (duo + 1) * pair]
        parts = ([], [], [])
        for which in range(2):
            at = 2 * duo + which
            gscore = (nt(half(gout, which), value) * slope_s[at]).astype(BF16)
            parts[0].append(tn(attn[at], gout))
            parts[1].append(nn(gscore, key))
            parts[2].append(tn(gscore, query))
        for block in range(3):
            start = (block + 1) * width + duo * pair
            cols = slice(start, start + pair)
            both = jnp.where(low, parts[block][0], parts[block][1])
            gproj[:, cols] = (both * slope_p[:, cols]).astype(BF16)

    def stage_zero(duo):
        columns = jnp.concatenate(
            [
                gproj[:, dp * width + duo * span : dp * width + (duo + 1) * span]
                for dp in range(group)
            ],
            axis=1,
        )
        store_part(
            duo + 1,
            tn(xn_ref[...], columns).astype(BF16),
            lambda edge, piece, dp: (4 * edge + piece) * depth,
            lambda edge, piece, dp: dp * span,
        )

    def ways(way):
        return (near, far) if way == 0 else (far, near)

    def stage_one(color):
        came(core_got.at[color], core_rsem.at[color])
        for way in range(2):
            first, second = ways(way)

            def both(dp):
                mine = part_ref[color, core, way, :, dp].astype(F32)
                return mine + core_got[color, way, :, dp].astype(F32)

            one_send[color, way, 0] = both(first).astype(BF16)
            one_send[color, way, 1] = both(third).astype(BF16)
            send(
                one_send.at[color, way],
                one_got.at[color, way],
                one_ssem.at[0],
                one_rsem.at[color],
                {"dp": first},
            )
            two_keep[color, way, 0] = both(me)
            two_keep[color, way, 1] = both(second)

    def stage_two(color):
        came(one_got.at[color], one_rsem.at[color])
        for way in range(2):
            two_send[color, way] = (
                two_keep[color, way, 1] + one_got[color, way, 1].astype(F32)
            ).astype(BF16)
            send(
                two_send.at[color, way],
                two_got.at[color, way],
                two_ssem.at[0],
                two_rsem.at[color],
                {"dp": ways(way)[1]},
            )

    def relayed(color):
        return color < RELAYED

    def stage_three(color):
        came(two_got.at[color], two_rsem.at[color])
        for way in range(2):
            summed = (
                two_keep[color, way, 0]
                + one_got[color, way, 0].astype(F32)
                + two_got[color, way].astype(F32)
            )
            two_keep[color, way, 0] = summed
            up_send[color, :, way] = summed.astype(BF16)

        @pl.when(outer)
        def _():
            if relayed(color):
                target = rs_got.at[color, pl.ds(0, 2)]
                send(up_send.at[color], target, up_ssem.at[0], up_rsem.at[color], hub)
            else:
                for slot, at, device in ((away, 2, far_hub), (side, 0, hub)):
                    send(
                        up_send.at[color, slot],
                        rs_got.at[color, at],
                        up_ssem.at[0],
                        up_rsem.at[color],
                        device,
                    )

        if not relayed(color):

            @pl.when(inner)
            def _():
                send(
                    up_send.at[color, away],
                    rs_got.at[color, 1],
                    up_ssem.at[0],
                    up_rsem.at[color],
                    mate,
                )

    def stage_b(color):
        @pl.when(inner)
        def _():
            came(rs_got.at[color, pl.ds(0, 2)], up_rsem.at[color])
            for way in range(2):
                up_send[color, away, way] = (
                    two_keep[color, way, 0, away] + rs_got[color, away, way].astype(F32)
                ).astype(BF16)
            send(
                up_send.at[color, away],
                rs_got.at[color, 2],
                up_ssem.at[0],
                mid_rsem.at[color],
                mate,
            )

    def stage_c(color):
        @pl.when(inner)
        def _():
            if relayed(color):
                came(rs_got.at[color, 2], mid_rsem.at[color])
                terms = (side, 2)
            else:
                came(rs_got.at[color, pl.ds(0, 3)], up_rsem.at[color])
                terms = (0, 1, 2)
            for way in range(2):
                summed = two_keep[color, way, 0, side]
                for term in terms:
                    summed = summed + rs_got[color, term, way].astype(F32)
                final_ref[color, core, side, way] = summed.astype(BF16)
            mine = final_ref.at[color, core, side]
            if not relayed(color):
                send(mine, mine, rim_ssem.at[0], ag_rsem.at[color], far_rim)
            send(mine, mine, mate_ssem.at[0], ag_rsem.at[color], mate)
            send(mine, mine, rim_ssem.at[0], ag_rsem.at[color], rim)
            send(mine, mine, fwd_ssem.at[0], fwd_rsem.at[color], partner)

    def stage_d(color):
        @pl.when(inner)
        def _():
            there = final_ref.at[color, core, away]
            came(there, ag_rsem.at[color])
            if relayed(color):
                send(there, there, rim_ssem.at[0], ag_rsem.at[color], rim)
            send(there, there, fwd_ssem.at[0], fwd_rsem.at[color], partner)

    def stage_e(color):
        @pl.when(outer)
        def _():
            there = final_ref.at[color, core]
            came(there, ag_rsem.at[color])
            send(there, there, fwd_ssem.at[0], fwd_rsem.at[color], partner)

    def stage_f(color):
        came(final_ref.at[color, other], fwd_rsem.at[color])
        if color == 0:
            for edge in range(2):
                for piece in range(4):
                    rows_at = slice(edge * depth, (edge + 1) * depth)
                    sum_ref[rows_at, piece * span : (piece + 1) * span] = (
                        final_ref[0, edge, piece // 2, piece % 2].astype(F32) * factor
                    )
        else:
            in_ref[:, (color - 1) * span : color * span] = (
                final_ref[color].astype(F32) * factor
            ).reshape(width, span)

    back_duo(0)
    stage_zero(0)
    stage_one(0)
    back_duo(1)
    stage_zero(1)
    stage_one(1)
    back_duo(2)
    stage_zero(2)
    back_duo(3)
    stage_zero(3)
    stage_one(2)
    stage_two(0)
    stage_one(3)
    grad_xn = nt(gproj[...], win_ref[...])
    stage_two(1)
    stage_one(4)
    stage_three(0)
    grad_tokens = (grad + norm_back(grad_xn, normed, inverse)).astype(BF16)
    out_ref[...] = tn(fetch, grad_tokens).astype(BF16).reshape(packed)
    stage_two(2)
    stage_three(1)
    stage_two(3)
    stage_b(0)
    stage_three(2)
    stage_two(4)
    stage_b(1)
    stage_three(3)
    stage_c(0)
    stage_three(4)
    rows_out(3, out_ref, back_ref)
    stage_b(2)
    stage_c(1)
    stage_d(0)
    stage_c(2)
    stage_c(3)
    stage_d(1)
    stage_e(0)
    stage_c(4)
    stage_d(2)
    stage_d(3)
    stage_e(1)
    stage_e(2)
    stage_d(4)
    came(others(back_ref), row_rsem.at[3])
    grad_ref[...] = tn(pick_ref[...], back_ref[...].reshape(total, width)).astype(BF16)
    stage_f(0)
    stage_e(3)
    stage_f(1)
    stage_f(2)
    stage_e(4)
    stage_f(3)
    stage_f(4)
    sent(others(at_send), row_ssem.at[0])
    sent(others(ct_send), row_ssem.at[2])
    sent(others(out_ref), row_ssem.at[3])
    sent(core_got, core_ssem.at[0])
    sent(one_send, one_ssem.at[0])
    sent(two_send, two_ssem.at[0])
    half_of = final_ref.at[pl.ds(0, colors), 0, 0]
    whole_of = final_ref.at[pl.ds(0, colors), 0]

    @pl.when(inner)
    def _():
        sent(half_of, up_ssem.at[0])
        sent(half_of, mate_ssem.at[0])
        sent(whole_of, rim_ssem.at[0])

    @pl.when(outer)
    def _():
        sent(whole_of, up_ssem.at[0])

    sent(whole_of, fwd_ssem.at[0])


def finish_kernel(*refs):
    count = len(refs) // 2
    sources, outs, sems = refs[:count], refs[count : 2 * count], refs[2 * count]
    copies = [
        pltpu.make_async_copy(sources[at], outs[at], sems.at[at]) for at in range(count)
    ]
    for copy in copies:
        copy.start()
    for copy in copies:
        copy.wait()


def gather_kernel(pick_ref, back_ref, ev_ref):
    group, slots, width = back_ref.shape
    ev_ref[...] = tn(pick_ref[...], back_ref[...].reshape(group * slots, width)).astype(BF16)


VMEM = pl.BlockSpec(memory_space=pltpu.VMEM)
SMEM = pl.BlockSpec(memory_space=pltpu.SMEM)


def shape_of(shape, dtype=BF16):
    return jax.ShapeDtypeStruct(shape, dtype)


def swap(send, ident):
    group = send.shape[0]
    return pl.pallas_call(
        swap_kernel,
        out_shape=shape_of(send.shape),
        in_specs=[VMEM],
        out_specs=VMEM,
        scratch_shapes=[
            pltpu.SemaphoreType.DMA((group,)),
            pltpu.SemaphoreType.DMA((group,)),
            pltpu.SemaphoreType.DMA,
        ],
        compiler_params=pltpu.CompilerParams(collective_id=ident, has_side_effects=True),
        name="swap",
    )(send)


def body(events, cotangent, weight_in, weight_out, plan_dest, plan_pos, seq_lengths):
    group = lax.axis_size("dp")
    replicas = lax.axis_size("replica")
    rows, width = events.shape
    inner = weight_in.shape[1]
    slots = 3 * rows // (2 * group)
    total = group * slots
    chain = replicas // 2
    pair = 2 * width // HEADS
    depth = width // (2 * chain)
    stacked = (
        group == 4
        and chain == 4
        and inner == group * width
        and pair * chain == width
        and pair % LANES == 0
        and depth % 16 == 0
        and slots <= LANES
        and total % LANES == 0
    )
    factor = 1.0 / (rows * group * replicas) ** 0.5
    outgoing_shape = shape_of((group, slots, width))
    wide = [
        pltpu.VMEM((rows, inner), BF16),
        pltpu.VMEM((rows, inner), F32),
    ]
    square = [
        pltpu.VMEM((HEADS, rows, rows), BF16),
        pltpu.VMEM((HEADS, rows, rows), F32),
    ]
    dest, place = plan_dest.reshape(1, rows), plan_pos.reshape(1, rows)
    if stacked:
        packed = pltpu.VMEM((group, slots, width), BF16)
        spots = pltpu.VMEM((group, 8, LANES), F32)
        duos = HEADS // 2
        colors = duos + 1
        piece = (depth, pair)
        sized = lambda *lead, dtype=BF16: pltpu.VMEM(lead + piece, dtype)
        dma = pltpu.SemaphoreType.DMA
        results = pl.pallas_call(
            functools.partial(whole_kernel, slots, factor),
            out_shape=(
                pltpu.VMEM((rows, width), BF16),
                pltpu.VMEM((width, width), F32),
                pltpu.VMEM((width // group, width), F32),
            ),
            in_specs=[pl.BlockSpec(memory_space=pl.ANY)] * 7,
            out_specs=(VMEM,) * 3,
            scratch_shapes=[
                sized(colors, 2, 2, 2),
                pltpu.SMEM(seq_lengths.shape, jnp.int32),
                pltpu.VMEM((1, rows), jnp.int32),
                pltpu.VMEM((1, rows), jnp.int32),
                pltpu.VMEM((rows, width), BF16),
                pltpu.VMEM((rows, width), BF16),
                pltpu.VMEM(weight_in.shape, BF16),
                pltpu.VMEM(weight_out.shape, BF16),
                pltpu.VMEM((total, rows), BF16),
                packed,
            ]
            + [packed, packed, spots] * 2
            + wide
            + [pltpu.VMEM((rows, inner), BF16)]
            + square
            + [
                pltpu.VMEM((rows, width), BF16),
                packed,
                sized(colors, 2, 2, 2, group),
                sized(colors, 2, 2, group),
                sized(colors, 2, 2, 2),
                sized(colors, 2, 2, 2),
                sized(colors, 2, 2, 2, dtype=F32),
                sized(colors, 2, 2),
                sized(colors, 2, 2),
                sized(colors, 2, 2),
                sized(colors, 3, 2),
                dma((7,)),
                dma((4,)),
                dma((4,)),
            ]
            + [dma((1,)), dma((colors,))] * 3
            + [dma((1,)), dma((colors,)), dma((RELAYED,)), dma((1,)), dma((1,)), dma((colors,))]
            + [dma((1,)), dma((colors,))],
            compiler_params=pltpu.CompilerParams(collective_id=0, has_side_effects=True),
            name="whole",
        )(seq_lengths, dest, place, events, cotangent, weight_in, weight_out)
        return pl.pallas_call(
            finish_kernel,
            out_shape=tuple(shape_of(value.shape, value.dtype) for value in results),
            in_specs=[VMEM] * 3,
            out_specs=(pl.BlockSpec(memory_space=pltpu.HBM),) * 3,
            scratch_shapes=[pltpu.SemaphoreType.DMA((3,))],
            name="finish",
        )(*[pltpu.with_memory_space_constraint(value, pltpu.VMEM) for value in results])
    send, pick = pl.pallas_call(
        functools.partial(prep_kernel, slots),
        out_shape=(shape_of((group, slots, 2 * width + LANES)), shape_of((total, rows))),
        in_specs=[VMEM] * 4,
        out_specs=(VMEM, VMEM),
        name="prep",
    )(dest, place, events, cotangent)
    recv = swap(send, 0)
    outgoing, normed_in, grad_proj, gated, grad_rows = pl.pallas_call(
        layer_kernel,
        out_shape=(
            outgoing_shape,
            shape_of((rows, width)),
            shape_of((rows, inner)),
            shape_of((rows, width)),
            shape_of((rows, width)),
        ),
        in_specs=[SMEM] + [VMEM] * 3,
        out_specs=(VMEM,) * 5,
        scratch_shapes=wide + square,
        name="layer",
    )(seq_lengths, recv, weight_in, weight_out)
    back = swap(outgoing, 1)
    grad_events = pl.pallas_call(
        gather_kernel,
        out_shape=shape_of((rows, width)),
        in_specs=[VMEM] * 2,
        out_specs=VMEM,
        name="finish",
    )(pick, back)
    rows_all = lax.all_gather(normed_in, "dp", axis=0, tiled=True)
    cot_all = lax.all_gather(grad_rows, "dp", axis=0, tiled=True)
    proj_cols = lax.all_to_all(grad_proj, "dp", split_axis=1, concat_axis=0, tiled=True)
    gated_cols = lax.all_to_all(gated, "dp", split_axis=1, concat_axis=0, tiled=True)
    shard_in = jnp.einsum("rd,rf->df", rows_all, proj_cols, preferred_element_type=F32)
    shard_out = jnp.einsum("re,rd->ed", gated_cols, cot_all, preferred_element_type=F32)
    total_in, total_out = lax.psum((shard_in, shard_out), "replica")
    return grad_events, total_in * factor, total_out * factor


def solution(mesh):
    return jax.shard_map(
        body,
        mesh=mesh,
        in_specs=(
            P(("dp", "replica"), None),
            P(("dp", "replica"), None),
            P(),
            P(),
            P(("dp", "replica")),
            P(("dp", "replica")),
            P(("dp", "replica"), None),
        ),
        out_specs=(P(("dp", "replica"), None), P(None, "dp"), P("dp", None)),
        check_vma=False,
    )
```

```python
import functools

import jax
import jax.numpy as jnp
from jax import lax
from jax.experimental import pallas as pl
from jax.experimental.pallas import tpu as pltpu
from jax.sharding import PartitionSpec as P

HEADS = 8
MAXLEN = 128
EPS = 1e-05
RELAYED = 0
ECHOED = 2
LANES = 128
MESH = pl.DeviceIdType.MESH
F32 = jnp.float32
BF16 = jnp.bfloat16


def contract(left, right, dims):
    return lax.dot_general(left, right, ((dims[:1], dims[1:]), ((), ())), preferred_element_type=F32)


def nn(left, right):
    return contract(left, right, (1, 0))


def nt(left, right):
    return contract(left, right, (1, 1))


def tn(left, right):
    return contract(left, right, (0, 0))


def normalize(values):
    center = values - jnp.mean(values, axis=-1, keepdims=True)
    inverse = lax.rsqrt(jnp.mean(center * center, axis=-1, keepdims=True) + EPS)
    return center * inverse, inverse


def norm_back(grad, normed, inverse):
    return inverse * (
        grad
        - jnp.mean(grad, axis=-1, keepdims=True)
        - normed * jnp.mean(grad * normed, axis=-1, keepdims=True)
    )


def prep_kernel(slot_count, dest_ref, pos_ref, ev_ref, ct_ref, send_ref, pick_ref):
    rows, width = ev_ref.shape
    group = send_ref.shape[0]
    dest = dest_ref[...]
    hot = lax.broadcasted_iota(jnp.int32, (8, rows), 0) == dest
    upper = lax.broadcasted_iota(jnp.int32, (rows, rows), 0) < lax.broadcasted_iota(
        jnp.int32, (rows, rows), 1
    )
    earlier = nn(
        jnp.where(hot, 1.0, 0.0).astype(BF16), jnp.where(upper, 1.0, 0.0).astype(BF16)
    )
    slot = jnp.sum(jnp.where(hot, earlier, 0.0), axis=0, keepdims=True).astype(jnp.int32)
    flat = dest * slot_count + slot
    total = group * slot_count
    chosen = lax.broadcasted_iota(jnp.int32, (total, rows), 0) == flat
    pick = jnp.where(chosen, 1.0, 0.0).astype(BF16)
    pick_ref[...] = pick
    place = jnp.sum(
        jnp.where(chosen, pos_ref[...].astype(F32) + 1.0, 0.0), axis=1, keepdims=True
    )
    shape = (group, slot_count)
    send_ref[:, :, :width] = nn(pick, ev_ref[...]).astype(BF16).reshape(shape + (width,))
    send_ref[:, :, width : 2 * width] = nn(pick, ct_ref[...]).astype(BF16).reshape(shape + (width,))
    send_ref[:, :, 2 * width :] = (
        jnp.broadcast_to(place, (total, LANES)).astype(BF16).reshape(shape + (LANES,))
    )


def swap_kernel(send_ref, recv_ref, send_sem, recv_sem, own_sem):
    group = lax.axis_size("dp")
    me = lax.axis_index("dp")
    barrier = pltpu.get_barrier_semaphore()
    for step in range(1, group):
        pl.semaphore_signal(
            barrier, inc=1, device_id={"dp": lax.rem(me + step, group)}, device_id_type=MESH
        )
    own = pltpu.make_async_copy(send_ref.at[me], recv_ref.at[me], own_sem)
    own.start()
    pl.semaphore_wait(barrier, group - 1)
    copies = []
    for step in range(1, group):
        peer = lax.rem(me + step, group)
        copy = pltpu.make_async_remote_copy(
            src_ref=send_ref.at[peer],
            dst_ref=recv_ref.at[me],
            send_sem=send_sem.at[step],
            recv_sem=recv_sem.at[step],
            device_id={"dp": peer},
            device_id_type=MESH,
        )
        copy.start()
        copies.append(copy)
    own.wait()
    for copy in copies:
        copy.wait()


def layer_kernel(
    len_ref,
    recv_ref,
    win_ref,
    wout_ref,
    out_ref,
    *rest,
):
    xn_out, gproj, gated_out, g_out, act, slope_p, attn, slope_s = rest
    group, slots, packed = recv_ref.shape
    width = wout_ref.shape[0]
    rows = act.shape[0]
    head = width // HEADS
    scale = 1.0 / head**0.5
    total = group * slots
    got = recv_ref[...].reshape(total, packed)
    place = got[:, 2 * width : 2 * width + 1].astype(F32) - 1.0
    spots = lax.broadcasted_iota(jnp.int32, (total, rows), 1).astype(F32)
    pick = jnp.where(place == spots, 1.0, 0.0).astype(BF16)
    tokens = tn(pick, got[:, :width])
    grad = tn(pick, got[:, width : 2 * width])
    grad16 = grad.astype(BF16)
    normed, inverse = normalize(tokens)
    xn = normed.astype(BF16)
    for block in range(4):
        cols = slice(block * width, (block + 1) * width)
        proj = nn(xn, win_ref[:, cols])
        sig = jax.nn.sigmoid(proj)
        act[:, cols] = (proj * sig).astype(BF16)
        slope_p[:, cols] = sig * (1.0 + proj * (1.0 - sig))
    row_at = lax.broadcasted_iota(jnp.int32, (rows, 1), 0)
    col_at = lax.broadcasted_iota(jnp.int32, (1, rows), 1)
    bound = jnp.int32(0)
    row_seg = jnp.zeros((rows, 1), jnp.int32)
    col_seg = jnp.zeros((1, rows), jnp.int32)
    for seq in range(len_ref.shape[1]):
        bound = bound + len_ref[0, seq]
        row_seg = row_seg + jnp.where(row_at >= bound, 1, 0)
        col_seg = col_seg + jnp.where(col_at >= bound, 1, 0)
    mask = (row_seg == col_seg) & (col_at <= row_at)
    pair = 2 * head
    low = lax.broadcasted_iota(jnp.int32, (rows, pair), 1) < head

    def half(values, which):
        return jnp.where(low if which == 0 else ~low, values, jnp.zeros_like(values))

    def cut(block, duo):
        start = block * width + duo * pair
        return act[:, start : start + pair]

    outs = []
    for duo in range(HEADS // 2):
        value, query, key = cut(1, duo), cut(2, duo), cut(3, duo)
        parts = []
        for which in range(2):
            at = 2 * duo + which
            scores = nt(half(query, which), key) * scale
            sig = jax.nn.sigmoid(scores)
            weight = jnp.where(mask, scores * sig * (1.0 / MAXLEN), 0.0).astype(BF16)
            attn[at] = weight
            slope_s[at] = jnp.where(
                mask, sig * (1.0 + scores * (1.0 - sig)) * (scale / MAXLEN), 0.0
            )
            parts.append(nn(weight, value))
        outs.append(jnp.where(low, parts[0], parts[1]))
    onorm, oinv = normalize(jnp.concatenate(outs, axis=1))
    gate = act[:, :width].astype(F32)
    gated = (gate * onorm).astype(BF16)
    grad_z = nt(grad16, wout_ref[...])
    gproj[:, :width] = (grad_z * onorm * slope_p[:, :width]).astype(BF16)
    grad_out = norm_back(grad_z * gate, onorm, oinv).astype(BF16)
    for duo in range(HEADS // 2):
        value, query, key = cut(1, duo), cut(2, duo), cut(3, duo)
        gout = grad_out[:, duo * pair : (duo + 1) * pair]
        parts = ([], [], [])
        for which in range(2):
            at = 2 * duo + which
            gscore = (nt(half(gout, which), value) * slope_s[at]).astype(BF16)
            parts[0].append(tn(attn[at], gout))
            parts[1].append(nn(gscore, key))
            parts[2].append(tn(gscore, query))
        for block in range(3):
            start = (block + 1) * width + duo * pair
            cols = slice(start, start + pair)
            both = jnp.where(low, parts[block][0], parts[block][1])
            gproj[:, cols] = (both * slope_p[:, cols]).astype(BF16)
    grad_xn = nt(gproj[...], win_ref[...])
    grad_tokens = (grad + norm_back(grad_xn, normed, inverse)).astype(BF16)
    out_ref[...] = nn(pick, grad_tokens).astype(BF16).reshape(group, slots, width)
    xn_out[...] = xn
    gated_out[...] = gated
    g_out[...] = grad16


def whole_kernel(
    slots,
    factor,
    len_any,
    dest_any,
    pos_any,
    ev_any,
    ct_any,
    win_any,
    wout_any,
    grad_ref,
    in_ref,
    sum_ref,
    final_ref,
    len_ref,
    dest_ref,
    pos_ref,
    ev_ref,
    ct_ref,
    win_ref,
    wout_ref,
    pick_ref,
    back_ref,
    ev_send,
    ct_send,
    at_send,
    ev_got,
    ct_got,
    at_got,
    act,
    slope_p,
    gproj,
    attn,
    slope_s,
    xn_ref,
    out_ref,
    part_ref,
    core_got,
    one_send,
    one_got,
    two_keep,
    two_send,
    two_got,
    up_send,
    rs_got,
    load_sems,
    row_ssem,
    row_rsem,
    core_ssem,
    core_rsem,
    one_ssem,
    one_rsem,
    two_ssem,
    two_rsem,
    up_ssem,
    up_rsem,
    mid_rsem,
    mate_ssem,
    rim_ssem,
    ag_rsem,
    fwd_ssem,
    fwd_rsem,
):
    rows, width = ev_ref.shape
    group = ev_send.shape[0]
    colors, depth, span = rs_got.shape[0], rs_got.shape[3], rs_got.shape[4]
    total = group * slots
    head = width // HEADS
    scale = 1.0 / head**0.5
    me = lax.axis_index("dp")
    rep = lax.axis_index("replica")
    core = lax.rem(rep, 2)
    other = 1 - core
    spot = rep // 2
    partner = {"replica": spot * 2 + other}
    low_bit, high_bit = lax.rem(me, 2), me // 2
    near = high_bit * 2 + 1 - low_bit
    far = (1 - high_bit) * 2 + low_bit
    third = 3 - me

    def dp_peer(step):
        return lax.rem(me + step, group)

    side = spot // 2
    away = 1 - side
    inner = (spot == 1) | (spot == 2)
    outer = ~inner
    hub = {"replica": (1 + side) * 2 + core}
    mate = {"replica": (3 - spot) * 2 + core}
    rim = {"replica": 3 * side * 2 + core}
    far_hub = {"replica": (2 - side) * 2 + core}
    far_rim = {"replica": 3 * away * 2 + core}

    loads = [
        pltpu.make_async_copy(source, target, load_sems.at[at])
        for at, (source, target) in enumerate(
            (
                (ev_any, ev_ref),
                (ct_any, ct_ref),
                (win_any, win_ref),
                (wout_any, wout_ref),
                (dest_any, dest_ref),
                (pos_any, pos_ref),
                (len_any, len_ref),
            )
        )
    ]
    for at in (4, 0, 5, 1, 6):
        loads[at].start()
    barrier = pltpu.get_barrier_semaphore()
    for step in range(1, group):
        pl.semaphore_signal(barrier, inc=1, device_id={"dp": dp_peer(step)}, device_id_type=MESH)
    pl.semaphore_signal(barrier, inc=1, device_id=partner, device_id_type=MESH)

    @pl.when(outer)
    def _():
        for device in (hub, far_hub):
            pl.semaphore_signal(barrier, inc=1, device_id=device, device_id_type=MESH)

    @pl.when(inner)
    def _():
        for device in (mate, rim, far_rim):
            pl.semaphore_signal(barrier, inc=1, device_id=device, device_id_type=MESH)

    def describe(src, dst, ssem, rsem, device):
        return pltpu.make_async_remote_copy(
            src_ref=src,
            dst_ref=dst,
            send_sem=ssem,
            recv_sem=rsem,
            device_id=device,
            device_id_type=MESH,
        )

    def send(src, dst, ssem, rsem, device):
        describe(src, dst, ssem, rsem, device).start()

    def sent(like, ssem):
        describe(like, like, ssem, ssem, partner).wait_send()

    def came(like, rsem):
        describe(like, like, rsem, rsem, partner).wait_recv()

    loads[4].wait()
    dest = dest_ref[...]
    hot = lax.broadcasted_iota(jnp.int32, (8, rows), 0) == dest
    upper = lax.broadcasted_iota(jnp.int32, (rows, rows), 0) < lax.broadcasted_iota(
        jnp.int32, (rows, rows), 1
    )
    earlier = nn(
        jnp.where(hot, 1.0, 0.0).astype(BF16), jnp.where(upper, 1.0, 0.0).astype(BF16)
    )
    slot = jnp.sum(jnp.where(hot, earlier, 0.0), axis=0, keepdims=True).astype(jnp.int32)
    slot_iota = lax.broadcasted_iota(jnp.int32, (total, rows), 0)
    pick = jnp.where(slot_iota == dest * slots + slot, 1.0, 0.0).astype(BF16)
    pick_ref[...] = pick
    packed = (group, slots, width)
    loads[0].wait()
    ev_send[...] = nn(pick, ev_ref[...]).astype(BF16).reshape(packed)
    pl.semaphore_wait(barrier, group + 2 + jnp.where(inner, 1, 0))

    def rows_out(kind, src, dst):
        for step in (3, 1, 2):
            peer = step ^ me
            send(src.at[peer], dst.at[me], row_ssem.at[kind], row_rsem.at[kind], {"dp": peer})
        dst[me] = src[me]

    def others(buffer):
        return buffer.at[pl.ds(0, group - 1)]

    rows_out(1, ev_send, ev_got)
    loads[2].start()
    loads[3].start()
    loads[5].wait()
    spots = jnp.broadcast_to(pos_ref[...] + 1, (8, rows)).astype(F32).astype(BF16)
    lane_iota = lax.broadcasted_iota(jnp.int32, (LANES, rows), 0)
    for dp in range(group):
        there = jnp.where((lane_iota == slot) & (dest == dp), 1.0, 0.0).astype(BF16)
        at_send[dp] = nt(spots, there)
    rows_out(0, at_send, at_got)
    loads[1].wait()
    ct_send[...] = nn(pick, ct_ref[...]).astype(BF16).reshape(packed)
    sent(others(ev_send), row_ssem.at[1])
    rows_out(2, ct_send, ct_got)

    came(others(at_got), row_rsem.at[0])
    came(others(ev_got), row_rsem.at[1])
    place = jnp.zeros((8, total), F32)
    blank = jnp.zeros((8, total - LANES), F32)
    for dp in range(group):
        there = jnp.concatenate([at_got[dp], blank], axis=1)
        place = place + pltpu.roll(there, dp * slots, 1)
    row_iota = lax.broadcasted_iota(jnp.int32, (rows, total), 0).astype(F32) + 1.0
    fetch = jnp.where(row_iota == place[:1], 1.0, 0.0).astype(BF16)
    tokens = nn(fetch, ev_got[...].reshape(total, width))
    normed, inverse = normalize(tokens)
    xn = normed.astype(BF16)
    xn_ref[...] = xn
    loads[2].wait()
    loads[3].wait()
    for block in range(4):
        cols = slice(block * width, (block + 1) * width)
        proj = nn(xn, win_ref[:, cols])
        sig = jax.nn.sigmoid(proj)
        act[:, cols] = (proj * sig).astype(BF16)
        slope_p[:, cols] = sig * (1.0 + proj * (1.0 - sig))
    row_at = lax.broadcasted_iota(jnp.int32, (rows, 1), 0)
    col_at = lax.broadcasted_iota(jnp.int32, (1, rows), 1)
    loads[6].wait()
    bound = jnp.int32(0)
    row_seg = jnp.zeros((rows, 1), jnp.int32)
    col_seg = jnp.zeros((1, rows), jnp.int32)
    for seq in range(len_ref.shape[1]):
        bound = bound + len_ref[0, seq]
        row_seg = row_seg + jnp.where(row_at >= bound, 1, 0)
        col_seg = col_seg + jnp.where(col_at >= bound, 1, 0)
    mask = (row_seg == col_seg) & (col_at <= row_at)
    pair = 2 * head
    low = lax.broadcasted_iota(jnp.int32, (rows, pair), 1) < head

    def half(values, which):
        return jnp.where(low if which == 0 else ~low, values, jnp.zeros_like(values))

    def cut(block, duo):
        start = block * width + duo * pair
        return act[:, start : start + pair]

    outs = []
    for duo in range(HEADS // 2):
        value, query, key = cut(1, duo), cut(2, duo), cut(3, duo)
        parts = []
        for which in range(2):
            at = 2 * duo + which
            scores = nt(half(query, which), key) * scale
            sig = jax.nn.sigmoid(scores)
            weight = jnp.where(mask, scores * sig * (1.0 / MAXLEN), 0.0).astype(BF16)
            attn[at] = weight
            slope_s[at] = jnp.where(
                mask, sig * (1.0 + scores * (1.0 - sig)) * (scale / MAXLEN), 0.0
            )
            parts.append(nn(weight, value))
        outs.append(jnp.where(low, parts[0], parts[1]))
    onorm, oinv = normalize(jnp.concatenate(outs, axis=1))
    gate = act[:, :width].astype(F32)
    gated = (gate * onorm).astype(BF16)

    came(others(ct_got), row_rsem.at[2])
    grad = nn(fetch, ct_got[...].reshape(total, width))
    grad16 = grad.astype(BF16)

    def store_part(color, whole, row_of, column_of):
        for edge in range(2):
            for piece in range(4):
                for dp in range(group):
                    row, column = row_of(edge, piece, dp), column_of(edge, piece, dp)
                    part_ref[color, edge, piece % 2, piece // 2, dp] = whole[
                        row : row + depth, column : column + span
                    ]
        send(
            part_ref.at[color, other],
            core_got.at[color],
            core_ssem.at[0],
            core_rsem.at[color],
            partner,
        )

    store_part(
        0,
        tn(gated, grad16).astype(BF16),
        lambda edge, piece, dp: (2 * dp + edge) * depth,
        lambda edge, piece, dp: piece * span,
    )
    grad_z = nt(grad16, wout_ref[...])
    gproj[:, :width] = (grad_z * onorm * slope_p[:, :width]).astype(BF16)
    grad_out = norm_back(grad_z * gate, onorm, oinv).astype(BF16)

    def back_duo(duo):
        value, query, key = cut(1, duo), cut(2, duo), cut(3, duo)
        gout = grad_out[:, duo * pair : (duo + 1) * pair]
        parts = ([], [], [])
        for which in range(2):
            at = 2 * duo + which
            gscore = (nt(half(gout, which), value) * slope_s[at]).astype(BF16)
            parts[0].append(tn(attn[at], gout))
            parts[1].append(nn(gscore, key))
            parts[2].append(tn(gscore, query))
        for block in range(3):
            start = (block + 1) * width + duo * pair
            cols = slice(start, start + pair)
            both = jnp.where(low, parts[block][0], parts[block][1])
            gproj[:, cols] = (both * slope_p[:, cols]).astype(BF16)

    def stage_zero(duo):
        columns = jnp.concatenate(
            [
                gproj[:, dp * width + duo * span : dp * width + (duo + 1) * span]
                for dp in range(group)
            ],
            axis=1,
        )
        store_part(
            duo + 1,
            tn(xn_ref[...], columns).astype(BF16),
            lambda edge, piece, dp: (4 * edge + piece) * depth,
            lambda edge, piece, dp: dp * span,
        )

    def ways(way):
        return (near, far) if way == 0 else (far, near)

    def stage_one(color):
        came(core_got.at[color], core_rsem.at[color])
        for way in range(2):
            first, second = ways(way)

            def both(dp):
                mine = part_ref[color, core, way, :, dp].astype(F32)
                return mine + core_got[color, way, :, dp].astype(F32)

            one_send[color, way, 0] = both(first).astype(BF16)
            one_send[color, way, 1] = both(third).astype(BF16)
            send(
                one_send.at[color, way],
                one_got.at[color, way],
                one_ssem.at[0],
                one_rsem.at[color],
                {"dp": first},
            )
            two_keep[color, way, 0] = both(me)
            two_keep[color, way, 1] = both(second)

    def stage_two(color):
        came(one_got.at[color], one_rsem.at[color])
        for way in range(2):
            two_send[color, way] = (
                two_keep[color, way, 1] + one_got[color, way, 1].astype(F32)
            ).astype(BF16)
            send(
                two_send.at[color, way],
                two_got.at[color, way],
                two_ssem.at[0],
                two_rsem.at[color],
                {"dp": ways(way)[1]},
            )

    def relayed(color):
        return color < RELAYED

    def echoed(color):
        return color < ECHOED

    def stage_three(color):
        came(two_got.at[color], two_rsem.at[color])
        for way in range(2):
            summed = (
                two_keep[color, way, 0]
                + one_got[color, way, 0].astype(F32)
                + two_got[color, way].astype(F32)
            )
            two_keep[color, way, 0] = summed
            up_send[color, :, way] = summed.astype(BF16)

        @pl.when(outer)
        def _():
            if relayed(color):
                target = rs_got.at[color, pl.ds(0, 2)]
                send(up_send.at[color], target, up_ssem.at[0], up_rsem.at[color], hub)
            else:
                for slot, at, device in ((away, 2, far_hub), (side, 0, hub)):
                    send(
                        up_send.at[color, slot],
                        rs_got.at[color, at],
                        up_ssem.at[0],
                        up_rsem.at[color],
                        device,
                    )

        if not relayed(color):

            @pl.when(inner)
            def _():
                send(
                    up_send.at[color, away],
                    rs_got.at[color, 1],
                    up_ssem.at[0],
                    up_rsem.at[color],
                    mate,
                )

    def stage_b(color):
        if not relayed(color):
            return

        @pl.when(inner)
        def _():
            came(rs_got.at[color, pl.ds(0, 2)], up_rsem.at[color])
            for way in range(2):
                up_send[color, away, way] = (
                    two_keep[color, way, 0, away] + rs_got[color, away, way].astype(F32)
                ).astype(BF16)
            send(
                up_send.at[color, away],
                rs_got.at[color, 2],
                up_ssem.at[0],
                mid_rsem.at[color],
                mate,
            )

    def stage_c(color):
        @pl.when(inner)
        def _():
            if relayed(color):
                came(rs_got.at[color, 2], mid_rsem.at[color])
                terms = (side, 2)
            else:
                came(rs_got.at[color, pl.ds(0, 3)], up_rsem.at[color])
                terms = (0, 1, 2)
            for way in range(2):
                summed = two_keep[color, way, 0, side]
                for term in terms:
                    summed = summed + rs_got[color, term, way].astype(F32)
                final_ref[color, core, side, way] = summed.astype(BF16)
            mine = final_ref.at[color, core, side]
            if not echoed(color):
                send(mine, mine, rim_ssem.at[0], ag_rsem.at[color], far_rim)
            send(mine, mine, mate_ssem.at[0], ag_rsem.at[color], mate)
            send(mine, mine, rim_ssem.at[0], ag_rsem.at[color], rim)
            send(mine, mine, fwd_ssem.at[0], fwd_rsem.at[color], partner)

    def stage_d(color):
        @pl.when(inner)
        def _():
            there = final_ref.at[color, core, away]
            came(there, ag_rsem.at[color])
            if echoed(color):
                send(there, there, rim_ssem.at[0], ag_rsem.at[color], rim)
            send(there, there, fwd_ssem.at[0], fwd_rsem.at[color], partner)

    def stage_e(color):
        @pl.when(outer)
        def _():
            there = final_ref.at[color, core]
            came(there, ag_rsem.at[color])
            send(there, there, fwd_ssem.at[0], fwd_rsem.at[color], partner)

    def stage_f(color):
        came(final_ref.at[color, other], fwd_rsem.at[color])
        if color == 0:
            for edge in range(2):
                for piece in range(4):
                    rows_at = slice(edge * depth, (edge + 1) * depth)
                    sum_ref[rows_at, piece * span : (piece + 1) * span] = (
                        final_ref[0, edge, piece // 2, piece % 2].astype(F32) * factor
                    )
        else:
            in_ref[:, (color - 1) * span : color * span] = (
                final_ref[color].astype(F32) * factor
            ).reshape(width, span)

    back_duo(0)
    stage_one(0)
    stage_zero(0)
    back_duo(1)
    stage_zero(1)
    stage_one(1)
    back_duo(2)
    stage_zero(2)
    back_duo(3)
    stage_zero(3)
    stage_two(0)
    stage_one(2)
    grad_xn = nt(gproj[...], win_ref[...])
    stage_two(1)
    stage_one(3)
    stage_one(4)
    grad_tokens = (grad + norm_back(grad_xn, normed, inverse)).astype(BF16)
    out_ref[...] = tn(fetch, grad_tokens).astype(BF16).reshape(packed)
    stage_three(0)
    stage_two(2)
    stage_three(1)
    stage_two(3)
    stage_two(4)
    stage_three(2)
    stage_b(1)
    stage_c(0)
    stage_three(3)
    stage_three(4)
    rows_out(3, out_ref, back_ref)
    stage_c(1)
    stage_b(2)
    stage_c(2)
    stage_d(0)
    stage_e(0)
    stage_c(3)
    stage_d(1)
    stage_e(1)
    stage_c(4)
    stage_d(2)
    stage_e(2)
    stage_d(3)
    stage_e(3)
    stage_d(4)
    came(others(back_ref), row_rsem.at[3])
    grad_ref[...] = tn(pick_ref[...], back_ref[...].reshape(total, width)).astype(BF16)
    stage_e(4)
    for color in range(colors):
        stage_f(color)
    sent(others(at_send), row_ssem.at[0])
    sent(others(ct_send), row_ssem.at[2])
    sent(others(out_ref), row_ssem.at[3])
    sent(core_got, core_ssem.at[0])
    sent(one_send, one_ssem.at[0])
    sent(two_send, two_ssem.at[0])
    half_of = final_ref.at[pl.ds(0, colors), 0, 0]
    whole_of = final_ref.at[pl.ds(0, colors), 0]

    @pl.when(inner)
    def _():
        sent(half_of, up_ssem.at[0])
        sent(half_of, mate_ssem.at[0])
        sent(whole_of, rim_ssem.at[0])

    @pl.when(outer)
    def _():
        sent(whole_of, up_ssem.at[0])

    sent(whole_of, fwd_ssem.at[0])


def finish_kernel(*refs):
    count = len(refs) // 2
    sources, outs, sems = refs[:count], refs[count : 2 * count], refs[2 * count]
    copies = [
        pltpu.make_async_copy(sources[at], outs[at], sems.at[at]) for at in range(count)
    ]
    for copy in copies:
        copy.start()
    for copy in copies:
        copy.wait()


def gather_kernel(pick_ref, back_ref, ev_ref):
    group, slots, width = back_ref.shape
    ev_ref[...] = tn(pick_ref[...], back_ref[...].reshape(group * slots, width)).astype(BF16)


VMEM = pl.BlockSpec(memory_space=pltpu.VMEM)
SMEM = pl.BlockSpec(memory_space=pltpu.SMEM)


def shape_of(shape, dtype=BF16):
    return jax.ShapeDtypeStruct(shape, dtype)


def swap(send, ident):
    group = send.shape[0]
    return pl.pallas_call(
        swap_kernel,
        out_shape=shape_of(send.shape),
        in_specs=[VMEM],
        out_specs=VMEM,
        scratch_shapes=[
            pltpu.SemaphoreType.DMA((group,)),
            pltpu.SemaphoreType.DMA((group,)),
            pltpu.SemaphoreType.DMA,
        ],
        compiler_params=pltpu.CompilerParams(collective_id=ident, has_side_effects=True),
        name="swap",
    )(send)


def body(events, cotangent, weight_in, weight_out, plan_dest, plan_pos, seq_lengths):
    group = lax.axis_size("dp")
    replicas = lax.axis_size("replica")
    rows, width = events.shape
    inner = weight_in.shape[1]
    slots = 3 * rows // (2 * group)
    total = group * slots
    chain = replicas // 2
    pair = 2 * width // HEADS
    depth = width // (2 * chain)
    stacked = (
        group == 4
        and chain == 4
        and inner == group * width
        and pair * chain == width
        and pair % LANES == 0
        and depth % 16 == 0
        and slots <= LANES
        and total % LANES == 0
    )
    factor = 1.0 / (rows * group * replicas) ** 0.5
    outgoing_shape = shape_of((group, slots, width))
    wide = [
        pltpu.VMEM((rows, inner), BF16),
        pltpu.VMEM((rows, inner), F32),
    ]
    square = [
        pltpu.VMEM((HEADS, rows, rows), BF16),
        pltpu.VMEM((HEADS, rows, rows), F32),
    ]
    dest, place = plan_dest.reshape(1, rows), plan_pos.reshape(1, rows)
    if stacked:
        packed = pltpu.VMEM((group, slots, width), BF16)
        spots = pltpu.VMEM((group, 8, LANES), F32)
        duos = HEADS // 2
        colors = duos + 1
        piece = (depth, pair)
        sized = lambda *lead, dtype=BF16: pltpu.VMEM(lead + piece, dtype)
        dma = pltpu.SemaphoreType.DMA
        results = pl.pallas_call(
            functools.partial(whole_kernel, slots, factor),
            out_shape=(
                pltpu.VMEM((rows, width), BF16),
                pltpu.VMEM((width, width), F32),
                pltpu.VMEM((width // group, width), F32),
            ),
            in_specs=[pl.BlockSpec(memory_space=pl.ANY)] * 7,
            out_specs=(VMEM,) * 3,
            scratch_shapes=[
                sized(colors, 2, 2, 2),
                pltpu.SMEM(seq_lengths.shape, jnp.int32),
                pltpu.VMEM((1, rows), jnp.int32),
                pltpu.VMEM((1, rows), jnp.int32),
                pltpu.VMEM((rows, width), BF16),
                pltpu.VMEM((rows, width), BF16),
                pltpu.VMEM(weight_in.shape, BF16),
                pltpu.VMEM(weight_out.shape, BF16),
                pltpu.VMEM((total, rows), BF16),
                packed,
            ]
            + [packed, packed, spots] * 2
            + wide
            + [pltpu.VMEM((rows, inner), BF16)]
            + square
            + [
                pltpu.VMEM((rows, width), BF16),
                packed,
                sized(colors, 2, 2, 2, group),
                sized(colors, 2, 2, group),
                sized(colors, 2, 2, 2),
                sized(colors, 2, 2, 2),
                sized(colors, 2, 2, 2, dtype=F32),
                sized(colors, 2, 2),
                sized(colors, 2, 2),
                sized(colors, 2, 2),
                sized(colors, 3, 2),
                dma((7,)),
                dma((4,)),
                dma((4,)),
            ]
            + [dma((1,)), dma((colors,))] * 3
            + [dma((1,)), dma((colors,)), dma((max(RELAYED, 1),)), dma((1,)), dma((1,)), dma((colors,))]
            + [dma((1,)), dma((colors,))],
            compiler_params=pltpu.CompilerParams(collective_id=0, has_side_effects=True),
            name="whole",
        )(seq_lengths, dest, place, events, cotangent, weight_in, weight_out)
        return pl.pallas_call(
            finish_kernel,
            out_shape=tuple(shape_of(value.shape, value.dtype) for value in results),
            in_specs=[VMEM] * 3,
            out_specs=(pl.BlockSpec(memory_space=pltpu.HBM),) * 3,
            scratch_shapes=[pltpu.SemaphoreType.DMA((3,))],
            name="finish",
        )(*[pltpu.with_memory_space_constraint(value, pltpu.VMEM) for value in results])
    send, pick = pl.pallas_call(
        functools.partial(prep_kernel, slots),
        out_shape=(shape_of((group, slots, 2 * width + LANES)), shape_of((total, rows))),
        in_specs=[VMEM] * 4,
        out_specs=(VMEM, VMEM),
        name="prep",
    )(dest, place, events, cotangent)
    recv = swap(send, 0)
    outgoing, normed_in, grad_proj, gated, grad_rows = pl.pallas_call(
        layer_kernel,
        out_shape=(
            outgoing_shape,
            shape_of((rows, width)),
            shape_of((rows, inner)),
            shape_of((rows, width)),
            shape_of((rows, width)),
        ),
        in_specs=[SMEM] + [VMEM] * 3,
        out_specs=(VMEM,) * 5,
        scratch_shapes=wide + square,
        name="layer",
    )(seq_lengths, recv, weight_in, weight_out)
    back = swap(outgoing, 1)
    grad_events = pl.pallas_call(
        gather_kernel,
        out_shape=shape_of((rows, width)),
        in_specs=[VMEM] * 2,
        out_specs=VMEM,
        name="finish",
    )(pick, back)
    rows_all = lax.all_gather(normed_in, "dp", axis=0, tiled=True)
    cot_all = lax.all_gather(grad_rows, "dp", axis=0, tiled=True)
    proj_cols = lax.all_to_all(grad_proj, "dp", split_axis=1, concat_axis=0, tiled=True)
    gated_cols = lax.all_to_all(gated, "dp", split_axis=1, concat_axis=0, tiled=True)
    shard_in = jnp.einsum("rd,rf->df", rows_all, proj_cols, preferred_element_type=F32)
    shard_out = jnp.einsum("re,rd->ed", gated_cols, cot_all, preferred_element_type=F32)
    total_in, total_out = lax.psum((shard_in, shard_out), "replica")
    return grad_events, total_in * factor, total_out * factor


def solution(mesh):
    return jax.shard_map(
        body,
        mesh=mesh,
        in_specs=(
            P(("dp", "replica"), None),
            P(("dp", "replica"), None),
            P(),
            P(),
            P(("dp", "replica")),
            P(("dp", "replica")),
            P(("dp", "replica"), None),
        ),
        out_specs=(P(("dp", "replica"), None), P(None, "dp"), P("dp", None)),
        check_vma=False,
    )
```

```python
import functools

import jax
import jax.numpy as jnp
from jax import lax
from jax.experimental import pallas as pl
from jax.experimental.pallas import tpu as pltpu
from jax.sharding import PartitionSpec as P

HEADS = 8
MAXLEN = 128
EPS = 1e-05
ECHOED = 2
PAIRED = 2
LANES = 128
MESH = pl.DeviceIdType.MESH
F32 = jnp.float32
BF16 = jnp.bfloat16


def contract(left, right, dims):
    return lax.dot_general(left, right, ((dims[:1], dims[1:]), ((), ())), preferred_element_type=F32)


def nn(left, right):
    return contract(left, right, (1, 0))


def nt(left, right):
    return contract(left, right, (1, 1))


def tn(left, right):
    return contract(left, right, (0, 0))


def normalize(values):
    center = values - jnp.mean(values, axis=-1, keepdims=True)
    inverse = lax.rsqrt(jnp.mean(center * center, axis=-1, keepdims=True) + EPS)
    return center * inverse, inverse


def norm_back(grad, normed, inverse):
    return inverse * (
        grad
        - jnp.mean(grad, axis=-1, keepdims=True)
        - normed * jnp.mean(grad * normed, axis=-1, keepdims=True)
    )


def prep_kernel(slot_count, dest_ref, pos_ref, ev_ref, ct_ref, send_ref, pick_ref):
    rows, width = ev_ref.shape
    group = send_ref.shape[0]
    dest = dest_ref[...]
    hot = lax.broadcasted_iota(jnp.int32, (8, rows), 0) == dest
    upper = lax.broadcasted_iota(jnp.int32, (rows, rows), 0) < lax.broadcasted_iota(
        jnp.int32, (rows, rows), 1
    )
    earlier = nn(
        jnp.where(hot, 1.0, 0.0).astype(BF16), jnp.where(upper, 1.0, 0.0).astype(BF16)
    )
    slot = jnp.sum(jnp.where(hot, earlier, 0.0), axis=0, keepdims=True).astype(jnp.int32)
    flat = dest * slot_count + slot
    total = group * slot_count
    chosen = lax.broadcasted_iota(jnp.int32, (total, rows), 0) == flat
    pick = jnp.where(chosen, 1.0, 0.0).astype(BF16)
    pick_ref[...] = pick
    place = jnp.sum(
        jnp.where(chosen, pos_ref[...].astype(F32) + 1.0, 0.0), axis=1, keepdims=True
    )
    shape = (group, slot_count)
    send_ref[:, :, :width] = nn(pick, ev_ref[...]).astype(BF16).reshape(shape + (width,))
    send_ref[:, :, width : 2 * width] = nn(pick, ct_ref[...]).astype(BF16).reshape(shape + (width,))
    send_ref[:, :, 2 * width :] = (
        jnp.broadcast_to(place, (total, LANES)).astype(BF16).reshape(shape + (LANES,))
    )


def swap_kernel(send_ref, recv_ref, send_sem, recv_sem, own_sem):
    group = lax.axis_size("dp")
    me = lax.axis_index("dp")
    barrier = pltpu.get_barrier_semaphore()
    for step in range(1, group):
        pl.semaphore_signal(
            barrier, inc=1, device_id={"dp": lax.rem(me + step, group)}, device_id_type=MESH
        )
    own = pltpu.make_async_copy(send_ref.at[me], recv_ref.at[me], own_sem)
    own.start()
    pl.semaphore_wait(barrier, group - 1)
    copies = []
    for step in range(1, group):
        peer = lax.rem(me + step, group)
        copy = pltpu.make_async_remote_copy(
            src_ref=send_ref.at[peer],
            dst_ref=recv_ref.at[me],
            send_sem=send_sem.at[step],
            recv_sem=recv_sem.at[step],
            device_id={"dp": peer},
            device_id_type=MESH,
        )
        copy.start()
        copies.append(copy)
    own.wait()
    for copy in copies:
        copy.wait()


def layer_kernel(
    len_ref,
    recv_ref,
    win_ref,
    wout_ref,
    out_ref,
    *rest,
):
    xn_out, gproj, gated_out, g_out, act, slope_p, attn, slope_s = rest
    group, slots, packed = recv_ref.shape
    width = wout_ref.shape[0]
    rows = act.shape[0]
    head = width // HEADS
    scale = 1.0 / head**0.5
    total = group * slots
    got = recv_ref[...].reshape(total, packed)
    place = got[:, 2 * width : 2 * width + 1].astype(F32) - 1.0
    spots = lax.broadcasted_iota(jnp.int32, (total, rows), 1).astype(F32)
    pick = jnp.where(place == spots, 1.0, 0.0).astype(BF16)
    tokens = tn(pick, got[:, :width])
    grad = tn(pick, got[:, width : 2 * width])
    grad16 = grad.astype(BF16)
    normed, inverse = normalize(tokens)
    xn = normed.astype(BF16)
    for block in range(4):
        cols = slice(block * width, (block + 1) * width)
        proj = nn(xn, win_ref[:, cols])
        sig = jax.nn.sigmoid(proj)
        act[:, cols] = (proj * sig).astype(BF16)
        slope_p[:, cols] = sig * (1.0 + proj * (1.0 - sig))
    row_at = lax.broadcasted_iota(jnp.int32, (rows, 1), 0)
    col_at = lax.broadcasted_iota(jnp.int32, (1, rows), 1)
    bound = jnp.int32(0)
    row_seg = jnp.zeros((rows, 1), jnp.int32)
    col_seg = jnp.zeros((1, rows), jnp.int32)
    for seq in range(len_ref.shape[1]):
        bound = bound + len_ref[0, seq]
        row_seg = row_seg + jnp.where(row_at >= bound, 1, 0)
        col_seg = col_seg + jnp.where(col_at >= bound, 1, 0)
    mask = (row_seg == col_seg) & (col_at <= row_at)
    pair = 2 * head
    low = lax.broadcasted_iota(jnp.int32, (rows, pair), 1) < head

    def half(values, which):
        return jnp.where(low if which == 0 else ~low, values, jnp.zeros_like(values))

    def cut(block, duo):
        start = block * width + duo * pair
        return act[:, start : start + pair]

    outs = []
    for duo in range(HEADS // 2):
        value, query, key = cut(1, duo), cut(2, duo), cut(3, duo)
        parts = []
        for which in range(2):
            at = 2 * duo + which
            scores = nt(half(query, which), key) * scale
            sig = jax.nn.sigmoid(scores)
            weight = jnp.where(mask, scores * sig * (1.0 / MAXLEN), 0.0).astype(BF16)
            attn[at] = weight
            slope_s[at] = jnp.where(
                mask, sig * (1.0 + scores * (1.0 - sig)) * (scale / MAXLEN), 0.0
            )
            parts.append(nn(weight, value))
        outs.append(jnp.where(low, parts[0], parts[1]))
    onorm, oinv = normalize(jnp.concatenate(outs, axis=1))
    gate = act[:, :width].astype(F32)
    gated = (gate * onorm).astype(BF16)
    grad_z = nt(grad16, wout_ref[...])
    gproj[:, :width] = (grad_z * onorm * slope_p[:, :width]).astype(BF16)
    grad_out = norm_back(grad_z * gate, onorm, oinv).astype(BF16)
    for duo in range(HEADS // 2):
        value, query, key = cut(1, duo), cut(2, duo), cut(3, duo)
        gout = grad_out[:, duo * pair : (duo + 1) * pair]
        parts = ([], [], [])
        for which in range(2):
            at = 2 * duo + which
            gscore = (nt(half(gout, which), value) * slope_s[at]).astype(BF16)
            parts[0].append(tn(attn[at], gout))
            parts[1].append(nn(gscore, key))
            parts[2].append(tn(gscore, query))
        for block in range(3):
            start = (block + 1) * width + duo * pair
            cols = slice(start, start + pair)
            both = jnp.where(low, parts[block][0], parts[block][1])
            gproj[:, cols] = (both * slope_p[:, cols]).astype(BF16)
    grad_xn = nt(gproj[...], win_ref[...])
    grad_tokens = (grad + norm_back(grad_xn, normed, inverse)).astype(BF16)
    out_ref[...] = nn(pick, grad_tokens).astype(BF16).reshape(group, slots, width)
    xn_out[...] = xn
    gated_out[...] = gated
    g_out[...] = grad16


def whole_kernel(
    slots,
    factor,
    len_any,
    dest_any,
    pos_any,
    ev_any,
    ct_any,
    win_any,
    wout_any,
    grad_ref,
    in_ref,
    sum_ref,
    final_ref,
    len_ref,
    dest_ref,
    pos_ref,
    ev_ref,
    ct_ref,
    win_ref,
    wout_ref,
    pick_ref,
    back_ref,
    ev_send,
    ct_send,
    at_send,
    ev_got,
    ct_got,
    at_got,
    act,
    slope_p,
    gproj,
    attn,
    slope_s,
    xn_ref,
    out_ref,
    part_ref,
    core_got,
    one_send,
    one_got,
    two_keep,
    two_send,
    two_got,
    up_send,
    rs_got,
    pair_send,
    pair_keep,
    pair_got,
    load_sems,
    row_ssem,
    row_rsem,
    core_ssem,
    core_rsem,
    one_ssem,
    one_rsem,
    two_ssem,
    two_rsem,
    up_ssem,
    up_rsem,
    pair_ssem,
    pair_rsem,
    cross_ssem,
    mate_ssem,
    rim_ssem,
    ag_rsem,
    fwd_ssem,
    fwd_rsem,
):
    rows, width = ev_ref.shape
    group = ev_send.shape[0]
    colors, depth, span = rs_got.shape[0], rs_got.shape[3], rs_got.shape[4]
    total = group * slots
    head = width // HEADS
    scale = 1.0 / head**0.5
    me = lax.axis_index("dp")
    rep = lax.axis_index("replica")
    core = lax.rem(rep, 2)
    other = 1 - core
    spot = rep // 2
    partner = {"replica": spot * 2 + other}
    low_bit, high_bit = lax.rem(me, 2), me // 2
    near = high_bit * 2 + 1 - low_bit
    far = (1 - high_bit) * 2 + low_bit
    third = 3 - me

    def dp_peer(step):
        return lax.rem(me + step, group)

    side = spot // 2
    away = 1 - side
    inner = (spot == 1) | (spot == 2)
    outer = ~inner
    hub = {"replica": (1 + side) * 2 + core}
    mate = {"replica": (3 - spot) * 2 + core}
    rim = {"replica": 3 * side * 2 + core}
    keep = 1 - lax.rem((spot + 1) // 2, 2)
    give = 1 - keep
    pal = {"replica": (spot + 1 - 2 * lax.rem(spot, 2)) * 2 + core}
    far_hub = {"replica": (2 - side) * 2 + core}
    far_rim = {"replica": 3 * away * 2 + core}

    loads = [
        pltpu.make_async_copy(source, target, load_sems.at[at])
        for at, (source, target) in enumerate(
            (
                (ev_any, ev_ref),
                (ct_any, ct_ref),
                (win_any, win_ref),
                (wout_any, wout_ref),
                (dest_any, dest_ref),
                (pos_any, pos_ref),
                (len_any, len_ref),
            )
        )
    ]
    for at in (4, 0, 5, 1, 6):
        loads[at].start()
    barrier = pltpu.get_barrier_semaphore()
    for step in range(1, group):
        pl.semaphore_signal(barrier, inc=1, device_id={"dp": dp_peer(step)}, device_id_type=MESH)
    pl.semaphore_signal(barrier, inc=1, device_id=partner, device_id_type=MESH)

    @pl.when(outer)
    def _():
        for device in (hub, far_hub, far_rim):
            pl.semaphore_signal(barrier, inc=1, device_id=device, device_id_type=MESH)

    @pl.when(inner)
    def _():
        for device in (mate, rim, far_rim):
            pl.semaphore_signal(barrier, inc=1, device_id=device, device_id_type=MESH)

    def describe(src, dst, ssem, rsem, device):
        return pltpu.make_async_remote_copy(
            src_ref=src,
            dst_ref=dst,
            send_sem=ssem,
            recv_sem=rsem,
            device_id=device,
            device_id_type=MESH,
        )

    def send(src, dst, ssem, rsem, device):
        describe(src, dst, ssem, rsem, device).start()

    def sent(like, ssem):
        describe(like, like, ssem, ssem, partner).wait_send()

    def came(like, rsem):
        describe(like, like, rsem, rsem, partner).wait_recv()

    loads[4].wait()
    dest = dest_ref[...]
    hot = lax.broadcasted_iota(jnp.int32, (8, rows), 0) == dest
    upper = lax.broadcasted_iota(jnp.int32, (rows, rows), 0) < lax.broadcasted_iota(
        jnp.int32, (rows, rows), 1
    )
    earlier = nn(
        jnp.where(hot, 1.0, 0.0).astype(BF16), jnp.where(upper, 1.0, 0.0).astype(BF16)
    )
    slot = jnp.sum(jnp.where(hot, earlier, 0.0), axis=0, keepdims=True).astype(jnp.int32)
    slot_iota = lax.broadcasted_iota(jnp.int32, (total, rows), 0)
    pick = jnp.where(slot_iota == dest * slots + slot, 1.0, 0.0).astype(BF16)
    pick_ref[...] = pick
    packed = (group, slots, width)
    loads[0].wait()
    ev_send[...] = nn(pick, ev_ref[...]).astype(BF16).reshape(packed)
    pl.semaphore_wait(barrier, group + 3)

    def rows_out(kind, src, dst):
        for step in (3, 1, 2):
            peer = step ^ me
            send(src.at[peer], dst.at[me], row_ssem.at[kind], row_rsem.at[kind], {"dp": peer})
        dst[me] = src[me]

    def others(buffer):
        return buffer.at[pl.ds(0, group - 1)]

    rows_out(1, ev_send, ev_got)
    loads[2].start()
    loads[3].start()
    loads[5].wait()
    spots = jnp.broadcast_to(pos_ref[...] + 1, (8, rows)).astype(F32).astype(BF16)
    lane_iota = lax.broadcasted_iota(jnp.int32, (LANES, rows), 0)
    for dp in range(group):
        there = jnp.where((lane_iota == slot) & (dest == dp), 1.0, 0.0).astype(BF16)
        at_send[dp] = nt(spots, there)
    rows_out(0, at_send, at_got)
    loads[1].wait()
    ct_send[...] = nn(pick, ct_ref[...]).astype(BF16).reshape(packed)
    sent(others(ev_send), row_ssem.at[1])
    rows_out(2, ct_send, ct_got)

    came(others(at_got), row_rsem.at[0])
    came(others(ev_got), row_rsem.at[1])
    place = jnp.zeros((8, total), F32)
    blank = jnp.zeros((8, total - LANES), F32)
    for dp in range(group):
        there = jnp.concatenate([at_got[dp], blank], axis=1)
        place = place + pltpu.roll(there, dp * slots, 1)
    row_iota = lax.broadcasted_iota(jnp.int32, (rows, total), 0).astype(F32) + 1.0
    fetch = jnp.where(row_iota == place[:1], 1.0, 0.0).astype(BF16)
    tokens = nn(fetch, ev_got[...].reshape(total, width))
    normed, inverse = normalize(tokens)
    xn = normed.astype(BF16)
    xn_ref[...] = xn
    loads[2].wait()
    loads[3].wait()
    for block in range(4):
        cols = slice(block * width, (block + 1) * width)
        proj = nn(xn, win_ref[:, cols])
        sig = jax.nn.sigmoid(proj)
        act[:, cols] = (proj * sig).astype(BF16)
        slope_p[:, cols] = sig * (1.0 + proj * (1.0 - sig))
    row_at = lax.broadcasted_iota(jnp.int32, (rows, 1), 0)
    col_at = lax.broadcasted_iota(jnp.int32, (1, rows), 1)
    loads[6].wait()
    bound = jnp.int32(0)
    row_seg = jnp.zeros((rows, 1), jnp.int32)
    col_seg = jnp.zeros((1, rows), jnp.int32)
    for seq in range(len_ref.shape[1]):
        bound = bound + len_ref[0, seq]
        row_seg = row_seg + jnp.where(row_at >= bound, 1, 0)
        col_seg = col_seg + jnp.where(col_at >= bound, 1, 0)
    mask = (row_seg == col_seg) & (col_at <= row_at)
    pair = 2 * head
    low = lax.broadcasted_iota(jnp.int32, (rows, pair), 1) < head

    def half(values, which):
        return jnp.where(low if which == 0 else ~low, values, jnp.zeros_like(values))

    def cut(block, duo):
        start = block * width + duo * pair
        return act[:, start : start + pair]

    outs = []
    for duo in range(HEADS // 2):
        value, query, key = cut(1, duo), cut(2, duo), cut(3, duo)
        parts = []
        for which in range(2):
            at = 2 * duo + which
            scores = nt(half(query, which), key) * scale
            sig = jax.nn.sigmoid(scores)
            weight = jnp.where(mask, scores * sig * (1.0 / MAXLEN), 0.0).astype(BF16)
            attn[at] = weight
            slope_s[at] = jnp.where(
                mask, sig * (1.0 + scores * (1.0 - sig)) * (scale / MAXLEN), 0.0
            )
            parts.append(nn(weight, value))
        outs.append(jnp.where(low, parts[0], parts[1]))
    onorm, oinv = normalize(jnp.concatenate(outs, axis=1))
    gate = act[:, :width].astype(F32)
    gated = (gate * onorm).astype(BF16)

    came(others(ct_got), row_rsem.at[2])
    grad = nn(fetch, ct_got[...].reshape(total, width))
    grad16 = grad.astype(BF16)

    def store_part(color, whole, row_of, column_of):
        for edge in range(2):
            for piece in range(4):
                for dp in range(group):
                    row, column = row_of(edge, piece, dp), column_of(edge, piece, dp)
                    part_ref[color, edge, piece % 2, piece // 2, dp] = whole[
                        row : row + depth, column : column + span
                    ]
        send(
            part_ref.at[color, other],
            core_got.at[color],
            core_ssem.at[0],
            core_rsem.at[color],
            partner,
        )

    store_part(
        0,
        tn(gated, grad16).astype(BF16),
        lambda edge, piece, dp: (2 * dp + edge) * depth,
        lambda edge, piece, dp: piece * span,
    )
    grad_z = nt(grad16, wout_ref[...])
    gproj[:, :width] = (grad_z * onorm * slope_p[:, :width]).astype(BF16)
    grad_out = norm_back(grad_z * gate, onorm, oinv).astype(BF16)

    def back_duo(duo):
        value, query, key = cut(1, duo), cut(2, duo), cut(3, duo)
        gout = grad_out[:, duo * pair : (duo + 1) * pair]
        parts = ([], [], [])
        for which in range(2):
            at = 2 * duo + which
            gscore = (nt(half(gout, which), value) * slope_s[at]).astype(BF16)
            parts[0].append(tn(attn[at], gout))
            parts[1].append(nn(gscore, key))
            parts[2].append(tn(gscore, query))
        for block in range(3):
            start = (block + 1) * width + duo * pair
            cols = slice(start, start + pair)
            both = jnp.where(low, parts[block][0], parts[block][1])
            gproj[:, cols] = (both * slope_p[:, cols]).astype(BF16)

    def stage_zero(duo):
        columns = jnp.concatenate(
            [
                gproj[:, dp * width + duo * span : dp * width + (duo + 1) * span]
                for dp in range(group)
            ],
            axis=1,
        )
        store_part(
            duo + 1,
            tn(xn_ref[...], columns).astype(BF16),
            lambda edge, piece, dp: (4 * edge + piece) * depth,
            lambda edge, piece, dp: dp * span,
        )

    def ways(way):
        return (near, far) if way == 0 else (far, near)

    def stage_one(color):
        came(core_got.at[color], core_rsem.at[color])
        for way in range(2):
            first, second = ways(way)

            def both(dp):
                mine = part_ref[color, core, way, :, dp].astype(F32)
                return mine + core_got[color, way, :, dp].astype(F32)

            one_send[color, way, 0] = both(first).astype(BF16)
            one_send[color, way, 1] = both(third).astype(BF16)
            send(
                one_send.at[color, way],
                one_got.at[color, way],
                one_ssem.at[0],
                one_rsem.at[color],
                {"dp": first},
            )
            two_keep[color, way, 0] = both(me)
            two_keep[color, way, 1] = both(second)

    def stage_two(color):
        came(one_got.at[color], one_rsem.at[color])
        for way in range(2):
            two_send[color, way] = (
                two_keep[color, way, 1] + one_got[color, way, 1].astype(F32)
            ).astype(BF16)
            send(
                two_send.at[color, way],
                two_got.at[color, way],
                two_ssem.at[0],
                two_rsem.at[color],
                {"dp": ways(way)[1]},
            )

    def echoed(color):
        return color < ECHOED

    def stage_three(color):
        came(two_got.at[color], two_rsem.at[color])
        for way in range(2):
            summed = (
                two_keep[color, way, 0]
                + one_got[color, way, 0].astype(F32)
                + two_got[color, way].astype(F32)
            )
            two_keep[color, way, 0] = summed
            up_send[color, :, way] = summed.astype(BF16)

        @pl.when(outer)
        def _():
            for slot, at, device in ((away, 2, far_hub), (side, 0, hub)):
                send(
                    up_send.at[color, slot],
                    rs_got.at[color, at],
                    up_ssem.at[0],
                    up_rsem.at[color],
                    device,
                )

        @pl.when(inner)
        def _():
            send(
                up_send.at[color, away],
                rs_got.at[color, 1],
                up_ssem.at[0],
                up_rsem.at[color],
                mate,
            )

    def stage_c(color):
        @pl.when(inner)
        def _():
            came(rs_got.at[color], up_rsem.at[color])
            for way in range(2):
                summed = two_keep[color, way, 0, side]
                for term in range(3):
                    summed = summed + rs_got[color, term, way].astype(F32)
                final_ref[color, core, side, way] = summed.astype(BF16)
            mine = final_ref.at[color, core, side]
            if not echoed(color):
                send(mine, mine, rim_ssem.at[0], ag_rsem.at[color], far_rim)
            send(mine, mine, mate_ssem.at[0], ag_rsem.at[color], mate)
            send(mine, mine, rim_ssem.at[0], ag_rsem.at[color], rim)
            send(mine, mine, fwd_ssem.at[0], fwd_rsem.at[color], partner)

    def stage_d(color):
        @pl.when(inner)
        def _():
            there = final_ref.at[color, core, away]
            came(there, ag_rsem.at[color])
            if echoed(color):
                send(there, there, rim_ssem.at[0], ag_rsem.at[color], rim)
            send(there, there, fwd_ssem.at[0], fwd_rsem.at[color], partner)

    def stage_e(color):
        @pl.when(outer)
        def _():
            there = final_ref.at[color, core]
            came(there, ag_rsem.at[color])
            send(there, there, fwd_ssem.at[0], fwd_rsem.at[color], partner)

    def pair_zero(color):
        came(core_got.at[color], core_rsem.at[color])
        for way in range(2):
            for dp in range(group):

                def both(slot):
                    mine = part_ref[color, core, way, slot, dp].astype(F32)
                    return mine + core_got[color, way, slot, dp].astype(F32)

                pair_send[way, dp] = both(give).astype(BF16)
                pair_keep[way, dp] = both(keep)
        send(pair_send, pair_got, pair_ssem.at[0], pair_rsem.at[0], pal)

    def pair_one(color):
        came(pair_got, pair_rsem.at[0])
        for way in range(2):
            first, second = ways(way)

            def both(dp):
                return pair_keep[way, dp] + pair_got[way, dp].astype(F32)

            one_send[color, way, 0, 0] = both(first).astype(BF16)
            one_send[color, way, 0, 1] = both(third).astype(BF16)
            send(
                one_send.at[color, way, 0],
                one_got.at[color, way, 0],
                one_ssem.at[1],
                one_rsem.at[color],
                {"dp": first},
            )
            two_keep[color, way, 0, 0] = both(me)
            two_keep[color, way, 0, 1] = both(second)

    def pair_two(color):
        came(one_got.at[color, pl.ds(0, 2), 0], one_rsem.at[color])
        for way in range(2):
            two_send[color, way, 0] = (
                two_keep[color, way, 0, 1] + one_got[color, way, 0, 1].astype(F32)
            ).astype(BF16)
            send(
                two_send.at[color, way, 0],
                two_got.at[color, way, 0],
                two_ssem.at[1],
                two_rsem.at[color],
                {"dp": ways(way)[1]},
            )

    def pair_three(color):
        came(two_got.at[color, pl.ds(0, 2), 0], two_rsem.at[color])
        for way in range(2):
            up_send[color, 0, way] = (
                two_keep[color, way, 0, 0]
                + one_got[color, way, 0, 0].astype(F32)
                + two_got[color, way, 0].astype(F32)
            ).astype(BF16)
        send(
            up_send.at[color, 0], rs_got.at[color, 0], cross_ssem.at[0], up_rsem.at[color], mate
        )

    def pair_four(color):
        came(rs_got.at[color, 0], up_rsem.at[color])
        for way in range(2):
            final_ref[color, core, keep, way] = (
                up_send[color, 0, way].astype(F32) + rs_got[color, 0, way].astype(F32)
            ).astype(BF16)
        mine = final_ref.at[color, core, keep]
        send(mine, mine, cross_ssem.at[0], ag_rsem.at[color], pal)
        send(mine, mine, fwd_ssem.at[0], fwd_rsem.at[color], partner)

    def pair_five(color):
        there = final_ref.at[color, core, give]
        came(there, ag_rsem.at[color])
        send(there, there, fwd_ssem.at[0], fwd_rsem.at[color], partner)

    def stage_f(color):
        came(final_ref.at[color, other], fwd_rsem.at[color])
        if color == 0:
            for edge in range(2):
                for piece in range(4):
                    rows_at = slice(edge * depth, (edge + 1) * depth)
                    sum_ref[rows_at, piece * span : (piece + 1) * span] = (
                        final_ref[0, edge, piece // 2, piece % 2].astype(F32) * factor
                    )
        else:
            in_ref[:, (color - 1) * span : color * span] = (
                final_ref[color].astype(F32) * factor
            ).reshape(width, span)

    back_duo(0)
    stage_zero(0)
    stage_one(0)
    back_duo(1)
    stage_zero(1)
    stage_one(1)
    back_duo(2)
    stage_zero(2)
    pair_zero(PAIRED)
    back_duo(3)
    stage_zero(3)
    stage_two(0)
    stage_one(3)
    grad_xn = nt(gproj[...], win_ref[...])
    stage_two(1)
    stage_one(4)
    grad_tokens = (grad + norm_back(grad_xn, normed, inverse)).astype(BF16)
    out_ref[...] = tn(fetch, grad_tokens).astype(BF16).reshape(packed)
    stage_three(0)
    pair_one(PAIRED)
    stage_two(3)
    stage_three(1)
    stage_two(4)
    pair_two(PAIRED)
    stage_three(3)
    stage_c(0)
    stage_three(4)
    pair_three(PAIRED)
    rows_out(3, out_ref, back_ref)
    stage_c(1)
    stage_c(3)
    stage_d(0)
    stage_c(4)
    pair_four(PAIRED)
    stage_d(1)
    stage_e(0)
    pair_five(PAIRED)
    stage_d(3)
    stage_e(1)
    stage_d(4)
    stage_e(3)
    came(others(back_ref), row_rsem.at[3])
    grad_ref[...] = tn(pick_ref[...], back_ref[...].reshape(total, width)).astype(BF16)
    stage_e(4)
    for color in range(colors):
        stage_f(color)
    sent(others(at_send), row_ssem.at[0])
    sent(others(ct_send), row_ssem.at[2])
    sent(others(out_ref), row_ssem.at[3])
    sent(core_got, core_ssem.at[0])
    plain = pl.ds(0, colors - 1)
    sent(one_send.at[plain], one_ssem.at[0])
    sent(two_send.at[plain], two_ssem.at[0])
    sent(final_ref.at[0, 0], one_ssem.at[1])
    sent(final_ref.at[0, 0, 0], two_ssem.at[1])
    sent(pair_send, pair_ssem.at[0])
    sent(final_ref.at[0, 0], cross_ssem.at[0])
    half_of = final_ref.at[plain, 0, 0]
    whole_of = final_ref.at[plain, 0]

    @pl.when(inner)
    def _():
        sent(half_of, up_ssem.at[0])
        sent(half_of, mate_ssem.at[0])
        sent(whole_of, rim_ssem.at[0])

    @pl.when(outer)
    def _():
        sent(whole_of, up_ssem.at[0])

    sent(final_ref.at[pl.ds(0, colors), 0], fwd_ssem.at[0])


def finish_kernel(*refs):
    count = len(refs) // 2
    sources, outs, sems = refs[:count], refs[count : 2 * count], refs[2 * count]
    copies = [
        pltpu.make_async_copy(sources[at], outs[at], sems.at[at]) for at in range(count)
    ]
    for copy in copies:
        copy.start()
    for copy in copies:
        copy.wait()


def gather_kernel(pick_ref, back_ref, ev_ref):
    group, slots, width = back_ref.shape
    ev_ref[...] = tn(pick_ref[...], back_ref[...].reshape(group * slots, width)).astype(BF16)


VMEM = pl.BlockSpec(memory_space=pltpu.VMEM)
SMEM = pl.BlockSpec(memory_space=pltpu.SMEM)


def shape_of(shape, dtype=BF16):
    return jax.ShapeDtypeStruct(shape, dtype)


def swap(send, ident):
    group = send.shape[0]
    return pl.pallas_call(
        swap_kernel,
        out_shape=shape_of(send.shape),
        in_specs=[VMEM],
        out_specs=VMEM,
        scratch_shapes=[
            pltpu.SemaphoreType.DMA((group,)),
            pltpu.SemaphoreType.DMA((group,)),
            pltpu.SemaphoreType.DMA,
        ],
        compiler_params=pltpu.CompilerParams(collective_id=ident, has_side_effects=True),
        name="swap",
    )(send)


def body(events, cotangent, weight_in, weight_out, plan_dest, plan_pos, seq_lengths):
    group = lax.axis_size("dp")
    replicas = lax.axis_size("replica")
    rows, width = events.shape
    inner = weight_in.shape[1]
    slots = 3 * rows // (2 * group)
    total = group * slots
    chain = replicas // 2
    pair = 2 * width // HEADS
    depth = width // (2 * chain)
    stacked = (
        group == 4
        and chain == 4
        and inner == group * width
        and pair * chain == width
        and pair % LANES == 0
        and depth % 16 == 0
        and slots <= LANES
        and total % LANES == 0
    )
    factor = 1.0 / (rows * group * replicas) ** 0.5
    outgoing_shape = shape_of((group, slots, width))
    wide = [
        pltpu.VMEM((rows, inner), BF16),
        pltpu.VMEM((rows, inner), F32),
    ]
    square = [
        pltpu.VMEM((HEADS, rows, rows), BF16),
        pltpu.VMEM((HEADS, rows, rows), F32),
    ]
    dest, place = plan_dest.reshape(1, rows), plan_pos.reshape(1, rows)
    if stacked:
        packed = pltpu.VMEM((group, slots, width), BF16)
        spots = pltpu.VMEM((group, 8, LANES), F32)
        duos = HEADS // 2
        colors = duos + 1
        piece = (depth, pair)
        sized = lambda *lead, dtype=BF16: pltpu.VMEM(lead + piece, dtype)
        dma = pltpu.SemaphoreType.DMA
        results = pl.pallas_call(
            functools.partial(whole_kernel, slots, factor),
            out_shape=(
                pltpu.VMEM((rows, width), BF16),
                pltpu.VMEM((width, width), F32),
                pltpu.VMEM((width // group, width), F32),
            ),
            in_specs=[pl.BlockSpec(memory_space=pl.ANY)] * 7,
            out_specs=(VMEM,) * 3,
            scratch_shapes=[
                sized(colors, 2, 2, 2),
                pltpu.SMEM(seq_lengths.shape, jnp.int32),
                pltpu.VMEM((1, rows), jnp.int32),
                pltpu.VMEM((1, rows), jnp.int32),
                pltpu.VMEM((rows, width), BF16),
                pltpu.VMEM((rows, width), BF16),
                pltpu.VMEM(weight_in.shape, BF16),
                pltpu.VMEM(weight_out.shape, BF16),
                pltpu.VMEM((total, rows), BF16),
                packed,
            ]
            + [packed, packed, spots] * 2
            + wide
            + [pltpu.VMEM((rows, inner), BF16)]
            + square
            + [
                pltpu.VMEM((rows, width), BF16),
                packed,
                sized(colors, 2, 2, 2, group),
                sized(colors, 2, 2, group),
                sized(colors, 2, 2, 2),
                sized(colors, 2, 2, 2),
                sized(colors, 2, 2, 2, dtype=F32),
                sized(colors, 2, 2),
                sized(colors, 2, 2),
                sized(colors, 2, 2),
                sized(colors, 3, 2),
                sized(2, group),
                sized(2, group, dtype=F32),
                sized(2, group),
                dma((7,)),
                dma((4,)),
                dma((4,)),
            ]
            + [dma((1,)), dma((colors,))]
            + [dma((2,)), dma((colors,))] * 2
            + [dma((1,)), dma((colors,))]
            + [dma((1,))] * 5
            + [dma((colors,)), dma((1,)), dma((colors,))],
            compiler_params=pltpu.CompilerParams(collective_id=0, has_side_effects=True),
            name="whole",
        )(seq_lengths, dest, place, events, cotangent, weight_in, weight_out)
        return pl.pallas_call(
            finish_kernel,
            out_shape=tuple(shape_of(value.shape, value.dtype) for value in results),
            in_specs=[VMEM] * 3,
            out_specs=(pl.BlockSpec(memory_space=pltpu.HBM),) * 3,
            scratch_shapes=[pltpu.SemaphoreType.DMA((3,))],
            name="finish",
        )(*[pltpu.with_memory_space_constraint(value, pltpu.VMEM) for value in results])
    send, pick = pl.pallas_call(
        functools.partial(prep_kernel, slots),
        out_shape=(shape_of((group, slots, 2 * width + LANES)), shape_of((total, rows))),
        in_specs=[VMEM] * 4,
        out_specs=(VMEM, VMEM),
        name="prep",
    )(dest, place, events, cotangent)
    recv = swap(send, 0)
    outgoing, normed_in, grad_proj, gated, grad_rows = pl.pallas_call(
        layer_kernel,
        out_shape=(
            outgoing_shape,
            shape_of((rows, width)),
            shape_of((rows, inner)),
            shape_of((rows, width)),
            shape_of((rows, width)),
        ),
        in_specs=[SMEM] + [VMEM] * 3,
        out_specs=(VMEM,) * 5,
        scratch_shapes=wide + square,
        name="layer",
    )(seq_lengths, recv, weight_in, weight_out)
    back = swap(outgoing, 1)
    grad_events = pl.pallas_call(
        gather_kernel,
        out_shape=shape_of((rows, width)),
        in_specs=[VMEM] * 2,
        out_specs=VMEM,
        name="finish",
    )(pick, back)
    rows_all = lax.all_gather(normed_in, "dp", axis=0, tiled=True)
    cot_all = lax.all_gather(grad_rows, "dp", axis=0, tiled=True)
    proj_cols = lax.all_to_all(grad_proj, "dp", split_axis=1, concat_axis=0, tiled=True)
    gated_cols = lax.all_to_all(gated, "dp", split_axis=1, concat_axis=0, tiled=True)
    shard_in = jnp.einsum("rd,rf->df", rows_all, proj_cols, preferred_element_type=F32)
    shard_out = jnp.einsum("re,rd->ed", gated_cols, cot_all, preferred_element_type=F32)
    total_in, total_out = lax.psum((shard_in, shard_out), "replica")
    return grad_events, total_in * factor, total_out * factor


def solution(mesh):
    return jax.shard_map(
        body,
        mesh=mesh,
        in_specs=(
            P(("dp", "replica"), None),
            P(("dp", "replica"), None),
            P(),
            P(),
            P(("dp", "replica")),
            P(("dp", "replica")),
            P(("dp", "replica"), None),
        ),
        out_specs=(P(("dp", "replica"), None), P(None, "dp"), P("dp", None)),
        check_vma=False,
    )
```

```python
import functools

import jax
import jax.numpy as jnp
from jax import lax
from jax.experimental import pallas as pl
from jax.experimental.pallas import tpu as pltpu
from jax.sharding import PartitionSpec as P

HEADS = 8
MAXLEN = 128
EPS = 1e-05
ECHOED = 2
PAIRED = 2
LANES = 128
MESH = pl.DeviceIdType.MESH
F32 = jnp.float32
BF16 = jnp.bfloat16


def contract(left, right, dims):
    return lax.dot_general(left, right, ((dims[:1], dims[1:]), ((), ())), preferred_element_type=F32)


def nn(left, right):
    return contract(left, right, (1, 0))


def nt(left, right):
    return contract(left, right, (1, 1))


def tn(left, right):
    return contract(left, right, (0, 0))


def normalize(values):
    center = values - jnp.mean(values, axis=-1, keepdims=True)
    inverse = lax.rsqrt(jnp.mean(center * center, axis=-1, keepdims=True) + EPS)
    return center * inverse, inverse


def norm_back(grad, normed, inverse):
    return inverse * (
        grad
        - jnp.mean(grad, axis=-1, keepdims=True)
        - normed * jnp.mean(grad * normed, axis=-1, keepdims=True)
    )


def prep_kernel(slot_count, dest_ref, pos_ref, ev_ref, ct_ref, send_ref, pick_ref):
    rows, width = ev_ref.shape
    group = send_ref.shape[0]
    dest = dest_ref[...]
    hot = lax.broadcasted_iota(jnp.int32, (8, rows), 0) == dest
    upper = lax.broadcasted_iota(jnp.int32, (rows, rows), 0) < lax.broadcasted_iota(
        jnp.int32, (rows, rows), 1
    )
    earlier = nn(
        jnp.where(hot, 1.0, 0.0).astype(BF16), jnp.where(upper, 1.0, 0.0).astype(BF16)
    )
    slot = jnp.sum(jnp.where(hot, earlier, 0.0), axis=0, keepdims=True).astype(jnp.int32)
    flat = dest * slot_count + slot
    total = group * slot_count
    chosen = lax.broadcasted_iota(jnp.int32, (total, rows), 0) == flat
    pick = jnp.where(chosen, 1.0, 0.0).astype(BF16)
    pick_ref[...] = pick
    place = jnp.sum(
        jnp.where(chosen, pos_ref[...].astype(F32) + 1.0, 0.0), axis=1, keepdims=True
    )
    shape = (group, slot_count)
    send_ref[:, :, :width] = nn(pick, ev_ref[...]).astype(BF16).reshape(shape + (width,))
    send_ref[:, :, width : 2 * width] = nn(pick, ct_ref[...]).astype(BF16).reshape(shape + (width,))
    send_ref[:, :, 2 * width :] = (
        jnp.broadcast_to(place, (total, LANES)).astype(BF16).reshape(shape + (LANES,))
    )


def swap_kernel(send_ref, recv_ref, send_sem, recv_sem, own_sem):
    group = lax.axis_size("dp")
    me = lax.axis_index("dp")
    barrier = pltpu.get_barrier_semaphore()
    for step in range(1, group):
        pl.semaphore_signal(
            barrier, inc=1, device_id={"dp": lax.rem(me + step, group)}, device_id_type=MESH
        )
    own = pltpu.make_async_copy(send_ref.at[me], recv_ref.at[me], own_sem)
    own.start()
    pl.semaphore_wait(barrier, group - 1)
    copies = []
    for step in range(1, group):
        peer = lax.rem(me + step, group)
        copy = pltpu.make_async_remote_copy(
            src_ref=send_ref.at[peer],
            dst_ref=recv_ref.at[me],
            send_sem=send_sem.at[step],
            recv_sem=recv_sem.at[step],
            device_id={"dp": peer},
            device_id_type=MESH,
        )
        copy.start()
        copies.append(copy)
    own.wait()
    for copy in copies:
        copy.wait()


def layer_kernel(
    len_ref,
    recv_ref,
    win_ref,
    wout_ref,
    out_ref,
    *rest,
):
    xn_out, gproj, gated_out, g_out, act, slope_p, attn, slope_s = rest
    group, slots, packed = recv_ref.shape
    width = wout_ref.shape[0]
    rows = act.shape[0]
    head = width // HEADS
    scale = 1.0 / head**0.5
    total = group * slots
    got = recv_ref[...].reshape(total, packed)
    place = got[:, 2 * width : 2 * width + 1].astype(F32) - 1.0
    spots = lax.broadcasted_iota(jnp.int32, (total, rows), 1).astype(F32)
    pick = jnp.where(place == spots, 1.0, 0.0).astype(BF16)
    tokens = tn(pick, got[:, :width])
    grad = tn(pick, got[:, width : 2 * width])
    grad16 = grad.astype(BF16)
    normed, inverse = normalize(tokens)
    xn = normed.astype(BF16)
    for block in range(4):
        cols = slice(block * width, (block + 1) * width)
        proj = nn(xn, win_ref[:, cols])
        sig = jax.nn.sigmoid(proj)
        act[:, cols] = (proj * sig).astype(BF16)
        slope_p[:, cols] = sig * (1.0 + proj * (1.0 - sig))
    row_at = lax.broadcasted_iota(jnp.int32, (rows, 1), 0)
    col_at = lax.broadcasted_iota(jnp.int32, (1, rows), 1)
    bound = jnp.int32(0)
    row_seg = jnp.zeros((rows, 1), jnp.int32)
    col_seg = jnp.zeros((1, rows), jnp.int32)
    for seq in range(len_ref.shape[1]):
        bound = bound + len_ref[0, seq]
        row_seg = row_seg + jnp.where(row_at >= bound, 1, 0)
        col_seg = col_seg + jnp.where(col_at >= bound, 1, 0)
    mask = (row_seg == col_seg) & (col_at <= row_at)
    pair = 2 * head
    low = lax.broadcasted_iota(jnp.int32, (rows, pair), 1) < head

    def half(values, which):
        return jnp.where(low if which == 0 else ~low, values, jnp.zeros_like(values))

    def cut(block, duo):
        start = block * width + duo * pair
        return act[:, start : start + pair]

    outs = []
    for duo in range(HEADS // 2):
        value, query, key = cut(1, duo), cut(2, duo), cut(3, duo)
        parts = []
        for which in range(2):
            at = 2 * duo + which
            scores = nt(half(query, which), key) * scale
            sig = jax.nn.sigmoid(scores)
            weight = jnp.where(mask, scores * sig * (1.0 / MAXLEN), 0.0).astype(BF16)
            attn[at] = weight
            slope_s[at] = jnp.where(
                mask, sig * (1.0 + scores * (1.0 - sig)) * (scale / MAXLEN), 0.0
            )
            parts.append(nn(weight, value))
        outs.append(jnp.where(low, parts[0], parts[1]))
    onorm, oinv = normalize(jnp.concatenate(outs, axis=1))
    gate = act[:, :width].astype(F32)
    gated = (gate * onorm).astype(BF16)
    grad_z = nt(grad16, wout_ref[...])
    gproj[:, :width] = (grad_z * onorm * slope_p[:, :width]).astype(BF16)
    grad_out = norm_back(grad_z * gate, onorm, oinv).astype(BF16)
    for duo in range(HEADS // 2):
        value, query, key = cut(1, duo), cut(2, duo), cut(3, duo)
        gout = grad_out[:, duo * pair : (duo + 1) * pair]
        parts = ([], [], [])
        for which in range(2):
            at = 2 * duo + which
            gscore = (nt(half(gout, which), value) * slope_s[at]).astype(BF16)
            parts[0].append(tn(attn[at], gout))
            parts[1].append(nn(gscore, key))
            parts[2].append(tn(gscore, query))
        for block in range(3):
            start = (block + 1) * width + duo * pair
            cols = slice(start, start + pair)
            both = jnp.where(low, parts[block][0], parts[block][1])
            gproj[:, cols] = (both * slope_p[:, cols]).astype(BF16)
    grad_xn = nt(gproj[...], win_ref[...])
    grad_tokens = (grad + norm_back(grad_xn, normed, inverse)).astype(BF16)
    out_ref[...] = nn(pick, grad_tokens).astype(BF16).reshape(group, slots, width)
    xn_out[...] = xn
    gated_out[...] = gated
    g_out[...] = grad16


def whole_kernel(
    slots,
    factor,
    len_any,
    dest_any,
    pos_any,
    ev_any,
    ct_any,
    win_any,
    wout_any,
    grad_ref,
    in_ref,
    sum_ref,
    final_ref,
    len_ref,
    dest_ref,
    pos_ref,
    ev_ref,
    ct_ref,
    win_ref,
    wout_ref,
    pick_ref,
    back_ref,
    ev_send,
    ct_send,
    at_send,
    ev_got,
    ct_got,
    at_got,
    act,
    slope_p,
    gproj,
    attn,
    slope_s,
    xn_ref,
    out_ref,
    part_ref,
    core_got,
    one_send,
    one_got,
    two_keep,
    two_send,
    two_got,
    up_send,
    rs_got,
    pair_send,
    pair_keep,
    pair_got,
    load_sems,
    turn_sem,
    row_ssem,
    row_rsem,
    core_ssem,
    core_rsem,
    one_ssem,
    one_rsem,
    two_ssem,
    two_rsem,
    up_ssem,
    up_rsem,
    pair_ssem,
    pair_rsem,
    cross_ssem,
    mate_ssem,
    rim_ssem,
    ag_rsem,
    fwd_ssem,
    fwd_rsem,
):
    rows, width = ev_ref.shape
    group = ev_send.shape[0]
    colors, depth, span = rs_got.shape[0], rs_got.shape[3], rs_got.shape[4]
    total = group * slots
    head = width // HEADS
    scale = 1.0 / head**0.5
    me = lax.axis_index("dp")
    rep = lax.axis_index("replica")
    core = lax.rem(rep, 2)
    other = 1 - core
    spot = rep // 2
    partner = {"replica": spot * 2 + other}
    low_bit, high_bit = lax.rem(me, 2), me // 2
    near = high_bit * 2 + 1 - low_bit
    far = (1 - high_bit) * 2 + low_bit
    third = 3 - me

    def dp_peer(step):
        return lax.rem(me + step, group)

    side = spot // 2
    away = 1 - side
    inner = (spot == 1) | (spot == 2)
    outer = ~inner
    hub = {"replica": (1 + side) * 2 + core}
    mate = {"replica": (3 - spot) * 2 + core}
    rim = {"replica": 3 * side * 2 + core}
    keep = 1 - lax.rem((spot + 1) // 2, 2)
    give = 1 - keep
    pal = {"replica": (spot + 1 - 2 * lax.rem(spot, 2)) * 2 + core}
    far_hub = {"replica": (2 - side) * 2 + core}
    far_rim = {"replica": 3 * away * 2 + core}

    loads = [
        pltpu.make_async_copy(source, target, load_sems.at[at])
        for at, (source, target) in enumerate(
            (
                (ev_any, ev_ref),
                (ct_any, ct_ref),
                (win_any, win_ref),
                (wout_any, wout_ref),
                (dest_any, dest_ref),
                (pos_any, pos_ref),
                (len_any, len_ref),
            )
        )
    ]
    for at in (4, 0, 5, 1, 6):
        loads[at].start()
    barrier = pltpu.get_barrier_semaphore()
    for step in range(1, group):
        pl.semaphore_signal(barrier, inc=1, device_id={"dp": dp_peer(step)}, device_id_type=MESH)
    pl.semaphore_signal(barrier, inc=1, device_id=partner, device_id_type=MESH)

    @pl.when(outer)
    def _():
        for device in (hub, far_hub, far_rim):
            pl.semaphore_signal(barrier, inc=1, device_id=device, device_id_type=MESH)

    @pl.when(inner)
    def _():
        for device in (mate, rim, far_rim):
            pl.semaphore_signal(barrier, inc=1, device_id=device, device_id_type=MESH)

    def describe(src, dst, ssem, rsem, device):
        return pltpu.make_async_remote_copy(
            src_ref=src,
            dst_ref=dst,
            send_sem=ssem,
            recv_sem=rsem,
            device_id=device,
            device_id_type=MESH,
        )

    def send(src, dst, ssem, rsem, device):
        describe(src, dst, ssem, rsem, device).start()

    def sent(like, ssem):
        describe(like, like, ssem, ssem, partner).wait_send()

    def came(like, rsem):
        describe(like, like, rsem, rsem, partner).wait_recv()

    loads[4].wait()
    dest = dest_ref[...]
    hot = lax.broadcasted_iota(jnp.int32, (8, rows), 0) == dest
    upper = lax.broadcasted_iota(jnp.int32, (rows, rows), 0) < lax.broadcasted_iota(
        jnp.int32, (rows, rows), 1
    )
    earlier = nn(
        jnp.where(hot, 1.0, 0.0).astype(BF16), jnp.where(upper, 1.0, 0.0).astype(BF16)
    )
    slot = jnp.sum(jnp.where(hot, earlier, 0.0), axis=0, keepdims=True).astype(jnp.int32)
    slot_iota = lax.broadcasted_iota(jnp.int32, (total, rows), 0)
    pick = jnp.where(slot_iota == dest * slots + slot, 1.0, 0.0).astype(BF16)
    pick_ref[...] = pick
    packed = (group, slots, width)
    loads[0].wait()
    ev_send[...] = nn(pick, ev_ref[...]).astype(BF16).reshape(packed)
    pl.semaphore_wait(barrier, group + 3)

    def rows_out(kind, src, dst):
        for step in (3, 1, 2):
            peer = step ^ me
            send(src.at[peer], dst.at[me], row_ssem.at[kind], row_rsem.at[kind], {"dp": peer})
        dst[me] = src[me]

    def others(buffer):
        return buffer.at[pl.ds(0, group - 1)]

    rows_out(1, ev_send, ev_got)
    loads[2].start()
    loads[3].start()
    loads[5].wait()
    spots = jnp.broadcast_to(pos_ref[...] + 1, (8, rows)).astype(F32).astype(BF16)
    lane_iota = lax.broadcasted_iota(jnp.int32, (LANES, rows), 0)
    for dp in range(group):
        there = jnp.where((lane_iota == slot) & (dest == dp), 1.0, 0.0).astype(BF16)
        at_send[dp] = nt(spots, there)
    rows_out(0, at_send, at_got)
    loads[1].wait()
    ct_send[...] = nn(pick, ct_ref[...]).astype(BF16).reshape(packed)

    @pl.when(core == 0)
    def _():
        rows_out(2, ct_send, ct_got)
        sent(others(ev_send), row_ssem.at[1])
        pl.semaphore_signal(turn_sem, inc=1, device_id=partner, device_id_type=MESH)

    @pl.when(core == 1)
    def _():
        sent(others(ev_send), row_ssem.at[1])
        pl.semaphore_wait(turn_sem, 1)
        rows_out(2, ct_send, ct_got)


    came(others(at_got), row_rsem.at[0])
    came(others(ev_got), row_rsem.at[1])
    place = jnp.zeros((8, total), F32)
    blank = jnp.zeros((8, total - LANES), F32)
    for dp in range(group):
        there = jnp.concatenate([at_got[dp], blank], axis=1)
        place = place + pltpu.roll(there, dp * slots, 1)
    row_iota = lax.broadcasted_iota(jnp.int32, (rows, total), 0).astype(F32) + 1.0
    fetch = jnp.where(row_iota == place[:1], 1.0, 0.0).astype(BF16)
    tokens = nn(fetch, ev_got[...].reshape(total, width))
    normed, inverse = normalize(tokens)
    xn = normed.astype(BF16)
    xn_ref[...] = xn
    loads[2].wait()
    loads[3].wait()
    for block in range(4):
        cols = slice(block * width, (block + 1) * width)
        proj = nn(xn, win_ref[:, cols])
        sig = jax.nn.sigmoid(proj)
        act[:, cols] = (proj * sig).astype(BF16)
        slope_p[:, cols] = sig * (1.0 + proj * (1.0 - sig))
    row_at = lax.broadcasted_iota(jnp.int32, (rows, 1), 0)
    col_at = lax.broadcasted_iota(jnp.int32, (1, rows), 1)
    loads[6].wait()
    bound = jnp.int32(0)
    row_seg = jnp.zeros((rows, 1), jnp.int32)
    col_seg = jnp.zeros((1, rows), jnp.int32)
    for seq in range(len_ref.shape[1]):
        bound = bound + len_ref[0, seq]
        row_seg = row_seg + jnp.where(row_at >= bound, 1, 0)
        col_seg = col_seg + jnp.where(col_at >= bound, 1, 0)
    mask = (row_seg == col_seg) & (col_at <= row_at)
    pair = 2 * head
    low = lax.broadcasted_iota(jnp.int32, (rows, pair), 1) < head

    def half(values, which):
        return jnp.where(low if which == 0 else ~low, values, jnp.zeros_like(values))

    def cut(block, duo):
        start = block * width + duo * pair
        return act[:, start : start + pair]

    outs = []
    for duo in range(HEADS // 2):
        value, query, key = cut(1, duo), cut(2, duo), cut(3, duo)
        parts = []
        for which in range(2):
            at = 2 * duo + which
            scores = nt(half(query, which), key) * scale
            sig = jax.nn.sigmoid(scores)
            weight = jnp.where(mask, scores * sig * (1.0 / MAXLEN), 0.0).astype(BF16)
            attn[at] = weight
            slope_s[at] = jnp.where(
                mask, sig * (1.0 + scores * (1.0 - sig)) * (scale / MAXLEN), 0.0
            )
            parts.append(nn(weight, value))
        outs.append(jnp.where(low, parts[0], parts[1]))
    onorm, oinv = normalize(jnp.concatenate(outs, axis=1))
    gate = act[:, :width].astype(F32)
    gated = (gate * onorm).astype(BF16)

    came(others(ct_got), row_rsem.at[2])
    grad = nn(fetch, ct_got[...].reshape(total, width))
    grad16 = grad.astype(BF16)

    def store_part(color, whole, row_of, column_of):
        for edge in range(2):
            for piece in range(4):
                for dp in range(group):
                    row, column = row_of(edge, piece, dp), column_of(edge, piece, dp)
                    part_ref[color, edge, piece % 2, piece // 2, dp] = whole[
                        row : row + depth, column : column + span
                    ]
        send(
            part_ref.at[color, other],
            core_got.at[color],
            core_ssem.at[0],
            core_rsem.at[color],
            partner,
        )

    store_part(
        0,
        tn(gated, grad16).astype(BF16),
        lambda edge, piece, dp: (2 * dp + edge) * depth,
        lambda edge, piece, dp: piece * span,
    )
    grad_z = nt(grad16, wout_ref[...])
    gproj[:, :width] = (grad_z * onorm * slope_p[:, :width]).astype(BF16)
    grad_out = norm_back(grad_z * gate, onorm, oinv).astype(BF16)

    def back_duo(duo):
        value, query, key = cut(1, duo), cut(2, duo), cut(3, duo)
        gout = grad_out[:, duo * pair : (duo + 1) * pair]
        parts = ([], [], [])
        for which in range(2):
            at = 2 * duo + which
            gscore = (nt(half(gout, which), value) * slope_s[at]).astype(BF16)
            parts[0].append(tn(attn[at], gout))
            parts[1].append(nn(gscore, key))
            parts[2].append(tn(gscore, query))
        for block in range(3):
            start = (block + 1) * width + duo * pair
            cols = slice(start, start + pair)
            both = jnp.where(low, parts[block][0], parts[block][1])
            gproj[:, cols] = (both * slope_p[:, cols]).astype(BF16)

    def stage_zero(duo):
        columns = jnp.concatenate(
            [
                gproj[:, dp * width + duo * span : dp * width + (duo + 1) * span]
                for dp in range(group)
            ],
            axis=1,
        )
        store_part(
            duo + 1,
            tn(xn_ref[...], columns).astype(BF16),
            lambda edge, piece, dp: (4 * edge + piece) * depth,
            lambda edge, piece, dp: dp * span,
        )

    def ways(way):
        return (near, far) if way == 0 else (far, near)

    def stage_one(color):
        came(core_got.at[color], core_rsem.at[color])
        for way in range(2):
            first, second = ways(way)

            def both(dp):
                mine = part_ref[color, core, way, :, dp].astype(F32)
                return mine + core_got[color, way, :, dp].astype(F32)

            one_send[color, way, 0] = both(first).astype(BF16)
            one_send[color, way, 1] = both(third).astype(BF16)
            send(
                one_send.at[color, way],
                one_got.at[color, way],
                one_ssem.at[0],
                one_rsem.at[color],
                {"dp": first},
            )
            two_keep[color, way, 0] = both(me)
            two_keep[color, way, 1] = both(second)

    def stage_two(color):
        came(one_got.at[color], one_rsem.at[color])
        for way in range(2):
            two_send[color, way] = (
                two_keep[color, way, 1] + one_got[color, way, 1].astype(F32)
            ).astype(BF16)
            send(
                two_send.at[color, way],
                two_got.at[color, way],
                two_ssem.at[0],
                two_rsem.at[color],
                {"dp": ways(way)[1]},
            )

    def echoed(color):
        return color < ECHOED

    def stage_three(color):
        came(two_got.at[color], two_rsem.at[color])
        for way in range(2):
            summed = (
                two_keep[color, way, 0]
                + one_got[color, way, 0].astype(F32)
                + two_got[color, way].astype(F32)
            )
            two_keep[color, way, 0] = summed
            up_send[color, :, way] = summed.astype(BF16)

        @pl.when(outer)
        def _():
            for slot, at, device in ((away, 2, far_hub), (side, 0, hub)):
                send(
                    up_send.at[color, slot],
                    rs_got.at[color, at],
                    up_ssem.at[0],
                    up_rsem.at[color],
                    device,
                )

        @pl.when(inner)
        def _():
            send(
                up_send.at[color, away],
                rs_got.at[color, 1],
                up_ssem.at[0],
                up_rsem.at[color],
                mate,
            )

    def stage_c(color):
        @pl.when(inner)
        def _():
            came(rs_got.at[color], up_rsem.at[color])
            for way in range(2):
                summed = two_keep[color, way, 0, side]
                for term in range(3):
                    summed = summed + rs_got[color, term, way].astype(F32)
                final_ref[color, core, side, way] = summed.astype(BF16)
            mine = final_ref.at[color, core, side]
            if not echoed(color):
                send(mine, mine, rim_ssem.at[0], ag_rsem.at[color], far_rim)
            send(mine, mine, mate_ssem.at[0], ag_rsem.at[color], mate)
            send(mine, mine, rim_ssem.at[0], ag_rsem.at[color], rim)
            send(mine, mine, fwd_ssem.at[0], fwd_rsem.at[color], partner)

    def stage_d(color):
        @pl.when(inner)
        def _():
            there = final_ref.at[color, core, away]
            came(there, ag_rsem.at[color])
            if echoed(color):
                send(there, there, rim_ssem.at[0], ag_rsem.at[color], rim)
            send(there, there, fwd_ssem.at[0], fwd_rsem.at[color], partner)

    def stage_e(color):
        @pl.when(outer)
        def _():
            there = final_ref.at[color, core]
            came(there, ag_rsem.at[color])
            send(there, there, fwd_ssem.at[0], fwd_rsem.at[color], partner)

    def pair_zero(color):
        came(core_got.at[color], core_rsem.at[color])
        for way in range(2):
            for dp in range(group):

                def both(slot):
                    mine = part_ref[color, core, way, slot, dp].astype(F32)
                    return mine + core_got[color, way, slot, dp].astype(F32)

                pair_send[way, dp] = both(give).astype(BF16)
                pair_keep[way, dp] = both(keep)
        send(pair_send, pair_got, pair_ssem.at[0], pair_rsem.at[0], pal)

    def pair_one(color):
        came(pair_got, pair_rsem.at[0])
        for way in range(2):
            first, second = ways(way)

            def both(dp):
                return pair_keep[way, dp] + pair_got[way, dp].astype(F32)

            one_send[color, way, 0, 0] = both(first).astype(BF16)
            one_send[color, way, 0, 1] = both(third).astype(BF16)
            send(
                one_send.at[color, way, 0],
                one_got.at[color, way, 0],
                one_ssem.at[1],
                one_rsem.at[color],
                {"dp": first},
            )
            two_keep[color, way, 0, 0] = both(me)
            two_keep[color, way, 0, 1] = both(second)

    def pair_two(color):
        came(one_got.at[color, pl.ds(0, 2), 0], one_rsem.at[color])
        for way in range(2):
            two_send[color, way, 0] = (
                two_keep[color, way, 0, 1] + one_got[color, way, 0, 1].astype(F32)
            ).astype(BF16)
            send(
                two_send.at[color, way, 0],
                two_got.at[color, way, 0],
                two_ssem.at[1],
                two_rsem.at[color],
                {"dp": ways(way)[1]},
            )

    def pair_three(color):
        came(two_got.at[color, pl.ds(0, 2), 0], two_rsem.at[color])
        for way in range(2):
            up_send[color, 0, way] = (
                two_keep[color, way, 0, 0]
                + one_got[color, way, 0, 0].astype(F32)
                + two_got[color, way, 0].astype(F32)
            ).astype(BF16)
        send(
            up_send.at[color, 0], rs_got.at[color, 0], cross_ssem.at[0], up_rsem.at[color], mate
        )

    def pair_four(color):
        came(rs_got.at[color, 0], up_rsem.at[color])
        for way in range(2):
            final_ref[color, core, keep, way] = (
                up_send[color, 0, way].astype(F32) + rs_got[color, 0, way].astype(F32)
            ).astype(BF16)
        mine = final_ref.at[color, core, keep]
        send(mine, mine, cross_ssem.at[0], ag_rsem.at[color], pal)
        send(mine, mine, fwd_ssem.at[0], fwd_rsem.at[color], partner)

    def pair_five(color):
        there = final_ref.at[color, core, give]
        came(there, ag_rsem.at[color])
        send(there, there, fwd_ssem.at[0], fwd_rsem.at[color], partner)

    def stage_f(color):
        came(final_ref.at[color, other], fwd_rsem.at[color])
        if color == 0:
            for edge in range(2):
                for piece in range(4):
                    rows_at = slice(edge * depth, (edge + 1) * depth)
                    sum_ref[rows_at, piece * span : (piece + 1) * span] = (
                        final_ref[0, edge, piece // 2, piece % 2].astype(F32) * factor
                    )
        else:
            in_ref[:, (color - 1) * span : color * span] = (
                final_ref[color].astype(F32) * factor
            ).reshape(width, span)

    back_duo(0)
    stage_zero(0)
    stage_one(0)
    back_duo(1)
    stage_zero(1)
    stage_one(1)
    back_duo(2)
    stage_zero(2)
    pair_zero(PAIRED)
    back_duo(3)
    stage_zero(3)
    stage_two(0)
    stage_one(3)
    grad_xn = nt(gproj[...], win_ref[...])
    stage_two(1)
    stage_one(4)
    grad_tokens = (grad + norm_back(grad_xn, normed, inverse)).astype(BF16)
    out_ref[...] = tn(fetch, grad_tokens).astype(BF16).reshape(packed)
    stage_three(0)
    pair_one(PAIRED)
    stage_two(3)
    stage_three(1)
    stage_two(4)
    pair_two(PAIRED)
    stage_three(3)
    stage_c(0)
    stage_three(4)
    pair_three(PAIRED)
    rows_out(3, out_ref, back_ref)
    stage_c(1)
    stage_c(3)
    stage_d(0)
    stage_c(4)
    pair_four(PAIRED)
    stage_d(1)
    stage_e(0)
    came(others(back_ref), row_rsem.at[3])
    grad_ref[...] = tn(pick_ref[...], back_ref[...].reshape(total, width)).astype(BF16)
    pair_five(PAIRED)
    stage_d(3)
    stage_e(1)
    stage_d(4)
    stage_e(3)
    stage_e(4)
    for color in range(colors):
        stage_f(color)
    sent(others(at_send), row_ssem.at[0])
    sent(others(ct_send), row_ssem.at[2])
    sent(others(out_ref), row_ssem.at[3])
    sent(core_got, core_ssem.at[0])
    plain = pl.ds(0, colors - 1)
    sent(one_send.at[plain], one_ssem.at[0])
    sent(two_send.at[plain], two_ssem.at[0])
    sent(final_ref.at[0, 0], one_ssem.at[1])
    sent(final_ref.at[0, 0, 0], two_ssem.at[1])
    sent(pair_send, pair_ssem.at[0])
    sent(final_ref.at[0, 0], cross_ssem.at[0])
    half_of = final_ref.at[plain, 0, 0]
    whole_of = final_ref.at[plain, 0]

    @pl.when(inner)
    def _():
        sent(half_of, up_ssem.at[0])
        sent(half_of, mate_ssem.at[0])
        sent(whole_of, rim_ssem.at[0])

    @pl.when(outer)
    def _():
        sent(whole_of, up_ssem.at[0])

    sent(final_ref.at[pl.ds(0, colors), 0], fwd_ssem.at[0])


def finish_kernel(*refs):
    count = len(refs) // 2
    sources, outs, sems = refs[:count], refs[count : 2 * count], refs[2 * count]
    copies = [
        pltpu.make_async_copy(sources[at], outs[at], sems.at[at]) for at in range(count)
    ]
    for copy in copies:
        copy.start()
    for copy in copies:
        copy.wait()


def gather_kernel(pick_ref, back_ref, ev_ref):
    group, slots, width = back_ref.shape
    ev_ref[...] = tn(pick_ref[...], back_ref[...].reshape(group * slots, width)).astype(BF16)


VMEM = pl.BlockSpec(memory_space=pltpu.VMEM)
SMEM = pl.BlockSpec(memory_space=pltpu.SMEM)


def shape_of(shape, dtype=BF16):
    return jax.ShapeDtypeStruct(shape, dtype)


def swap(send, ident):
    group = send.shape[0]
    return pl.pallas_call(
        swap_kernel,
        out_shape=shape_of(send.shape),
        in_specs=[VMEM],
        out_specs=VMEM,
        scratch_shapes=[
            pltpu.SemaphoreType.DMA((group,)),
            pltpu.SemaphoreType.DMA((group,)),
            pltpu.SemaphoreType.DMA,
        ],
        compiler_params=pltpu.CompilerParams(collective_id=ident, has_side_effects=True),
        name="swap",
    )(send)


def body(events, cotangent, weight_in, weight_out, plan_dest, plan_pos, seq_lengths):
    group = lax.axis_size("dp")
    replicas = lax.axis_size("replica")
    rows, width = events.shape
    inner = weight_in.shape[1]
    slots = 3 * rows // (2 * group)
    total = group * slots
    chain = replicas // 2
    pair = 2 * width // HEADS
    depth = width // (2 * chain)
    stacked = (
        group == 4
        and chain == 4
        and inner == group * width
        and pair * chain == width
        and pair % LANES == 0
        and depth % 16 == 0
        and slots <= LANES
        and total % LANES == 0
    )
    factor = 1.0 / (rows * group * replicas) ** 0.5
    outgoing_shape = shape_of((group, slots, width))
    wide = [
        pltpu.VMEM((rows, inner), BF16),
        pltpu.VMEM((rows, inner), F32),
    ]
    square = [
        pltpu.VMEM((HEADS, rows, rows), BF16),
        pltpu.VMEM((HEADS, rows, rows), F32),
    ]
    dest, place = plan_dest.reshape(1, rows), plan_pos.reshape(1, rows)
    if stacked:
        packed = pltpu.VMEM((group, slots, width), BF16)
        spots = pltpu.VMEM((group, 8, LANES), F32)
        duos = HEADS // 2
        colors = duos + 1
        piece = (depth, pair)
        sized = lambda *lead, dtype=BF16: pltpu.VMEM(lead + piece, dtype)
        dma = pltpu.SemaphoreType.DMA
        results = pl.pallas_call(
            functools.partial(whole_kernel, slots, factor),
            out_shape=(
                pltpu.VMEM((rows, width), BF16),
                pltpu.VMEM((width, width), F32),
                pltpu.VMEM((width // group, width), F32),
            ),
            in_specs=[pl.BlockSpec(memory_space=pl.ANY)] * 7,
            out_specs=(VMEM,) * 3,
            scratch_shapes=[
                sized(colors, 2, 2, 2),
                pltpu.SMEM(seq_lengths.shape, jnp.int32),
                pltpu.VMEM((1, rows), jnp.int32),
                pltpu.VMEM((1, rows), jnp.int32),
                pltpu.VMEM((rows, width), BF16),
                pltpu.VMEM((rows, width), BF16),
                pltpu.VMEM(weight_in.shape, BF16),
                pltpu.VMEM(weight_out.shape, BF16),
                pltpu.VMEM((total, rows), BF16),
                packed,
            ]
            + [packed, packed, spots] * 2
            + wide
            + [pltpu.VMEM((rows, inner), BF16)]
            + square
            + [
                pltpu.VMEM((rows, width), BF16),
                packed,
                sized(colors, 2, 2, 2, group),
                sized(colors, 2, 2, group),
                sized(colors, 2, 2, 2),
                sized(colors, 2, 2, 2),
                sized(colors, 2, 2, 2, dtype=F32),
                sized(colors, 2, 2),
                sized(colors, 2, 2),
                sized(colors, 2, 2),
                sized(colors, 3, 2),
                sized(2, group),
                sized(2, group, dtype=F32),
                sized(2, group),
                dma((7,)),
                pltpu.SemaphoreType.REGULAR,
                dma((4,)),
                dma((4,)),
            ]
            + [dma((1,)), dma((colors,))]
            + [dma((2,)), dma((colors,))] * 2
            + [dma((1,)), dma((colors,))]
            + [dma((1,))] * 5
            + [dma((colors,)), dma((1,)), dma((colors,))],
            compiler_params=pltpu.CompilerParams(collective_id=0, has_side_effects=True),
            name="whole",
        )(seq_lengths, dest, place, events, cotangent, weight_in, weight_out)
        return pl.pallas_call(
            finish_kernel,
            out_shape=tuple(shape_of(value.shape, value.dtype) for value in results),
            in_specs=[VMEM] * 3,
            out_specs=(pl.BlockSpec(memory_space=pltpu.HBM),) * 3,
            scratch_shapes=[pltpu.SemaphoreType.DMA((3,))],
            name="finish",
        )(*[pltpu.with_memory_space_constraint(value, pltpu.VMEM) for value in results])
    send, pick = pl.pallas_call(
        functools.partial(prep_kernel, slots),
        out_shape=(shape_of((group, slots, 2 * width + LANES)), shape_of((total, rows))),
        in_specs=[VMEM] * 4,
        out_specs=(VMEM, VMEM),
        name="prep",
    )(dest, place, events, cotangent)
    recv = swap(send, 0)
    outgoing, normed_in, grad_proj, gated, grad_rows = pl.pallas_call(
        layer_kernel,
        out_shape=(
            outgoing_shape,
            shape_of((rows, width)),
            shape_of((rows, inner)),
            shape_of((rows, width)),
            shape_of((rows, width)),
        ),
        in_specs=[SMEM] + [VMEM] * 3,
        out_specs=(VMEM,) * 5,
        scratch_shapes=wide + square,
        name="layer",
    )(seq_lengths, recv, weight_in, weight_out)
    back = swap(outgoing, 1)
    grad_events = pl.pallas_call(
        gather_kernel,
        out_shape=shape_of((rows, width)),
        in_specs=[VMEM] * 2,
        out_specs=VMEM,
        name="finish",
    )(pick, back)
    rows_all = lax.all_gather(normed_in, "dp", axis=0, tiled=True)
    cot_all = lax.all_gather(grad_rows, "dp", axis=0, tiled=True)
    proj_cols = lax.all_to_all(grad_proj, "dp", split_axis=1, concat_axis=0, tiled=True)
    gated_cols = lax.all_to_all(gated, "dp", split_axis=1, concat_axis=0, tiled=True)
    shard_in = jnp.einsum("rd,rf->df", rows_all, proj_cols, preferred_element_type=F32)
    shard_out = jnp.einsum("re,rd->ed", gated_cols, cot_all, preferred_element_type=F32)
    total_in, total_out = lax.psum((shard_in, shard_out), "replica")
    return grad_events, total_in * factor, total_out * factor


def solution(mesh):
    return jax.shard_map(
        body,
        mesh=mesh,
        in_specs=(
            P(("dp", "replica"), None),
            P(("dp", "replica"), None),
            P(),
            P(),
            P(("dp", "replica")),
            P(("dp", "replica")),
            P(("dp", "replica"), None),
        ),
        out_specs=(P(("dp", "replica"), None), P(None, "dp"), P("dp", None)),
        check_vma=False,
    )
```

```python
import functools

import jax
import jax.numpy as jnp
from jax import lax
from jax.experimental import pallas as pl
from jax.experimental.pallas import tpu as pltpu
from jax.sharding import PartitionSpec as P

HEADS = 8
MAXLEN = 128
EPS = 1e-05
ECHOED = 1
PAIRED = 2
LANES = 128
MESH = pl.DeviceIdType.MESH
F32 = jnp.float32
BF16 = jnp.bfloat16


def contract(left, right, dims):
    return lax.dot_general(left, right, ((dims[:1], dims[1:]), ((), ())), preferred_element_type=F32)


def nn(left, right):
    return contract(left, right, (1, 0))


def nt(left, right):
    return contract(left, right, (1, 1))


def tn(left, right):
    return contract(left, right, (0, 0))


def normalize(values):
    center = values - jnp.mean(values, axis=-1, keepdims=True)
    inverse = lax.rsqrt(jnp.mean(center * center, axis=-1, keepdims=True) + EPS)
    return center * inverse, inverse


def norm_back(grad, normed, inverse):
    return inverse * (
        grad
        - jnp.mean(grad, axis=-1, keepdims=True)
        - normed * jnp.mean(grad * normed, axis=-1, keepdims=True)
    )


def prep_kernel(slot_count, dest_ref, pos_ref, ev_ref, ct_ref, send_ref, pick_ref):
    rows, width = ev_ref.shape
    group = send_ref.shape[0]
    dest = dest_ref[...]
    hot = lax.broadcasted_iota(jnp.int32, (8, rows), 0) == dest
    upper = lax.broadcasted_iota(jnp.int32, (rows, rows), 0) < lax.broadcasted_iota(
        jnp.int32, (rows, rows), 1
    )
    earlier = nn(
        jnp.where(hot, 1.0, 0.0).astype(BF16), jnp.where(upper, 1.0, 0.0).astype(BF16)
    )
    slot = jnp.sum(jnp.where(hot, earlier, 0.0), axis=0, keepdims=True).astype(jnp.int32)
    flat = dest * slot_count + slot
    total = group * slot_count
    chosen = lax.broadcasted_iota(jnp.int32, (total, rows), 0) == flat
    pick = jnp.where(chosen, 1.0, 0.0).astype(BF16)
    pick_ref[...] = pick
    place = jnp.sum(
        jnp.where(chosen, pos_ref[...].astype(F32) + 1.0, 0.0), axis=1, keepdims=True
    )
    shape = (group, slot_count)
    send_ref[:, :, :width] = nn(pick, ev_ref[...]).astype(BF16).reshape(shape + (width,))
    send_ref[:, :, width : 2 * width] = nn(pick, ct_ref[...]).astype(BF16).reshape(shape + (width,))
    send_ref[:, :, 2 * width :] = (
        jnp.broadcast_to(place, (total, LANES)).astype(BF16).reshape(shape + (LANES,))
    )


def swap_kernel(send_ref, recv_ref, send_sem, recv_sem, own_sem):
    group = lax.axis_size("dp")
    me = lax.axis_index("dp")
    barrier = pltpu.get_barrier_semaphore()
    for step in range(1, group):
        pl.semaphore_signal(
            barrier, inc=1, device_id={"dp": lax.rem(me + step, group)}, device_id_type=MESH
        )
    own = pltpu.make_async_copy(send_ref.at[me], recv_ref.at[me], own_sem)
    own.start()
    pl.semaphore_wait(barrier, group - 1)
    copies = []
    for step in range(1, group):
        peer = lax.rem(me + step, group)
        copy = pltpu.make_async_remote_copy(
            src_ref=send_ref.at[peer],
            dst_ref=recv_ref.at[me],
            send_sem=send_sem.at[step],
            recv_sem=recv_sem.at[step],
            device_id={"dp": peer},
            device_id_type=MESH,
        )
        copy.start()
        copies.append(copy)
    own.wait()
    for copy in copies:
        copy.wait()


def layer_kernel(
    len_ref,
    recv_ref,
    win_ref,
    wout_ref,
    out_ref,
    *rest,
):
    xn_out, gproj, gated_out, g_out, act, slope_p, attn, slope_s = rest
    group, slots, packed = recv_ref.shape
    width = wout_ref.shape[0]
    rows = act.shape[0]
    head = width // HEADS
    scale = 1.0 / head**0.5
    total = group * slots
    got = recv_ref[...].reshape(total, packed)
    place = got[:, 2 * width : 2 * width + 1].astype(F32) - 1.0
    spots = lax.broadcasted_iota(jnp.int32, (total, rows), 1).astype(F32)
    pick = jnp.where(place == spots, 1.0, 0.0).astype(BF16)
    tokens = tn(pick, got[:, :width])
    grad = tn(pick, got[:, width : 2 * width])
    grad16 = grad.astype(BF16)
    normed, inverse = normalize(tokens)
    xn = normed.astype(BF16)
    for block in range(4):
        cols = slice(block * width, (block + 1) * width)
        proj = nn(xn, win_ref[:, cols])
        sig = jax.nn.sigmoid(proj)
        act[:, cols] = (proj * sig).astype(BF16)
        slope_p[:, cols] = sig * (1.0 + proj * (1.0 - sig))
    row_at = lax.broadcasted_iota(jnp.int32, (rows, 1), 0)
    col_at = lax.broadcasted_iota(jnp.int32, (1, rows), 1)
    bound = jnp.int32(0)
    row_seg = jnp.zeros((rows, 1), jnp.int32)
    col_seg = jnp.zeros((1, rows), jnp.int32)
    for seq in range(len_ref.shape[1]):
        bound = bound + len_ref[0, seq]
        row_seg = row_seg + jnp.where(row_at >= bound, 1, 0)
        col_seg = col_seg + jnp.where(col_at >= bound, 1, 0)
    mask = (row_seg == col_seg) & (col_at <= row_at)
    pair = 2 * head
    low = lax.broadcasted_iota(jnp.int32, (rows, pair), 1) < head

    def half(values, which):
        return jnp.where(low if which == 0 else ~low, values, jnp.zeros_like(values))

    def cut(block, duo):
        start = block * width + duo * pair
        return act[:, start : start + pair]

    outs = []
    for duo in range(HEADS // 2):
        value, query, key = cut(1, duo), cut(2, duo), cut(3, duo)
        parts = []
        for which in range(2):
            at = 2 * duo + which
            scores = nt(half(query, which), key) * scale
            sig = jax.nn.sigmoid(scores)
            weight = jnp.where(mask, scores * sig * (1.0 / MAXLEN), 0.0).astype(BF16)
            attn[at] = weight
            slope_s[at] = jnp.where(
                mask, sig * (1.0 + scores * (1.0 - sig)) * (scale / MAXLEN), 0.0
            )
            parts.append(nn(weight, value))
        outs.append(jnp.where(low, parts[0], parts[1]))
    onorm, oinv = normalize(jnp.concatenate(outs, axis=1))
    gate = act[:, :width].astype(F32)
    gated = (gate * onorm).astype(BF16)
    grad_z = nt(grad16, wout_ref[...])
    gproj[:, :width] = (grad_z * onorm * slope_p[:, :width]).astype(BF16)
    grad_out = norm_back(grad_z * gate, onorm, oinv).astype(BF16)
    for duo in range(HEADS // 2):
        value, query, key = cut(1, duo), cut(2, duo), cut(3, duo)
        gout = grad_out[:, duo * pair : (duo + 1) * pair]
        parts = ([], [], [])
        for which in range(2):
            at = 2 * duo + which
            gscore = (nt(half(gout, which), value) * slope_s[at]).astype(BF16)
            parts[0].append(tn(attn[at], gout))
            parts[1].append(nn(gscore, key))
            parts[2].append(tn(gscore, query))
        for block in range(3):
            start = (block + 1) * width + duo * pair
            cols = slice(start, start + pair)
            both = jnp.where(low, parts[block][0], parts[block][1])
            gproj[:, cols] = (both * slope_p[:, cols]).astype(BF16)
    grad_xn = nt(gproj[...], win_ref[...])
    grad_tokens = (grad + norm_back(grad_xn, normed, inverse)).astype(BF16)
    out_ref[...] = nn(pick, grad_tokens).astype(BF16).reshape(group, slots, width)
    xn_out[...] = xn
    gated_out[...] = gated
    g_out[...] = grad16


def whole_kernel(
    slots,
    factor,
    len_any,
    dest_any,
    pos_any,
    ev_any,
    ct_any,
    win_any,
    wout_any,
    grad_ref,
    in_ref,
    sum_ref,
    final_ref,
    len_ref,
    dest_ref,
    pos_ref,
    ev_ref,
    ct_ref,
    win_ref,
    wout_ref,
    pick_ref,
    back_ref,
    ev_send,
    ct_send,
    at_send,
    ev_got,
    ct_got,
    at_got,
    act,
    slope_p,
    gproj,
    attn,
    slope_s,
    xn_ref,
    out_ref,
    part_ref,
    core_got,
    one_send,
    one_got,
    two_keep,
    two_send,
    two_got,
    up_send,
    rs_got,
    pair_send,
    pair_keep,
    pair_got,
    load_sems,
    turn_sem,
    row_ssem,
    row_rsem,
    core_ssem,
    core_rsem,
    one_ssem,
    one_rsem,
    two_ssem,
    two_rsem,
    up_ssem,
    up_rsem,
    pair_ssem,
    pair_rsem,
    cross_ssem,
    mate_ssem,
    rim_ssem,
    ag_rsem,
    fwd_ssem,
    fwd_rsem,
):
    rows, width = ev_ref.shape
    group = ev_send.shape[0]
    colors, depth, span = rs_got.shape[0], rs_got.shape[3], rs_got.shape[4]
    total = group * slots
    head = width // HEADS
    scale = 1.0 / head**0.5
    me = lax.axis_index("dp")
    rep = lax.axis_index("replica")
    core = lax.rem(rep, 2)
    other = 1 - core
    spot = rep // 2
    partner = {"replica": spot * 2 + other}
    low_bit, high_bit = lax.rem(me, 2), me // 2
    near = high_bit * 2 + 1 - low_bit
    far = (1 - high_bit) * 2 + low_bit
    third = 3 - me

    def dp_peer(step):
        return lax.rem(me + step, group)

    side = spot // 2
    away = 1 - side
    inner = (spot == 1) | (spot == 2)
    outer = ~inner
    hub = {"replica": (1 + side) * 2 + core}
    mate = {"replica": (3 - spot) * 2 + core}
    rim = {"replica": 3 * side * 2 + core}
    keep = 1 - lax.rem((spot + 1) // 2, 2)
    give = 1 - keep
    pal = {"replica": (spot + 1 - 2 * lax.rem(spot, 2)) * 2 + core}
    far_hub = {"replica": (2 - side) * 2 + core}
    far_rim = {"replica": 3 * away * 2 + core}

    loads = [
        pltpu.make_async_copy(source, target, load_sems.at[at])
        for at, (source, target) in enumerate(
            (
                (ev_any, ev_ref),
                (ct_any, ct_ref),
                (win_any, win_ref),
                (wout_any, wout_ref),
                (dest_any, dest_ref),
                (pos_any, pos_ref),
                (len_any, len_ref),
            )
        )
    ]
    for at in (4, 0, 5, 1, 6):
        loads[at].start()
    barrier = pltpu.get_barrier_semaphore()
    for step in range(1, group):
        pl.semaphore_signal(barrier, inc=1, device_id={"dp": dp_peer(step)}, device_id_type=MESH)
    pl.semaphore_signal(barrier, inc=1, device_id=partner, device_id_type=MESH)

    @pl.when(outer)
    def _():
        for device in (hub, far_hub, far_rim):
            pl.semaphore_signal(barrier, inc=1, device_id=device, device_id_type=MESH)

    @pl.when(inner)
    def _():
        for device in (mate, rim, far_rim):
            pl.semaphore_signal(barrier, inc=1, device_id=device, device_id_type=MESH)

    def describe(src, dst, ssem, rsem, device):
        return pltpu.make_async_remote_copy(
            src_ref=src,
            dst_ref=dst,
            send_sem=ssem,
            recv_sem=rsem,
            device_id=device,
            device_id_type=MESH,
        )

    def send(src, dst, ssem, rsem, device):
        describe(src, dst, ssem, rsem, device).start()

    def sent(like, ssem):
        describe(like, like, ssem, ssem, partner).wait_send()

    def came(like, rsem):
        describe(like, like, rsem, rsem, partner).wait_recv()

    loads[4].wait()
    dest = dest_ref[...]
    hot = lax.broadcasted_iota(jnp.int32, (8, rows), 0) == dest
    upper = lax.broadcasted_iota(jnp.int32, (rows, rows), 0) < lax.broadcasted_iota(
        jnp.int32, (rows, rows), 1
    )
    earlier = nn(
        jnp.where(hot, 1.0, 0.0).astype(BF16), jnp.where(upper, 1.0, 0.0).astype(BF16)
    )
    slot = jnp.sum(jnp.where(hot, earlier, 0.0), axis=0, keepdims=True).astype(jnp.int32)
    slot_iota = lax.broadcasted_iota(jnp.int32, (total, rows), 0)
    pick = jnp.where(slot_iota == dest * slots + slot, 1.0, 0.0).astype(BF16)
    pick_ref[...] = pick
    packed = (group, slots, width)
    loads[0].wait()
    ev_send[...] = nn(pick, ev_ref[...]).astype(BF16).reshape(packed)
    loads[5].wait()
    spots = jnp.broadcast_to(pos_ref[...] + 1, (8, rows)).astype(F32).astype(BF16)
    lane_iota = lax.broadcasted_iota(jnp.int32, (LANES, rows), 0)
    for dp in range(group):
        there = jnp.where((lane_iota == slot) & (dest == dp), 1.0, 0.0).astype(BF16)
        at_send[dp] = nt(spots, there)
    pl.semaphore_wait(barrier, group + 3)

    def rows_out(kind, src, dst):
        for step in (3, 1, 2):
            peer = step ^ me
            send(src.at[peer], dst.at[me], row_ssem.at[kind], row_rsem.at[kind], {"dp": peer})
        dst[me] = src[me]

    def others(buffer):
        return buffer.at[pl.ds(0, group - 1)]

    rows_out(0, at_send, at_got)
    rows_out(1, ev_send, ev_got)
    loads[2].start()
    loads[3].start()
    loads[1].wait()
    ct_send[...] = nn(pick, ct_ref[...]).astype(BF16).reshape(packed)

    @pl.when(core == 0)
    def _():
        rows_out(2, ct_send, ct_got)
        sent(others(ev_send), row_ssem.at[1])
        pl.semaphore_signal(turn_sem, inc=1, device_id=partner, device_id_type=MESH)

    @pl.when(core == 1)
    def _():
        sent(others(ev_send), row_ssem.at[1])
        pl.semaphore_wait(turn_sem, 1)
        rows_out(2, ct_send, ct_got)


    came(others(at_got), row_rsem.at[0])
    place = jnp.zeros((8, total), F32)
    blank = jnp.zeros((8, total - LANES), F32)
    for dp in range(group):
        there = jnp.concatenate([at_got[dp], blank], axis=1)
        place = place + pltpu.roll(there, dp * slots, 1)
    row_iota = lax.broadcasted_iota(jnp.int32, (rows, total), 0).astype(F32) + 1.0
    fetch = jnp.where(row_iota == place[:1], 1.0, 0.0).astype(BF16)
    row_at = lax.broadcasted_iota(jnp.int32, (rows, 1), 0)
    col_at = lax.broadcasted_iota(jnp.int32, (1, rows), 1)
    loads[6].wait()
    bound = jnp.int32(0)
    row_seg = jnp.zeros((rows, 1), jnp.int32)
    col_seg = jnp.zeros((1, rows), jnp.int32)
    for seq in range(len_ref.shape[1]):
        bound = bound + len_ref[0, seq]
        row_seg = row_seg + jnp.where(row_at >= bound, 1, 0)
        col_seg = col_seg + jnp.where(col_at >= bound, 1, 0)
    came(others(ev_got), row_rsem.at[1])
    tokens = nn(fetch, ev_got[...].reshape(total, width))
    normed, inverse = normalize(tokens)
    xn = normed.astype(BF16)
    xn_ref[...] = xn
    loads[2].wait()
    loads[3].wait()
    for block in range(4):
        cols = slice(block * width, (block + 1) * width)
        proj = nn(xn, win_ref[:, cols])
        sig = jax.nn.sigmoid(proj)
        act[:, cols] = (proj * sig).astype(BF16)
        slope_p[:, cols] = sig * (1.0 + proj * (1.0 - sig))
    mask = (row_seg == col_seg) & (col_at <= row_at)
    pair = 2 * head
    low = lax.broadcasted_iota(jnp.int32, (rows, pair), 1) < head

    def half(values, which):
        return jnp.where(low if which == 0 else ~low, values, jnp.zeros_like(values))

    def cut(block, duo):
        start = block * width + duo * pair
        return act[:, start : start + pair]

    outs = []
    for duo in range(HEADS // 2):
        value, query, key = cut(1, duo), cut(2, duo), cut(3, duo)
        parts = []
        for which in range(2):
            at = 2 * duo + which
            scores = nt(half(query, which), key) * scale
            sig = jax.nn.sigmoid(scores)
            weight = jnp.where(mask, scores * sig * (1.0 / MAXLEN), 0.0).astype(BF16)
            attn[at] = weight
            slope_s[at] = jnp.where(
                mask, sig * (1.0 + scores * (1.0 - sig)) * (scale / MAXLEN), 0.0
            )
            parts.append(nn(weight, value))
        outs.append(jnp.where(low, parts[0], parts[1]))
    onorm, oinv = normalize(jnp.concatenate(outs, axis=1))
    gate = act[:, :width].astype(F32)
    gated = (gate * onorm).astype(BF16)
    gated_slots = tn(fetch, gated).astype(BF16)

    came(others(ct_got), row_rsem.at[2])
    ct_slots = ct_got[...].reshape(total, width)

    def store_part(color, whole, row_of, column_of):
        for edge in range(2):
            for piece in range(4):
                for dp in range(group):
                    row, column = row_of(edge, piece, dp), column_of(edge, piece, dp)
                    part_ref[color, edge, piece % 2, piece // 2, dp] = whole[
                        row : row + depth, column : column + span
                    ]
        send(
            part_ref.at[color, other],
            core_got.at[color],
            core_ssem.at[0],
            core_rsem.at[color],
            partner,
        )

    store_part(
        0,
        tn(gated_slots, ct_slots).astype(BF16),
        lambda edge, piece, dp: (2 * dp + edge) * depth,
        lambda edge, piece, dp: piece * span,
    )
    grad = nn(fetch, ct_slots)
    grad_z = nt(grad.astype(BF16), wout_ref[...])
    gproj[:, :width] = (grad_z * onorm * slope_p[:, :width]).astype(BF16)
    grad_out = norm_back(grad_z * gate, onorm, oinv).astype(BF16)

    def back_duo(duo):
        value, query, key = cut(1, duo), cut(2, duo), cut(3, duo)
        gout = grad_out[:, duo * pair : (duo + 1) * pair]
        parts = ([], [], [])
        for which in range(2):
            at = 2 * duo + which
            gscore = (nt(half(gout, which), value) * slope_s[at]).astype(BF16)
            parts[0].append(tn(attn[at], gout))
            parts[1].append(nn(gscore, key))
            parts[2].append(tn(gscore, query))
        for block in range(3):
            start = (block + 1) * width + duo * pair
            cols = slice(start, start + pair)
            both = jnp.where(low, parts[block][0], parts[block][1])
            gproj[:, cols] = (both * slope_p[:, cols]).astype(BF16)

    def stage_zero(duo):
        columns = jnp.concatenate(
            [
                gproj[:, dp * width + duo * span : dp * width + (duo + 1) * span]
                for dp in range(group)
            ],
            axis=1,
        )
        store_part(
            duo + 1,
            tn(xn_ref[...], columns).astype(BF16),
            lambda edge, piece, dp: (4 * edge + piece) * depth,
            lambda edge, piece, dp: dp * span,
        )

    def ways(way):
        return (near, far) if way == 0 else (far, near)

    def stage_one(color):
        came(core_got.at[color], core_rsem.at[color])
        for way in range(2):
            first, second = ways(way)

            def both(dp):
                mine = part_ref[color, core, way, :, dp].astype(F32)
                return mine + core_got[color, way, :, dp].astype(F32)

            one_send[color, way, 0] = both(first).astype(BF16)
            one_send[color, way, 1] = both(third).astype(BF16)
            send(
                one_send.at[color, way],
                one_got.at[color, way],
                one_ssem.at[0],
                one_rsem.at[color],
                {"dp": first},
            )
            two_keep[color, way, 0] = both(me)
            two_keep[color, way, 1] = both(second)

    def stage_two(color):
        came(one_got.at[color], one_rsem.at[color])
        for way in range(2):
            two_send[color, way] = (
                two_keep[color, way, 1] + one_got[color, way, 1].astype(F32)
            ).astype(BF16)
            send(
                two_send.at[color, way],
                two_got.at[color, way],
                two_ssem.at[0],
                two_rsem.at[color],
                {"dp": ways(way)[1]},
            )

    def echoed(color):
        return color < ECHOED

    def stage_three(color):
        came(two_got.at[color], two_rsem.at[color])
        for way in range(2):
            summed = (
                two_keep[color, way, 0]
                + one_got[color, way, 0].astype(F32)
                + two_got[color, way].astype(F32)
            )
            two_keep[color, way, 0] = summed
            up_send[color, :, way] = summed.astype(BF16)

        @pl.when(outer)
        def _():
            for slot, at, device in ((away, 2, far_hub), (side, 0, hub)):
                send(
                    up_send.at[color, slot],
                    rs_got.at[color, at],
                    up_ssem.at[0],
                    up_rsem.at[color],
                    device,
                )

        @pl.when(inner)
        def _():
            send(
                up_send.at[color, away],
                rs_got.at[color, 1],
                up_ssem.at[0],
                up_rsem.at[color],
                mate,
            )

    def stage_c(color):
        @pl.when(inner)
        def _():
            came(rs_got.at[color], up_rsem.at[color])
            for way in range(2):
                summed = two_keep[color, way, 0, side]
                for term in range(3):
                    summed = summed + rs_got[color, term, way].astype(F32)
                final_ref[color, core, side, way] = summed.astype(BF16)
            mine = final_ref.at[color, core, side]
            if not echoed(color):
                send(mine, mine, rim_ssem.at[0], ag_rsem.at[color], far_rim)
            send(mine, mine, mate_ssem.at[0], ag_rsem.at[color], mate)
            send(mine, mine, rim_ssem.at[0], ag_rsem.at[color], rim)
            send(mine, mine, fwd_ssem.at[0], fwd_rsem.at[color], partner)

    def stage_d(color):
        @pl.when(inner)
        def _():
            there = final_ref.at[color, core, away]
            came(there, ag_rsem.at[color])
            if echoed(color):
                send(there, there, rim_ssem.at[0], ag_rsem.at[color], rim)
            send(there, there, fwd_ssem.at[0], fwd_rsem.at[color], partner)

    def stage_e(color):
        @pl.when(outer)
        def _():
            there = final_ref.at[color, core]
            came(there, ag_rsem.at[color])
            send(there, there, fwd_ssem.at[0], fwd_rsem.at[color], partner)

    def pair_zero(color):
        came(core_got.at[color], core_rsem.at[color])
        for way in range(2):
            for dp in range(group):

                def both(slot):
                    mine = part_ref[color, core, way, slot, dp].astype(F32)
                    return mine + core_got[color, way, slot, dp].astype(F32)

                pair_send[way, dp] = both(give).astype(BF16)
                pair_keep[way, dp] = both(keep)
        send(pair_send, pair_got, pair_ssem.at[0], pair_rsem.at[0], pal)

    def pair_one(color):
        came(pair_got, pair_rsem.at[0])
        for way in range(2):
            first, second = ways(way)

            def both(dp):
                return pair_keep[way, dp] + pair_got[way, dp].astype(F32)

            one_send[color, way, 0, 0] = both(first).astype(BF16)
            one_send[color, way, 0, 1] = both(third).astype(BF16)
            send(
                one_send.at[color, way, 0],
                one_got.at[color, way, 0],
                one_ssem.at[1],
                one_rsem.at[color],
                {"dp": first},
            )
            two_keep[color, way, 0, 0] = both(me)
            two_keep[color, way, 0, 1] = both(second)

    def pair_two(color):
        came(one_got.at[color, pl.ds(0, 2), 0], one_rsem.at[color])
        for way in range(2):
            two_send[color, way, 0] = (
                two_keep[color, way, 0, 1] + one_got[color, way, 0, 1].astype(F32)
            ).astype(BF16)
            send(
                two_send.at[color, way, 0],
                two_got.at[color, way, 0],
                two_ssem.at[1],
                two_rsem.at[color],
                {"dp": ways(way)[1]},
            )

    def pair_three(color):
        came(two_got.at[color, pl.ds(0, 2), 0], two_rsem.at[color])
        for way in range(2):
            up_send[color, 0, way] = (
                two_keep[color, way, 0, 0]
                + one_got[color, way, 0, 0].astype(F32)
                + two_got[color, way, 0].astype(F32)
            ).astype(BF16)
        send(
            up_send.at[color, 0], rs_got.at[color, 0], cross_ssem.at[0], up_rsem.at[color], mate
        )

    def pair_four(color):
        came(rs_got.at[color, 0], up_rsem.at[color])
        for way in range(2):
            final_ref[color, core, keep, way] = (
                up_send[color, 0, way].astype(F32) + rs_got[color, 0, way].astype(F32)
            ).astype(BF16)
        mine = final_ref.at[color, core, keep]
        send(mine, mine, cross_ssem.at[0], ag_rsem.at[color], pal)
        send(mine, mine, fwd_ssem.at[0], fwd_rsem.at[color], partner)

    def pair_five(color):
        there = final_ref.at[color, core, give]
        came(there, ag_rsem.at[color])
        send(there, there, fwd_ssem.at[0], fwd_rsem.at[color], partner)

    def stage_f(color):
        came(final_ref.at[color, other], fwd_rsem.at[color])
        if color == 0:
            for edge in range(2):
                for piece in range(4):
                    rows_at = slice(edge * depth, (edge + 1) * depth)
                    sum_ref[rows_at, piece * span : (piece + 1) * span] = (
                        final_ref[0, edge, piece // 2, piece % 2].astype(F32) * factor
                    )
        else:
            in_ref[:, (color - 1) * span : color * span] = (
                final_ref[color].astype(F32) * factor
            ).reshape(width, span)

    back_duo(0)
    stage_one(0)
    stage_zero(0)
    back_duo(1)
    stage_zero(1)
    stage_one(1)
    back_duo(2)
    stage_zero(2)
    pair_zero(PAIRED)
    back_duo(3)
    stage_zero(3)
    stage_two(0)
    stage_one(3)
    grad_xn = nt(gproj[...], win_ref[...])
    stage_two(1)
    stage_one(4)
    grad_tokens = (grad + norm_back(grad_xn, normed, inverse)).astype(BF16)
    out_ref[...] = tn(fetch, grad_tokens).astype(BF16).reshape(packed)
    stage_three(0)
    pair_one(PAIRED)
    stage_two(3)
    stage_three(1)
    stage_two(4)
    pair_two(PAIRED)
    stage_three(3)
    stage_c(0)
    stage_three(4)
    pair_three(PAIRED)
    rows_out(3, out_ref, back_ref)
    stage_c(1)
    stage_c(3)
    stage_d(0)
    stage_c(4)
    pair_four(PAIRED)
    stage_d(1)
    stage_e(0)
    came(others(back_ref), row_rsem.at[3])
    grad_ref[...] = tn(pick_ref[...], back_ref[...].reshape(total, width)).astype(BF16)
    pair_five(PAIRED)
    stage_d(3)
    stage_e(1)
    stage_d(4)
    stage_e(3)
    stage_e(4)
    for color in range(colors):
        stage_f(color)
    sent(others(at_send), row_ssem.at[0])
    sent(others(ct_send), row_ssem.at[2])
    sent(others(out_ref), row_ssem.at[3])
    sent(core_got, core_ssem.at[0])
    plain = pl.ds(0, colors - 1)
    sent(one_send.at[plain], one_ssem.at[0])
    sent(two_send.at[plain], two_ssem.at[0])
    sent(final_ref.at[0, 0], one_ssem.at[1])
    sent(final_ref.at[0, 0, 0], two_ssem.at[1])
    sent(pair_send, pair_ssem.at[0])
    sent(final_ref.at[0, 0], cross_ssem.at[0])
    half_of = final_ref.at[plain, 0, 0]
    whole_of = final_ref.at[plain, 0]

    @pl.when(inner)
    def _():
        sent(half_of, up_ssem.at[0])
        sent(half_of, mate_ssem.at[0])
        sent(whole_of, rim_ssem.at[0])

    @pl.when(outer)
    def _():
        sent(whole_of, up_ssem.at[0])

    sent(final_ref.at[pl.ds(0, colors), 0], fwd_ssem.at[0])


def finish_kernel(*refs):
    count = len(refs) // 2
    sources, outs, sems = refs[:count], refs[count : 2 * count], refs[2 * count]
    copies = [
        pltpu.make_async_copy(sources[at], outs[at], sems.at[at]) for at in range(count)
    ]
    for copy in copies:
        copy.start()
    for copy in copies:
        copy.wait()


def gather_kernel(pick_ref, back_ref, ev_ref):
    group, slots, width = back_ref.shape
    ev_ref[...] = tn(pick_ref[...], back_ref[...].reshape(group * slots, width)).astype(BF16)


VMEM = pl.BlockSpec(memory_space=pltpu.VMEM)
SMEM = pl.BlockSpec(memory_space=pltpu.SMEM)


def shape_of(shape, dtype=BF16):
    return jax.ShapeDtypeStruct(shape, dtype)


def swap(send, ident):
    group = send.shape[0]
    return pl.pallas_call(
        swap_kernel,
        out_shape=shape_of(send.shape),
        in_specs=[VMEM],
        out_specs=VMEM,
        scratch_shapes=[
            pltpu.SemaphoreType.DMA((group,)),
            pltpu.SemaphoreType.DMA((group,)),
            pltpu.SemaphoreType.DMA,
        ],
        compiler_params=pltpu.CompilerParams(collective_id=ident, has_side_effects=True),
        name="swap",
    )(send)


def body(events, cotangent, weight_in, weight_out, plan_dest, plan_pos, seq_lengths):
    group = lax.axis_size("dp")
    replicas = lax.axis_size("replica")
    rows, width = events.shape
    inner = weight_in.shape[1]
    slots = 3 * rows // (2 * group)
    total = group * slots
    chain = replicas // 2
    pair = 2 * width // HEADS
    depth = width // (2 * chain)
    stacked = (
        group == 4
        and chain == 4
        and inner == group * width
        and pair * chain == width
        and pair % LANES == 0
        and depth % 16 == 0
        and slots <= LANES
        and total % LANES == 0
    )
    factor = 1.0 / (rows * group * replicas) ** 0.5
    outgoing_shape = shape_of((group, slots, width))
    wide = [
        pltpu.VMEM((rows, inner), BF16),
        pltpu.VMEM((rows, inner), F32),
    ]
    square = [
        pltpu.VMEM((HEADS, rows, rows), BF16),
        pltpu.VMEM((HEADS, rows, rows), F32),
    ]
    dest, place = plan_dest.reshape(1, rows), plan_pos.reshape(1, rows)
    if stacked:
        packed = pltpu.VMEM((group, slots, width), BF16)
        spots = pltpu.VMEM((group, 8, LANES), F32)
        duos = HEADS // 2
        colors = duos + 1
        piece = (depth, pair)
        sized = lambda *lead, dtype=BF16: pltpu.VMEM(lead + piece, dtype)
        dma = pltpu.SemaphoreType.DMA
        results = pl.pallas_call(
            functools.partial(whole_kernel, slots, factor),
            out_shape=(
                pltpu.VMEM((rows, width), BF16),
                pltpu.VMEM((width, width), F32),
                pltpu.VMEM((width // group, width), F32),
            ),
            in_specs=[pl.BlockSpec(memory_space=pl.ANY)] * 7,
            out_specs=(VMEM,) * 3,
            scratch_shapes=[
                sized(colors, 2, 2, 2),
                pltpu.SMEM(seq_lengths.shape, jnp.int32),
                pltpu.VMEM((1, rows), jnp.int32),
                pltpu.VMEM((1, rows), jnp.int32),
                pltpu.VMEM((rows, width), BF16),
                pltpu.VMEM((rows, width), BF16),
                pltpu.VMEM(weight_in.shape, BF16),
                pltpu.VMEM(weight_out.shape, BF16),
                pltpu.VMEM((total, rows), BF16),
                packed,
            ]
            + [packed, packed, spots] * 2
            + wide
            + [pltpu.VMEM((rows, inner), BF16)]
            + square
            + [
                pltpu.VMEM((rows, width), BF16),
                packed,
                sized(colors, 2, 2, 2, group),
                sized(colors, 2, 2, group),
                sized(colors, 2, 2, 2),
                sized(colors, 2, 2, 2),
                sized(colors, 2, 2, 2, dtype=F32),
                sized(colors, 2, 2),
                sized(colors, 2, 2),
                sized(colors, 2, 2),
                sized(colors, 3, 2),
                sized(2, group),
                sized(2, group, dtype=F32),
                sized(2, group),
                dma((7,)),
                pltpu.SemaphoreType.REGULAR,
                dma((4,)),
                dma((4,)),
            ]
            + [dma((1,)), dma((colors,))]
            + [dma((2,)), dma((colors,))] * 2
            + [dma((1,)), dma((colors,))]
            + [dma((1,))] * 5
            + [dma((colors,)), dma((1,)), dma((colors,))],
            compiler_params=pltpu.CompilerParams(collective_id=0, has_side_effects=True),
            name="whole",
        )(seq_lengths, dest, place, events, cotangent, weight_in, weight_out)
        return pl.pallas_call(
            finish_kernel,
            out_shape=tuple(shape_of(value.shape, value.dtype) for value in results),
            in_specs=[VMEM] * 3,
            out_specs=(pl.BlockSpec(memory_space=pltpu.HBM),) * 3,
            scratch_shapes=[pltpu.SemaphoreType.DMA((3,))],
            name="finish",
        )(*[pltpu.with_memory_space_constraint(value, pltpu.VMEM) for value in results])
    send, pick = pl.pallas_call(
        functools.partial(prep_kernel, slots),
        out_shape=(shape_of((group, slots, 2 * width + LANES)), shape_of((total, rows))),
        in_specs=[VMEM] * 4,
        out_specs=(VMEM, VMEM),
        name="prep",
    )(dest, place, events, cotangent)
    recv = swap(send, 0)
    outgoing, normed_in, grad_proj, gated, grad_rows = pl.pallas_call(
        layer_kernel,
        out_shape=(
            outgoing_shape,
            shape_of((rows, width)),
            shape_of((rows, inner)),
            shape_of((rows, width)),
            shape_of((rows, width)),
        ),
        in_specs=[SMEM] + [VMEM] * 3,
        out_specs=(VMEM,) * 5,
        scratch_shapes=wide + square,
        name="layer",
    )(seq_lengths, recv, weight_in, weight_out)
    back = swap(outgoing, 1)
    grad_events = pl.pallas_call(
        gather_kernel,
        out_shape=shape_of((rows, width)),
        in_specs=[VMEM] * 2,
        out_specs=VMEM,
        name="finish",
    )(pick, back)
    rows_all = lax.all_gather(normed_in, "dp", axis=0, tiled=True)
    cot_all = lax.all_gather(grad_rows, "dp", axis=0, tiled=True)
    proj_cols = lax.all_to_all(grad_proj, "dp", split_axis=1, concat_axis=0, tiled=True)
    gated_cols = lax.all_to_all(gated, "dp", split_axis=1, concat_axis=0, tiled=True)
    shard_in = jnp.einsum("rd,rf->df", rows_all, proj_cols, preferred_element_type=F32)
    shard_out = jnp.einsum("re,rd->ed", gated_cols, cot_all, preferred_element_type=F32)
    total_in, total_out = lax.psum((shard_in, shard_out), "replica")
    return grad_events, total_in * factor, total_out * factor


def solution(mesh):
    return jax.shard_map(
        body,
        mesh=mesh,
        in_specs=(
            P(("dp", "replica"), None),
            P(("dp", "replica"), None),
            P(),
            P(),
            P(("dp", "replica")),
            P(("dp", "replica")),
            P(("dp", "replica"), None),
        ),
        out_specs=(P(("dp", "replica"), None), P(None, "dp"), P("dp", None)),
        check_vma=False,
    )
```
